32 devices in a mesh: tm: 4 (over y, x), rows: 8 (over z, core).
Axes of the slice: x: 2, y: 2, z: 4, core: 2. Of those that a mesh axis runs over, the one named last changes fastest.
Arguments:
- latents: bfloat16 [4, 32, 104, 384], P('tm', 'rows')
- row_valid: int32 [32], P('rows'), may hold values from 0 to 1, as said below
- norm_gain: float32 [384], replicated, may hold values from 0.25 to 1.75
- conv_weight: bfloat16 [10368, 384], P('tm'), may hold values from -0.0625 to 0.0625
- attn_gain: float32 [384], replicated, may hold values from 0.25 to 1.75
- w_query: bfloat16 [384, 384], replicated
- w_key: bfloat16 [384, 384], replicated
- w_value: bfloat16 [384, 384], replicated, may hold values from -0.3125 to 0.3125
- w_out: bfloat16 [384, 384], replicated, may hold values from -0.3125 to 0.3125
- cotangent: bfloat16 [4, 32, 104, 384], P('tm', 'rows'), may hold values from -6 to 6
Outputs:
- input_grad: bfloat16 [4, 32, 104, 384], P('tm', 'rows')
- conv_weight_grad: float32 [10368, 384], P(('tm', 'rows'))
- attn_weight_grad: float32 [1536, 384], P(('tm', 'rows'))
The draws below stay inside these ranges and needn't reach their ends.
Inputs may be any that keep to these rules, and one draw needn't show every extreme that they name: row_valid is 1 on rows 0 to 15 and 0 on row 31; the rows between may be either.
All inputs are finite; a program needn't handle non-finite values.
Results may differ from the reference program's by a relative error of at most 0.01.
Values may be sent and summed in bfloat16 or wider, within the bound.
A program may use at most 192 MiB of HBM per device.

```python
import math
import jax
import jax.numpy as jnp
from jax import lax

C = 384
W = 104
R_DEV = 4
FRAMES = 4
H = 32
N_ROWS = 8


def draw_latents(key, part):
    full_shape = (FRAMES, H, W, C)
    return jnp.clip(jax.random.normal(key, full_shape, jnp.float32), -6.0, 6.0).astype(jnp.bfloat16)


def draw_row_valid(key, part):
    coin = jax.random.randint(jax.random.fold_in(key, 5), (H,), 0, 2)
    row_at = jnp.arange(H)
    picked = jnp.where(row_at < H // 2, 1, coin)
    return jnp.where(row_at == H - 1, 0, picked).astype(jnp.int32)


def query_key_pair(key):
    sub_one, sub_two = jax.random.split(jax.random.fold_in(key, 11), 2)
    root_scale = 1.0 / math.sqrt(C)
    base_draw = jnp.clip(jax.random.normal(sub_one, (C, C), jnp.float32), -5.0, 5.0) * root_scale
    other_draw = jnp.clip(jax.random.normal(sub_two, (C, C), jnp.float32), -5.0, 5.0) * root_scale
    query_draw = base_draw
    key_draw = other_draw
    return (query_draw, key_draw)


def draw_w_query(key, part):
    return query_key_pair(key)[0].astype(jnp.bfloat16)


def draw_w_key(key, part):
    return query_key_pair(key)[1].astype(jnp.bfloat16)


def shard_levels(rng, dims, shards, least, high):
    def one(axis_at, parts):
        heights = jax.random.uniform(jax.random.fold_in(jax.random.fold_in(rng, 6), axis_at), (parts,), jnp.float32, least / len(shards), high / len(shards))
        return jnp.repeat(jnp.exp(heights), dims[axis_at] // parts).reshape((-1,) + (1,) * (len(dims) - axis_at - 1))

    loudness = one(*shards[0])
    for cut in shards[1:]:
        loudness = loudness * one(*cut)
    return loudness


def gaussian(stream_key, dims, scale, bound, cuts=(), kind=jnp.bfloat16):
    result = scale * jax.random.normal(stream_key, dims, jnp.float32)
    if cuts:
        result = result * shard_levels(stream_key, dims, cuts, -0.22, 0.18)
    return jnp.clip(result, -bound, bound).astype(kind)


def setup_inputs(seed: int = 0) -> dict:
    splits = jax.random.split(jax.random.key(seed), 11)
    return {
        "latents": draw_latents(jax.random.fold_in(splits[10], 71), 0),
        "row_valid": draw_row_valid(jax.random.fold_in(splits[10], 71), 0),
        "norm_gain": jnp.clip(1.0 + 0.15 * jax.random.normal(splits[2], (C,), jnp.float32), 0.25, 1.75),
        "conv_weight": gaussian(splits[3], (27 * C, C), (27 * C) ** -0.5, 0.0625, ((0, 4),)),
        "attn_gain": jnp.clip(1.0 + 0.15 * jax.random.normal(splits[4], (C,), jnp.float32), 0.25, 1.75),
        "w_query": draw_w_query(jax.random.fold_in(splits[10], 71), 0),
        "w_key": draw_w_key(jax.random.fold_in(splits[10], 71), 0),
        "w_value": gaussian(splits[7], (C, C), C ** -0.5, 0.3125),
        "w_out": gaussian(splits[8], (C, C), C ** -0.5, 0.3125),
        "cotangent": gaussian(splits[9], (FRAMES, H, W, C), 1.0, 6.0, ((0, 4), (1, 8))),
    }


epsilon = 1e-06

def silu_slope(inputs):
    logistic = jax.nn.sigmoid(inputs)
    return logistic * (1.0 + inputs * (1.0 - logistic))

def rounded_terms(terms):
    return lax.optimization_barrier(terms.astype(jnp.bfloat16)).astype(jnp.float32)

def frame_backward(queries, keys_all, values_all, d_attended, key_flags):
    channels = queries.shape[1]
    inv_root = 1.0 / math.sqrt(channels)
    slab_size = R_DEV * W
    block_q = queries.reshape(N_ROWS, slab_size, channels)
    block_d = d_attended.reshape(N_ROWS, slab_size, channels)

    def one_slab(running, pair_in):
        slab_q, slab_d = pair_in
        scores = jnp.dot(slab_q, keys_all.T, preferred_element_type=jnp.float32) * inv_root
        scores = jnp.where(key_flags[None, :] > 0, scores, -jnp.inf)
        row_max = lax.optimization_barrier(jnp.max(scores, axis=1, keepdims=True))
        exponent = jnp.exp(scores - row_max)
        weights = exponent / lax.optimization_barrier(jnp.sum(exponent, axis=1, keepdims=True))
        weights_b = weights.astype(jnp.bfloat16)
        attended = jnp.dot(weights_b, values_all, preferred_element_type=jnp.float32).astype(jnp.bfloat16)
        d_weights = jnp.dot(slab_d, values_all.T, preferred_element_type=jnp.float32)
        row_delta = lax.optimization_barrier(jnp.sum(slab_d.astype(jnp.float32) * attended.astype(jnp.float32), axis=1, keepdims=True))
        d_scores = (weights * (d_weights - row_delta) * inv_root).astype(jnp.bfloat16)
        d_query = jnp.dot(d_scores, keys_all, preferred_element_type=jnp.float32).astype(jnp.bfloat16)
        key_term = rounded_terms(jnp.dot(d_scores.T, slab_q, preferred_element_type=jnp.float32))
        value_term = rounded_terms(jnp.dot(weights_b.T, slab_d, preferred_element_type=jnp.float32))
        return ((running[0] + key_term, running[1] + value_term), (attended, d_query))
    start_sums = (jnp.zeros(keys_all.shape, jnp.float32), jnp.zeros(values_all.shape, jnp.float32))
    key_value, per_slab = lax.scan(one_slab, start_sums, (block_q, block_d))
    attended = per_slab[0].reshape(-1, channels)
    d_query = per_slab[1].reshape(-1, channels)
    return (attended, d_query, key_value[0].astype(jnp.bfloat16), key_value[1].astype(jnp.bfloat16))

def reference(latents, row_valid, norm_gain, conv_weight, attn_gain, w_query, w_key, w_value, w_out, cotangent):
    frame_count, height, col_count, channels = latents.shape
    frame_cells = height * col_count
    cell_total = frame_count * frame_cells
    grad_scale = 1.0 / math.sqrt(cell_total)
    cell_factor = jnp.broadcast_to(row_valid.astype(jnp.float32)[None, :, None], (frame_count, height, col_count)).reshape(cell_total, 1)
    inputs = latents.reshape(cell_total, channels).astype(jnp.float32)
    first_scale = lax.rsqrt(lax.optimization_barrier(jnp.mean(inputs * inputs, axis=1, keepdims=True)) + epsilon)
    normed_one = inputs * first_scale
    gated_in = normed_one * norm_gain
    conv_in = (jax.nn.silu(gated_in) * cell_factor).astype(jnp.bfloat16).reshape(frame_count, height, col_count, channels)
    history = jnp.pad(conv_in, ((2, 0), (1, 1), (1, 1), (0, 0)))
    conv_out = jnp.zeros((cell_total, channels), jnp.float32)
    for time_tap in range(3):
        for row_tap in range(3):
            for col_tap in range(3):
                tap_index = 9 * time_tap + 3 * row_tap + col_tap
                tap_rows = history[time_tap:time_tap + frame_count, row_tap:row_tap + height, col_tap:col_tap + col_count].reshape(cell_total, channels)
                conv_out = conv_out + jnp.dot(tap_rows, conv_weight[tap_index * channels:(tap_index + 1) * channels], preferred_element_type=jnp.float32)
    mixed_out = (inputs + conv_out).astype(jnp.bfloat16)
    mixed_f = mixed_out.astype(jnp.float32)
    second_scale = lax.rsqrt(lax.optimization_barrier(jnp.mean(mixed_f * mixed_f, axis=1, keepdims=True)) + epsilon)
    normed_two = mixed_f * second_scale
    attn_in = (normed_two * attn_gain).astype(jnp.bfloat16)
    queries = jnp.dot(attn_in, w_query, preferred_element_type=jnp.float32).astype(jnp.bfloat16)
    keys_own = jnp.dot(attn_in, w_key, preferred_element_type=jnp.float32).astype(jnp.bfloat16)
    values_own = jnp.dot(attn_in, w_value, preferred_element_type=jnp.float32).astype(jnp.bfloat16)
    live_cells = cell_factor > 0
    grad_out = jnp.where(live_cells, cotangent.reshape(cell_total, channels), jnp.zeros((), jnp.bfloat16))
    d_attended = jnp.dot(grad_out, w_out.T, preferred_element_type=jnp.float32).astype(jnp.bfloat16)
    key_flags = jnp.repeat(row_valid.astype(jnp.bfloat16), col_count)

    def per_frame(frame_in):
        frame_q, frame_k, frame_v, frame_d = frame_in
        return frame_backward(frame_q, frame_k, frame_v, frame_d, key_flags)
    framed = (queries.reshape(frame_count, frame_cells, channels), keys_own.reshape(frame_count, frame_cells, channels), values_own.reshape(frame_count, frame_cells, channels), d_attended.reshape(frame_count, frame_cells, channels))
    attended, d_query, d_key, d_value = lax.map(per_frame, framed)
    attended = attended.reshape(cell_total, channels)
    d_query = d_query.reshape(cell_total, channels)
    d_key = d_key.reshape(cell_total, channels)
    d_value = d_value.reshape(cell_total, channels)
    attn_weight_grad = jnp.concatenate([jnp.dot(attn_in.T, d_query, preferred_element_type=jnp.float32), jnp.dot(attn_in.T, d_key, preferred_element_type=jnp.float32), jnp.dot(attn_in.T, d_value, preferred_element_type=jnp.float32), jnp.dot(attended.T, grad_out, preferred_element_type=jnp.float32)], axis=0) * grad_scale
    d_normed = jnp.dot(d_query, w_query.T, preferred_element_type=jnp.float32) + jnp.dot(d_key, w_key.T, preferred_element_type=jnp.float32) + jnp.dot(d_value, w_value.T, preferred_element_type=jnp.float32)
    scaled_two = attn_gain * d_normed
    d_mixed = grad_out.astype(jnp.float32) + second_scale * (scaled_two - normed_two * lax.optimization_barrier(jnp.mean(scaled_two * normed_two, axis=1, keepdims=True)))
    d_conv = d_mixed.astype(jnp.bfloat16)
    spread_block = jnp.pad(d_conv.reshape(frame_count, height, col_count, channels), ((0, 2), (1, 1), (1, 1), (0, 0)))
    d_input = jnp.zeros((cell_total, channels), jnp.float32)
    grad_blocks = []
    for time_tap in range(3):
        for row_tap in range(3):
            for col_tap in range(3):
                tap_index = 9 * time_tap + 3 * row_tap + col_tap
                tap_rows = history[time_tap:time_tap + frame_count, row_tap:row_tap + height, col_tap:col_tap + col_count].reshape(cell_total, channels)
                grad_blocks.append(jnp.dot(tap_rows.T, d_conv, preferred_element_type=jnp.float32) * grad_scale)
                ahead_rows = spread_block[2 - time_tap:2 - time_tap + frame_count, 2 - row_tap:2 - row_tap + height, 2 - col_tap:2 - col_tap + col_count].reshape(cell_total, channels)
                d_input = d_input + jnp.dot(ahead_rows, conv_weight[tap_index * channels:(tap_index + 1) * channels].T, preferred_element_type=jnp.float32)
    conv_weight_grad = jnp.concatenate(grad_blocks, axis=0)
    d_input = d_input * cell_factor
    scaled_one = norm_gain * d_input * silu_slope(gated_in)
    input_grad = d_mixed + first_scale * (scaled_one - normed_one * lax.optimization_barrier(jnp.mean(scaled_one * normed_one, axis=1, keepdims=True)))
    return (input_grad.astype(jnp.bfloat16).reshape(latents.shape), conv_weight_grad, attn_weight_grad)
```

```python
import functools
import math

import jax
import jax.numpy as jnp
from jax import lax
from jax.experimental import pallas as pl
from jax.experimental.pallas import tpu as pltpu
from jax.sharding import PartitionSpec as P

epsilon = 1e-06
MESH = pl.DeviceIdType.MESH
ANY = pl.BlockSpec(memory_space=pl.ANY)
IN_VMEM = pl.BlockSpec(memory_space=pltpu.VMEM)
FLAG_ROWS = 16


def contract_last(first_op, second_op):
    return lax.dot_general(
        first_op, second_op, (((1,), (1,)), ((), ())), preferred_element_type=jnp.float32
    )


def contract_first(first_op, second_op):
    return lax.dot_general(
        first_op, second_op, (((0,), (0,)), ((), ())), preferred_element_type=jnp.float32
    )


def dot(first_op, second_op):
    return jnp.dot(first_op, second_op, preferred_element_type=jnp.float32)


def silu_slope(inputs):
    logistic = jax.nn.sigmoid(inputs)
    return logistic * (1.0 + inputs * (1.0 - logistic))


def params(collective_id, mebibytes=40):
    return pltpu.CompilerParams(
        collective_id=collective_id,
        has_side_effects=True,
        vmem_limit_bytes=mebibytes * 1024 * 1024,
    )


def signal(barrier, tm_at, row_at):
    pl.semaphore_signal(barrier, inc=1, device_id=(tm_at, row_at), device_id_type=MESH)


def remote(src, dst, send_sem, recv_sem, tm_at, row_at):
    return pltpu.make_async_remote_copy(
        src_ref=src,
        dst_ref=dst,
        send_sem=send_sem,
        recv_sem=recv_sem,
        device_id=(tm_at, row_at),
        device_id_type=MESH,
    )


def slabs_kernel(frames, slabs, x, o, local_sem, send_sem, recv_sem):
    t, r = lax.axis_index("tm"), lax.axis_index("rows")
    rows = x.shape[0]
    has_above, has_below = r > 0, r < slabs - 1
    others = [lax.rem(t + d, frames) for d in range(frames)]
    barrier = pltpu.get_barrier_semaphore()
    for d in range(1, frames):
        signal(barrier, others[d], r)

    @pl.when(has_above)
    def _():
        for d in range(frames):
            signal(barrier, others[d], r - 1)

    @pl.when(has_below)
    def _():
        for d in range(frames):
            signal(barrier, others[d], r + 1)

    sides = has_above.astype(jnp.int32) + has_below.astype(jnp.int32)
    pl.semaphore_wait(barrier, frames - 1 + frames * sides)

    own = pltpu.make_async_copy(x, o.at[t, pl.ds(1, rows)], local_sem)
    own.start()
    slab = [
        remote(x, o.at[t, pl.ds(1, rows)], send_sem.at[d], recv_sem.at[d], others[d], r)
        for d in range(1, frames)
    ]
    down = [
        remote(
            x.at[rows - 1],
            o.at[t, 0],
            send_sem.at[frames + d],
            recv_sem.at[frames + d],
            others[d],
            r + 1,
        )
        for d in range(frames)
    ]
    up = [
        remote(
            x.at[0],
            o.at[t, rows + 1],
            send_sem.at[2 * frames + d],
            recv_sem.at[2 * frames + d],
            others[d],
            r - 1,
        )
        for d in range(frames)
    ]

    @pl.when(has_below)
    def _():
        for copy in down:
            copy.start()

    @pl.when(has_above)
    def _():
        for copy in up:
            copy.start()

    for copy in slab:
        copy.start()
    own.wait()
    for copy in slab:
        copy.wait()

    @pl.when(has_below)
    def _():
        for copy in down:
            copy.wait_send()
        for copy in up:
            copy.wait_recv()

    @pl.when(has_above)
    def _():
        for copy in up:
            copy.wait_send()
        for copy in down:
            copy.wait_recv()


def gather_slabs(block, collective_id):
    frames, slabs = lax.axis_size("tm"), lax.axis_size("rows")
    rows, cols, channels = block.shape
    result = pl.pallas_call(
        functools.partial(slabs_kernel, frames, slabs),
        out_shape=jax.ShapeDtypeStruct((frames, rows + 2, cols, channels), block.dtype),
        in_specs=[ANY],
        out_specs=ANY,
        scratch_shapes=[
            pltpu.SemaphoreType.DMA,
            pltpu.SemaphoreType.DMA((3 * frames,)),
            pltpu.SemaphoreType.DMA((3 * frames,)),
        ],
        compiler_params=params(collective_id),
    )(block)
    r = lax.axis_index("rows")
    row_at = lax.broadcasted_iota(jnp.int32, (1, rows + 2, 1, 1), 1)
    inside = ((row_at > 0) | (r > 0)) & ((row_at < rows + 1) | (r < slabs - 1))
    return jnp.where(inside, result, jnp.zeros((), block.dtype))


def swap_kernel(frames, count, *refs):
    xs, os = refs[:count], refs[count : 2 * count]
    local_sem, send_sem, recv_sem = refs[2 * count :]
    t, r = lax.axis_index("tm"), lax.axis_index("rows")
    others = [lax.rem(t + d, frames) for d in range(frames)]
    barrier = pltpu.get_barrier_semaphore()
    for d in range(1, frames):
        signal(barrier, others[d], r)
    pl.semaphore_wait(barrier, frames - 1)
    copies = []
    for i, (x, o) in enumerate(zip(xs, os)):
        for d in range(1, frames):
            copies.append(
                remote(
                    x.at[others[d]], o.at[t], send_sem.at[i, d], recv_sem.at[i, d], others[d], r
                )
            )
        copies.append(pltpu.make_async_copy(x.at[t], o.at[t], local_sem.at[i]))
    for copy in copies:
        copy.start()
    for copy in copies:
        copy.wait()


def swap_over_tm(arrays, collective_id):
    frames, count = lax.axis_size("tm"), len(arrays)
    return pl.pallas_call(
        functools.partial(swap_kernel, frames, count),
        out_shape=[jax.ShapeDtypeStruct(a.shape, a.dtype) for a in arrays],
        in_specs=[ANY] * count,
        out_specs=[ANY] * count,
        scratch_shapes=[
            pltpu.SemaphoreType.DMA((count,)),
            pltpu.SemaphoreType.DMA((count, frames)),
            pltpu.SemaphoreType.DMA((count, frames)),
        ],
        compiler_params=params(collective_id),
    )(*arrays)


def halves_of(size):
    near = size // 2 // 16 * 16
    return ((0, near), (near, size - near))


def attention_kernel(frames, slabs, grad_scale, inv_root, *refs):
    (mixed, cotangent, flag_tile, gain, w_query, w_key, w_value, w_out) = refs[:8]
    (d_mixed_out, d_conv_out, stack_out) = refs[8:11]
    (cells, cells_t, prob, d_weights, tops, sums, dots, flags) = refs[11:19]
    (mine, near, ready, arrive, own_total, weighted_t, d_cells_t) = refs[19:26]
    (queries, key_side, value_side, d_attended, grad_out) = refs[26:31]
    (grads, grads_in) = refs[31:33]
    (flag_sems, sib_sems, hop_sems, hand_sems, near_sems, far_send, far_recv, grad_sems) = refs[33:]
    pairs = slabs // 2
    rows, cols, channels = cotangent.shape
    size = rows * cols
    halves = halves_of(size)
    t, r = lax.axis_index("tm"), lax.axis_index("rows")
    q, c = lax.div(r, 2), lax.rem(r, 2)
    other = 1 - c
    sibling = 2 * q + other
    frame_at = [lax.rem(t + d, frames) for d in range(frames)]
    slab_at = [lax.rem(r + d, slabs) for d in range(slabs)]
    barrier = pltpu.get_barrier_semaphore()
    for d in range(1, slabs):
        signal(barrier, t, slab_at[d])
    for d in range(1, frames):
        signal(barrier, frame_at[d], r)

    mixed_f = mixed[...].astype(jnp.float32)
    second_scale = lax.rsqrt(jnp.mean(mixed_f * mixed_f, axis=1, keepdims=True) + epsilon)
    attn_in = (mixed_f * second_scale * gain[...]).astype(jnp.bfloat16)
    cells[r] = attn_in
    flags[r] = flag_tile[...]
    pl.semaphore_wait(barrier, slabs + frames - 2)

    flag_copies = [
        remote(
            flag_tile, flags.at[r], flag_sems.at[0, d], flag_sems.at[1, d], t, slab_at[d]
        )
        for d in range(1, slabs)
    ]

    def sources(step, side):
        return q - step if side == 0 else q + step

    def arrives(step, side):
        at = sources(step, side)
        return jnp.logical_and(at >= 0, at < pairs)

    def onward(step, side):
        ahead = q < pairs - 1 if side == 0 else q > 0
        return jnp.logical_and(ahead, arrives(step, side))

    def hop(step, side, half):
        start, count = halves[half]
        part = cells.at[2 * sources(step - 1, side) + c, pl.ds(start, count)]
        target = r + 2 if side == 0 else r - 2
        return remote(
            part, part, hop_sems.at[0, side, step, half], hop_sems.at[1, side, step, half], t, target
        )

    def hand(step, side):
        part = cells.at[2 * sources(step, side) + c]
        return remote(
            part, part, hand_sems.at[0, side, step], hand_sems.at[1, side, step], t, sibling
        )

    to_sibling = remote(cells.at[r], cells.at[r], sib_sems.at[0], sib_sems.at[1], t, sibling)
    for half in range(2):
        for side in range(2):

            @pl.when(onward(0, side))
            def _():
                hop(1, side, half).start()

    to_sibling.start()
    for copy in flag_copies:
        copy.start()

    for h in range(rows):
        flag = flag_tile[h : h + 1, 0:1].astype(jnp.float32)
        part = cotangent[h].astype(jnp.float32)
        grad_out[h * cols : (h + 1) * cols, :] = jnp.where(flag > 0, part, 0.0).astype(jnp.bfloat16)
    queries[...] = dot(attn_in, w_query[...]).astype(jnp.bfloat16)
    key_side[...] = contract_last(queries[...], w_key[...]).astype(jnp.bfloat16)
    d_attended[...] = contract_last(grad_out[...], w_out[...]).astype(jnp.bfloat16)
    value_side[...] = contract_last(d_attended[...], w_value[...]).astype(jnp.bfloat16)
    for copy in flag_copies:
        copy.wait()

    lowest = float(jnp.finfo(jnp.float32).min)

    def absorb(j):
        block = cells[j]
        scores = contract_last(block, key_side[...]) * inv_root
        kept = []
        for h in range(rows):
            flag = flags[j, h : h + 1, 0:1].astype(jnp.float32)
            kept.append(jnp.where(flag > 0, scores[h * cols : (h + 1) * cols], lowest))
        scores = jnp.concatenate(kept, axis=0)
        top = jnp.max(scores, axis=0, keepdims=True)
        exponent = jnp.exp(scores - top)
        prob[j] = exponent
        d_weight = contract_last(block, value_side[...])
        d_weights[j] = d_weight
        tops[j] = top
        sums[j] = jnp.sum(exponent, axis=0, keepdims=True)
        dots[j] = jnp.sum(exponent * d_weight, axis=0, keepdims=True)
        cells_t[j] = block.T

    def absorb_pair(step, side):
        @pl.when(arrives(step, side))
        def _():
            base = 2 * sources(step, side)
            absorb(base + c)
            hand(step, side).wait_recv()
            absorb(base + other)

    def pass_on(step, half):
        for side in range(2):

            @pl.when(arrives(step, side))
            def _():
                hop(step, side, half).wait_recv()

            @pl.when(onward(step, side))
            def _():
                hop(step + 1, side, half).start()

            if half == 1:

                @pl.when(arrives(step, side))
                def _():
                    hand(step, side).start()

    def own_pair(i, carry):
        @pl.when(i == 1)
        def _():
            to_sibling.wait_recv()

        absorb(2 * q + c + i * (other - c))
        return carry

    lax.fori_loop(0, 2, own_pair, 0)
    pass_on(1, 0)
    pass_on(1, 1)
    for step in range(1, pairs):
        absorb_pair(step, 0)
        if step < pairs - 1:
            pass_on(step + 1, 0)
        absorb_pair(step, 1)
        if step < pairs - 1:
            pass_on(step + 1, 1)

    top_all = tops[0]
    for j in range(1, slabs):
        top_all = jnp.maximum(top_all, tops[j])
    total_sum = jnp.zeros_like(top_all)
    total_dot = jnp.zeros_like(top_all)
    for j in range(slabs):
        rescale = jnp.exp(tops[j] - top_all)
        total_sum = total_sum + rescale * sums[j]
        total_dot = total_dot + rescale * dots[j]
        tops[j] = rescale
    inverse = 1.0 / total_sum
    row_delta = total_dot * inverse
    weighted_t[...] = jnp.zeros_like(weighted_t)
    d_cells_t[...] = jnp.zeros_like(d_cells_t)

    def emit(j):
        weights = prob[j] * (tops[j] * inverse)
        weights_b = weights.astype(jnp.bfloat16)
        d_scores = (weights * (d_weights[j] - row_delta) * inv_root).astype(jnp.bfloat16)
        block_t = cells_t[j]
        weighted_t[...] += dot(block_t, weights_b)
        d_cells_t[...] += dot(block_t, d_scores)
        return dot(d_scores, key_side[...]) + dot(weights_b, value_side[...])

    def give(d):
        part = mine.at[d]
        return remote(part, near.at[d], near_sems.at[0, d], near_sems.at[1, d], t, sibling)

    def far(d, side, half):
        start, count = halves[half]
        target = r + 2 - 4 * side
        return remote(
            ready.at[d, pl.ds(start, count)],
            arrive.at[side, d, pl.ds(start, count)],
            far_send.at[d, half],
            far_recv.at[side, d, half],
            t,
            target,
        )

    low_half = (q < (pairs + 1) // 2).astype(jnp.int32)
    right_count = pairs - 1 - q

    def chip_order(i):
        from_right = pairs - 1 - i
        low_order = jnp.where(i < right_count, from_right, i - right_count)
        high_order = jnp.where(i < q, i, pairs - 1 - (i - q))
        order = low_half * low_order + (1 - low_half) * high_order
        return jnp.where(i == pairs - 1, q, order)

    def one_chip(i, carry):
        d = chip_order(i)
        mine[d] = emit(2 * d + other).astype(jnp.bfloat16)
        give(d).start()
        term = emit(2 * d + c)
        give(d).wait_recv()
        term = term + near[d].astype(jnp.float32)

        @pl.when(i == pairs - 1)
        def _():
            own_total[...] = term

        @pl.when(i < pairs - 1)
        def _():
            ready[d] = term.astype(jnp.bfloat16)

        @pl.when(jnp.logical_and(q == 0, d > q))
        def _():
            far(d, 0, 0).start()
            far(d, 0, 1).start()

        @pl.when(jnp.logical_and(q == pairs - 1, d < q))
        def _():
            far(d, 1, 0).start()
            far(d, 1, 1).start()

        return carry

    lax.fori_loop(0, pairs, one_chip, 0)

    weighted_b = weighted_t[...].astype(jnp.bfloat16)
    d_cells_b = d_cells_t[...].astype(jnp.bfloat16)
    attended = contract_first(weighted_b, w_value[...]).astype(jnp.bfloat16)
    d_query = contract_first(d_cells_b, w_key[...]).astype(jnp.bfloat16)
    blocks = [
        contract_first(cells[r], d_query),
        dot(d_cells_b, queries[...]),
        dot(weighted_b, d_attended[...]),
        contract_first(attended, grad_out[...]),
    ]
    for i, block in enumerate(blocks):
        grads[i * channels : (i + 1) * channels, :] = (block * grad_scale).astype(jnp.bfloat16)
    share = 4 * channels // frames
    grad_copies = [
        remote(
            grads.at[pl.ds(pl.multiple_of(frame_at[d] * share, share), share)],
            grads_in.at[d],
            grad_sems.at[0, d],
            grad_sems.at[1, d],
            frame_at[d],
            r,
        )
        for d in range(1, frames)
    ]
    for copy in grad_copies:
        copy.start()
    own_total[...] += contract_last(d_query, w_query[...])

    def relay(phase, carry):
        side = jnp.where(phase == 0, 1 - low_half, low_half)
        has_up = jnp.where(side == 0, q > 0, q < pairs - 1)
        count = jnp.where(side == 0, right_count, q)

        def one(i, carry):
            d = jnp.where(side == 0, pairs - 1 - i, i)

            @pl.when(jnp.logical_and(has_up, i < count))
            def _():
                for half in range(2):
                    start, length = halves[half]
                    part = pl.ds(start, length)
                    far(d, side, half).wait_recv()
                    ready[d, part] = (
                        ready[d, part].astype(jnp.float32)
                        + arrive[side, d, part].astype(jnp.float32)
                    ).astype(jnp.bfloat16)
                    far(d, side, half).start()

            return carry

        return lax.fori_loop(0, pairs - 1, one, carry)

    lax.fori_loop(0, 2, relay, 0)

    for copy in grad_copies:
        copy.wait_recv()
    stack = grads[pl.ds(pl.multiple_of(t * share, share), share), :].astype(jnp.float32)
    for d in range(1, frames):
        stack = stack + grads_in[d].astype(jnp.float32)
    stack_out[...] = stack.astype(stack_out.dtype)

    for side in range(2):

        @pl.when(q > 0 if side == 0 else q < pairs - 1)
        def _():
            for half in range(2):
                start, length = halves[half]
                far(q, side, half).wait_recv()
                part = pl.ds(start, length)
                own_total[part, :] += arrive[side, q, part].astype(jnp.float32)

    mixed_f = mixed[...].astype(jnp.float32)
    second_scale = lax.rsqrt(jnp.mean(mixed_f * mixed_f, axis=1, keepdims=True) + epsilon)
    normed_two = mixed_f * second_scale
    scaled_two = gain[...] * own_total[...]
    d_mixed = grad_out[...].astype(jnp.float32) + second_scale * (
        scaled_two - normed_two * jnp.mean(scaled_two * normed_two, axis=1, keepdims=True)
    )
    d_mixed_out[...] = d_mixed
    d_conv_out[...] = d_mixed.astype(jnp.bfloat16).reshape(rows, cols, channels)

    to_sibling.wait_send()
    for side in range(2):
        for step in range(1, pairs):

            @pl.when(onward(step - 1, side))
            def _():
                for half in range(2):
                    hop(step, side, half).wait_send()

            @pl.when(arrives(step, side))
            def _():
                hand(step, side).wait_send()

    for d in range(pairs):
        give(d).wait_send()

        @pl.when(q != d)
        def _():
            for half in range(2):
                far(d, 0, half).wait_send()

    for copy in grad_copies:
        copy.wait_send()


def attend(mixed, cotangent, flag_tile, gain, w_query, w_key, w_value, w_out, scales, collective_id):
    frames, slabs = lax.axis_size("tm"), lax.axis_size("rows")
    pairs = slabs // 2
    rows, cols, channels = cotangent.shape
    size = rows * cols
    bf16, f32 = jnp.bfloat16, jnp.float32
    share = 4 * channels // frames
    dma = pltpu.SemaphoreType.DMA
    return pl.pallas_call(
        functools.partial(attention_kernel, frames, slabs, *scales),
        out_shape=[
            jax.ShapeDtypeStruct((size, channels), f32),
            jax.ShapeDtypeStruct((rows, cols, channels), bf16),
            jax.ShapeDtypeStruct((share, channels), bf16),
        ],
        in_specs=[IN_VMEM] * 8,
        out_specs=[IN_VMEM] * 3,
        scratch_shapes=[
            pltpu.VMEM((slabs, size, channels), bf16),
            pltpu.VMEM((slabs, channels, size), bf16),
            pltpu.VMEM((slabs, size, size), f32),
            pltpu.VMEM((slabs, size, size), f32),
            pltpu.VMEM((slabs, 1, size), f32),
            pltpu.VMEM((slabs, 1, size), f32),
            pltpu.VMEM((slabs, 1, size), f32),
            pltpu.VMEM((slabs,) + flag_tile.shape, bf16),
            pltpu.VMEM((pairs, size, channels), bf16),
            pltpu.VMEM((pairs, size, channels), bf16),
            pltpu.VMEM((pairs, size, channels), bf16),
            pltpu.VMEM((2, pairs, size, channels), bf16),
            pltpu.VMEM((size, channels), f32),
            pltpu.VMEM((channels, size), f32),
            pltpu.VMEM((channels, size), f32),
            pltpu.VMEM((size, channels), bf16),
            pltpu.VMEM((size, channels), bf16),
            pltpu.VMEM((size, channels), bf16),
            pltpu.VMEM((size, channels), bf16),
            pltpu.VMEM((size, channels), bf16),
            pltpu.VMEM((4 * channels, channels), bf16),
            pltpu.VMEM((frames, share, channels), bf16),
            dma((2, slabs)),
            dma((2,)),
            dma((2, 2, pairs + 1, 2)),
            dma((2, 2, pairs)),
            dma((2, pairs)),
            dma((pairs, 2)),
            dma((2, pairs, 2)),
            dma((2, frames)),
        ],
        compiler_params=params(collective_id, 62),
    )(mixed, cotangent, flag_tile, gain, w_query, w_key, w_value, w_out)


def column_shifts(slabs, before, after):
    cols = slabs.shape[2]
    width = -(-cols // 16) * 16
    spare = width - cols
    edges = ((before, after), (0, 0))
    return jnp.stack(
        [jnp.pad(slabs, edges + ((1, spare - 1), (0, 0)))]
        + [jnp.pad(slabs, edges + ((0, spare), (0, 0)))]
        + [jnp.pad(slabs[:, :, 1:], edges + ((0, spare + 1), (0, 0)))]
    )


def taps_kernel(rows, cols, transposed, taps, shifted, weight, out, columns):
    f = pl.program_id(0)
    width, channels = shifted.shape[3:]
    count = taps.shape[0]
    total = None
    for j in range(count):
        window = shifted[taps[j, 2], taps[j, 0] + f, pl.ds(taps[j, 1], rows)]
        window = window.reshape(rows * width, channels)
        columns[:, j * channels : (j + 1) * channels] = window
        if transposed:
            term = contract_last(window, weight[j * channels : (j + 1) * channels, :])
            total = term if total is None else total + term
    if not transposed:
        total = dot(columns[...], weight[...])
    total = total.astype(out.dtype).reshape(rows, width, channels)
    out[0] = total[:, :cols]


def sum_taps(shifted, taps, weight, rows, cols, transposed):
    frames = shifted.shape[1] - 2
    width, channels = shifted.shape[3:]
    count = taps.shape[0]
    out = jax.ShapeDtypeStruct((frames, rows, cols, channels), jnp.bfloat16)
    out_spec = pl.BlockSpec((1, rows, cols, channels), lambda f: (f, 0, 0, 0))
    block = (rows * width, count * channels)
    columns = jax.ShapeDtypeStruct((frames * block[0], block[1]), jnp.bfloat16)
    columns_spec = pl.BlockSpec(block, lambda f: (f, 0))
    flops = 2 * frames * block[0] * block[1] * channels
    return pl.pallas_call(
        functools.partial(taps_kernel, rows, cols, transposed),
        grid=(frames,),
        out_shape=out if transposed else (out, columns),
        in_specs=[pl.BlockSpec(memory_space=pltpu.SMEM), IN_VMEM, IN_VMEM],
        out_specs=out_spec if transposed else (out_spec, columns_spec),
        scratch_shapes=[pltpu.VMEM(block, jnp.bfloat16)] if transposed else [],
        cost_estimate=pl.CostEstimate(flops=flops, bytes_accessed=20_000_000, transcendentals=0),
        compiler_params=pltpu.CompilerParams(vmem_limit_bytes=48 * 1024 * 1024),
    )(taps, shifted, weight)


def per_device(
    latents, row_valid, norm_gain, conv_weight, attn_gain, w_query, w_key, w_value, w_out, cotangent
):
    bf16 = jnp.bfloat16
    shape_all = latents.shape
    rows_dev, col_count, channels = shape_all[1:]
    slab_size = rows_dev * col_count
    frames, slabs = lax.axis_size("tm"), lax.axis_size("rows")
    t = lax.axis_index("tm")
    grad_scale = 1.0 / math.sqrt(frames * slabs * slab_size)
    inv_root = 1.0 / math.sqrt(channels)

    own_rows = conv_weight.shape[0]
    tap_total = own_rows * frames // channels
    tap_count = max(
        -(-((i * own_rows) % channels + own_rows) // channels) for i in range(frames)
    )
    first_tap = lax.div(t * own_rows, channels)
    weight_from = t * own_rows - first_tap * channels
    own_weight = lax.dynamic_update_slice(
        jnp.zeros((tap_count * channels, channels), bf16), conv_weight, (weight_from, 0)
    )
    k = jnp.minimum(first_tap + jnp.arange(tap_count, dtype=jnp.int32), tap_total - 1)
    taps = jnp.stack([k // 9, k % 9 // 3, k % 3], axis=1)

    cell_factor = jnp.repeat(row_valid.astype(jnp.float32), col_count)[:, None]
    inputs = latents.reshape(slab_size, channels).astype(jnp.float32)
    first_scale = lax.rsqrt(jnp.mean(inputs * inputs, axis=1, keepdims=True) + epsilon)
    normed_one = inputs * first_scale
    gated_in = normed_one * norm_gain
    conv_in = (jax.nn.silu(gated_in) * cell_factor).astype(bf16)

    history = gather_slabs(conv_in.reshape(rows_dev, col_count, channels), 0)
    conv_terms, columns = sum_taps(
        column_shifts(history, 2, 0), taps, own_weight, rows_dev, col_count, False
    )
    conv_terms = conv_terms.reshape(frames, slab_size, channels)
    (conv_terms,) = swap_over_tm([conv_terms], 1)
    conv_out = jnp.sum(conv_terms.astype(jnp.float32), axis=0)

    mixed = (inputs + conv_out).astype(bf16)
    flag_tile = jnp.pad(row_valid.astype(bf16), (0, FLAG_ROWS - rows_dev))
    flag_tile = jnp.broadcast_to(flag_tile[:, None], (FLAG_ROWS, 128))
    d_mixed, d_conv, stack = attend(
        mixed,
        cotangent.reshape(shape_all[1:]),
        flag_tile,
        attn_gain[None],
        w_query,
        w_key,
        w_value,
        w_out,
        (grad_scale, inv_root),
        2,
    )
    attn_weight_grad = lax.psum_scatter(stack, "rows", scatter_dimension=0, tiled=True)
    attn_weight_grad = attn_weight_grad.astype(jnp.float32)

    spread = gather_slabs(d_conv, 4)
    spare = columns.shape[0] // (frames * rows_dev) - col_count
    d_conv_all = jnp.pad(spread[:, 1 : 1 + rows_dev], ((0, 0), (0, 0), (0, spare), (0, 0)))
    weight_terms = contract_first(columns, d_conv_all.reshape(-1, channels)) * grad_scale
    weight_terms = lax.dynamic_slice(
        weight_terms.astype(bf16), (weight_from, 0), (own_rows, channels)
    )
    block_rows = own_rows // slabs
    padded_rows = -(-block_rows // 16) * 16
    weight_terms = jnp.pad(
        weight_terms.reshape(slabs, block_rows, channels),
        ((0, 0), (0, padded_rows - block_rows), (0, 0)),
    )
    weight_sums = lax.psum_scatter(
        weight_terms.reshape(slabs * padded_rows, channels), "rows", scatter_dimension=0, tiled=True
    )
    conv_weight_grad = weight_sums[:block_rows].astype(jnp.float32)

    input_terms = sum_taps(
        column_shifts(spread, 0, 2), 2 - taps, own_weight, rows_dev, col_count, True
    )
    (input_terms,) = swap_over_tm([input_terms.reshape(frames, slab_size, channels)], 5)
    d_input = jnp.sum(input_terms.astype(jnp.float32), axis=0) * cell_factor
    scaled_one = norm_gain * d_input * silu_slope(gated_in)
    input_grad = d_mixed + first_scale * (
        scaled_one - normed_one * jnp.mean(scaled_one * normed_one, axis=1, keepdims=True)
    )
    return (input_grad.astype(bf16).reshape(shape_all), conv_weight_grad, attn_weight_grad)


def solution(mesh):
    return jax.shard_map(
        per_device,
        mesh=mesh,
        in_specs=(
            P("tm", "rows", None, None),
            P("rows"),
            P(),
            P("tm", None),
            P(),
            P(),
            P(),
            P(),
            P(),
            P("tm", "rows", None, None),
        ),
        out_specs=(P("tm", "rows", None, None), P(("tm", "rows"), None), P(("tm", "rows"), None)),
        check_vma=False,
    )
```

```python
import functools
import math

import jax
import jax.numpy as jnp
from jax import lax
from jax.experimental import pallas as pl
from jax.experimental.pallas import tpu as pltpu
from jax.sharding import PartitionSpec as P

epsilon = 1e-06
MESH = pl.DeviceIdType.MESH
ANY = pl.BlockSpec(memory_space=pl.ANY)
IN_VMEM = pl.BlockSpec(memory_space=pltpu.VMEM)
FLAG_ROWS = 16


def contract_last(first_op, second_op):
    return lax.dot_general(
        first_op, second_op, (((1,), (1,)), ((), ())), preferred_element_type=jnp.float32
    )


def contract_first(first_op, second_op):
    return lax.dot_general(
        first_op, second_op, (((0,), (0,)), ((), ())), preferred_element_type=jnp.float32
    )


def dot(first_op, second_op):
    return jnp.dot(first_op, second_op, preferred_element_type=jnp.float32)


def silu_slope(inputs):
    logistic = jax.nn.sigmoid(inputs)
    return logistic * (1.0 + inputs * (1.0 - logistic))


def params(collective_id, mebibytes=40):
    return pltpu.CompilerParams(
        collective_id=collective_id,
        has_side_effects=True,
        vmem_limit_bytes=mebibytes * 1024 * 1024,
    )


def signal(barrier, tm_at, row_at):
    pl.semaphore_signal(barrier, inc=1, device_id=(tm_at, row_at), device_id_type=MESH)


def remote(src, dst, send_sem, recv_sem, tm_at, row_at):
    return pltpu.make_async_remote_copy(
        src_ref=src,
        dst_ref=dst,
        send_sem=send_sem,
        recv_sem=recv_sem,
        device_id=(tm_at, row_at),
        device_id_type=MESH,
    )


def slabs_kernel(frames, slabs, x, o, local_sem, send_sem, recv_sem):
    t, r = lax.axis_index("tm"), lax.axis_index("rows")
    rows = x.shape[0]
    has_above, has_below = r > 0, r < slabs - 1
    others = [lax.rem(t + d, frames) for d in range(frames)]
    barrier = pltpu.get_barrier_semaphore()
    for d in range(1, frames):
        signal(barrier, others[d], r)

    @pl.when(has_above)
    def _():
        for d in range(frames):
            signal(barrier, others[d], r - 1)

    @pl.when(has_below)
    def _():
        for d in range(frames):
            signal(barrier, others[d], r + 1)

    sides = has_above.astype(jnp.int32) + has_below.astype(jnp.int32)
    pl.semaphore_wait(barrier, frames - 1 + frames * sides)

    own = pltpu.make_async_copy(x, o.at[t, pl.ds(1, rows)], local_sem)
    own.start()
    slab = [
        remote(x, o.at[t, pl.ds(1, rows)], send_sem.at[d], recv_sem.at[d], others[d], r)
        for d in range(1, frames)
    ]
    down = [
        remote(
            x.at[rows - 1],
            o.at[t, 0],
            send_sem.at[frames + d],
            recv_sem.at[frames + d],
            others[d],
            r + 1,
        )
        for d in range(frames)
    ]
    up = [
        remote(
            x.at[0],
            o.at[t, rows + 1],
            send_sem.at[2 * frames + d],
            recv_sem.at[2 * frames + d],
            others[d],
            r - 1,
        )
        for d in range(frames)
    ]

    @pl.when(has_below)
    def _():
        for copy in down:
            copy.start()

    @pl.when(has_above)
    def _():
        for copy in up:
            copy.start()

    for copy in slab:
        copy.start()
    own.wait()
    for copy in slab:
        copy.wait()

    @pl.when(has_below)
    def _():
        for copy in down:
            copy.wait_send()
        for copy in up:
            copy.wait_recv()

    @pl.when(has_above)
    def _():
        for copy in up:
            copy.wait_send()
        for copy in down:
            copy.wait_recv()


def gather_slabs(block, collective_id):
    frames, slabs = lax.axis_size("tm"), lax.axis_size("rows")
    rows, cols, channels = block.shape
    result = pl.pallas_call(
        functools.partial(slabs_kernel, frames, slabs),
        out_shape=jax.ShapeDtypeStruct((frames, rows + 2, cols, channels), block.dtype),
        in_specs=[ANY],
        out_specs=ANY,
        scratch_shapes=[
            pltpu.SemaphoreType.DMA,
            pltpu.SemaphoreType.DMA((3 * frames,)),
            pltpu.SemaphoreType.DMA((3 * frames,)),
        ],
        compiler_params=params(collective_id),
    )(block)
    r = lax.axis_index("rows")
    row_at = lax.broadcasted_iota(jnp.int32, (1, rows + 2, 1, 1), 1)
    inside = ((row_at > 0) | (r > 0)) & ((row_at < rows + 1) | (r < slabs - 1))
    return jnp.where(inside, result, jnp.zeros((), block.dtype))


def swap_kernel(frames, count, *refs):
    xs, os = refs[:count], refs[count : 2 * count]
    local_sem, send_sem, recv_sem = refs[2 * count :]
    t, r = lax.axis_index("tm"), lax.axis_index("rows")
    others = [lax.rem(t + d, frames) for d in range(frames)]
    barrier = pltpu.get_barrier_semaphore()
    for d in range(1, frames):
        signal(barrier, others[d], r)
    pl.semaphore_wait(barrier, frames - 1)
    copies = []
    for i, (x, o) in enumerate(zip(xs, os)):
        for d in range(1, frames):
            copies.append(
                remote(
                    x.at[others[d]], o.at[t], send_sem.at[i, d], recv_sem.at[i, d], others[d], r
                )
            )
        copies.append(pltpu.make_async_copy(x.at[t], o.at[t], local_sem.at[i]))
    for copy in copies:
        copy.start()
    for copy in copies:
        copy.wait()


def swap_over_tm(arrays, collective_id):
    frames, count = lax.axis_size("tm"), len(arrays)
    return pl.pallas_call(
        functools.partial(swap_kernel, frames, count),
        out_shape=[jax.ShapeDtypeStruct(a.shape, a.dtype) for a in arrays],
        in_specs=[ANY] * count,
        out_specs=[ANY] * count,
        scratch_shapes=[
            pltpu.SemaphoreType.DMA((count,)),
            pltpu.SemaphoreType.DMA((count, frames)),
            pltpu.SemaphoreType.DMA((count, frames)),
        ],
        compiler_params=params(collective_id),
    )(*arrays)


def halves_of(size):
    near = size // 2 // 16 * 16
    return ((0, near), (near, size - near))


def attention_kernel(frames, slabs, grad_scale, inv_root, *refs):
    (mixed, cotangent, flag_tile, gain, w_query, w_key, w_value, w_out) = refs[:8]
    (d_mixed_out, d_conv_out, stack_out) = refs[8:11]
    (cells, cells_t, prob, d_weights, tops, sums, dots, flags) = refs[11:19]
    (mine, near, ready, arrive, own_total, weighted_t, d_cells_t) = refs[19:26]
    (queries, key_side, value_side, d_attended, grad_out) = refs[26:31]
    (grads, grads_in) = refs[31:33]
    (flag_sems, sib_sems, hop_sems, hand_sems, near_sems, far_send, far_recv, grad_sems) = refs[33:]
    pairs = slabs // 2
    rows, cols, channels = cotangent.shape
    size = rows * cols
    halves = halves_of(size)
    t, r = lax.axis_index("tm"), lax.axis_index("rows")
    q, c = lax.div(r, 2), lax.rem(r, 2)
    other = 1 - c
    sibling = 2 * q + other
    frame_at = [lax.rem(t + d, frames) for d in range(frames)]
    slab_at = [lax.rem(r + d, slabs) for d in range(slabs)]
    barrier = pltpu.get_barrier_semaphore()
    for d in range(1, slabs):
        signal(barrier, t, slab_at[d])
    for d in range(1, frames):
        signal(barrier, frame_at[d], r)

    mixed_f = mixed[...].astype(jnp.float32)
    second_scale = lax.rsqrt(jnp.mean(mixed_f * mixed_f, axis=1, keepdims=True) + epsilon)
    attn_in = (mixed_f * second_scale * gain[...]).astype(jnp.bfloat16)
    cells[r] = attn_in
    flags[r] = flag_tile[...]
    pl.semaphore_wait(barrier, slabs + frames - 2)

    flag_copies = [
        remote(
            flag_tile, flags.at[r], flag_sems.at[0, d], flag_sems.at[1, d], t, slab_at[d]
        )
        for d in range(1, slabs)
    ]

    def sources(step, side):
        return q - step if side == 0 else q + step

    def arrives(step, side):
        at = sources(step, side)
        return jnp.logical_and(at >= 0, at < pairs)

    def onward(step, side):
        ahead = q < pairs - 1 if side == 0 else q > 0
        return jnp.logical_and(ahead, arrives(step, side))

    def hop(step, side, half):
        start, count = halves[half]
        part = cells.at[2 * sources(step - 1, side) + c, pl.ds(start, count)]
        target = r + 2 if side == 0 else r - 2
        return remote(
            part, part, hop_sems.at[0, side, step, half], hop_sems.at[1, side, step, half], t, target
        )

    def hand(step, side):
        part = cells.at[2 * sources(step, side) + c]
        return remote(
            part, part, hand_sems.at[0, side, step], hand_sems.at[1, side, step], t, sibling
        )

    to_sibling = remote(cells.at[r], cells.at[r], sib_sems.at[0], sib_sems.at[1], t, sibling)
    for half in range(2):
        for side in range(2):

            @pl.when(onward(0, side))
            def _():
                hop(1, side, half).start()

    to_sibling.start()
    for copy in flag_copies:
        copy.start()

    for h in range(rows):
        flag = flag_tile[h : h + 1, 0:1].astype(jnp.float32)
        part = cotangent[h].astype(jnp.float32)
        grad_out[h * cols : (h + 1) * cols, :] = jnp.where(flag > 0, part, 0.0).astype(jnp.bfloat16)
    queries[...] = dot(attn_in, w_query[...]).astype(jnp.bfloat16)
    key_side[...] = contract_last(queries[...], w_key[...]).astype(jnp.bfloat16)
    d_attended[...] = contract_last(grad_out[...], w_out[...]).astype(jnp.bfloat16)
    value_side[...] = contract_last(d_attended[...], w_value[...]).astype(jnp.bfloat16)
    for copy in flag_copies:
        copy.wait()

    lowest = float(jnp.finfo(jnp.float32).min)

    def absorb(j):
        block = cells[j]
        scores = contract_last(block, key_side[...]) * inv_root
        kept = []
        for h in range(rows):
            flag = flags[j, h : h + 1, 0:1].astype(jnp.float32)
            kept.append(jnp.where(flag > 0, scores[h * cols : (h + 1) * cols], lowest))
        scores = jnp.concatenate(kept, axis=0)
        top = jnp.max(scores, axis=0, keepdims=True)
        exponent = jnp.exp(scores - top)
        prob[j] = exponent
        d_weight = contract_last(block, value_side[...])
        d_weights[j] = d_weight
        tops[j] = top
        sums[j] = jnp.sum(exponent, axis=0, keepdims=True)
        dots[j] = jnp.sum(exponent * d_weight, axis=0, keepdims=True)
        cells_t[j] = block.T

    def absorb_pair(step, side):
        @pl.when(arrives(step, side))
        def _():
            base = 2 * sources(step, side)
            absorb(base + c)
            hand(step, side).wait_recv()
            absorb(base + other)

    def pass_on(step, half):
        for side in range(2):

            @pl.when(arrives(step, side))
            def _():
                hop(step, side, half).wait_recv()

            @pl.when(onward(step, side))
            def _():
                hop(step + 1, side, half).start()

            if half == 1:

                @pl.when(arrives(step, side))
                def _():
                    hand(step, side).start()

    def own_pair(i, carry):
        @pl.when(i == 1)
        def _():
            to_sibling.wait_recv()

        absorb(2 * q + c + i * (other - c))
        return carry

    lax.fori_loop(0, 2, own_pair, 0)
    pass_on(1, 0)
    pass_on(1, 1)
    for step in range(1, pairs):
        absorb_pair(step, 0)
        if step < pairs - 1:
            pass_on(step + 1, 0)
        absorb_pair(step, 1)
        if step < pairs - 1:
            pass_on(step + 1, 1)

    top_all = tops[0]
    for j in range(1, slabs):
        top_all = jnp.maximum(top_all, tops[j])
    total_sum = jnp.zeros_like(top_all)
    total_dot = jnp.zeros_like(top_all)
    for j in range(slabs):
        rescale = jnp.exp(tops[j] - top_all)
        total_sum = total_sum + rescale * sums[j]
        total_dot = total_dot + rescale * dots[j]
        tops[j] = rescale
    inverse = 1.0 / total_sum
    row_delta = total_dot * inverse
    weighted_t[...] = jnp.zeros_like(weighted_t)
    d_cells_t[...] = jnp.zeros_like(d_cells_t)

    def emit(j):
        weights = prob[j] * (tops[j] * inverse)
        weights_b = weights.astype(jnp.bfloat16)
        d_scores = (weights * (d_weights[j] - row_delta) * inv_root).astype(jnp.bfloat16)
        block_t = cells_t[j]
        weighted_t[...] += dot(block_t, weights_b)
        d_cells_t[...] += dot(block_t, d_scores)
        return dot(d_scores, key_side[...]) + dot(weights_b, value_side[...])

    def give(d):
        part = mine.at[d]
        return remote(part, near.at[d], near_sems.at[0, d], near_sems.at[1, d], t, sibling)

    def far(d, side, half):
        start, count = halves[half]
        target = r + 2 - 4 * side
        return remote(
            ready.at[d, pl.ds(start, count)],
            arrive.at[side, d, pl.ds(start, count)],
            far_send.at[d, half],
            far_recv.at[side, d, half],
            t,
            target,
        )

    low_half = (q < (pairs + 1) // 2).astype(jnp.int32)
    right_count = pairs - 1 - q

    def chip_order(i):
        from_right = pairs - 1 - i
        low_order = jnp.where(i < right_count, from_right, i - right_count)
        high_order = jnp.where(i < q, i, pairs - 1 - (i - q))
        order = low_half * low_order + (1 - low_half) * high_order
        return jnp.where(i == pairs - 1, q, order)

    def one_chip(i, carry):
        d = chip_order(i)
        mine[d] = emit(2 * d + other).astype(jnp.bfloat16)
        give(d).start()
        term = emit(2 * d + c)
        give(d).wait_recv()
        term = term + near[d].astype(jnp.float32)

        @pl.when(i == pairs - 1)
        def _():
            own_total[...] = term

        @pl.when(i < pairs - 1)
        def _():
            ready[d] = term.astype(jnp.bfloat16)

        @pl.when(jnp.logical_and(q == 0, d > q))
        def _():
            far(d, 0, 0).start()
            far(d, 0, 1).start()

        @pl.when(jnp.logical_and(q == pairs - 1, d < q))
        def _():
            far(d, 1, 0).start()
            far(d, 1, 1).start()

        return carry

    lax.fori_loop(0, pairs, one_chip, 0)

    weighted_b = weighted_t[...].astype(jnp.bfloat16)
    d_cells_b = d_cells_t[...].astype(jnp.bfloat16)
    attended = contract_first(weighted_b, w_value[...]).astype(jnp.bfloat16)
    d_query = contract_first(d_cells_b, w_key[...]).astype(jnp.bfloat16)
    blocks = [
        contract_first(cells[r], d_query),
        dot(d_cells_b, queries[...]),
        dot(weighted_b, d_attended[...]),
        contract_first(attended, grad_out[...]),
    ]
    for i, block in enumerate(blocks):
        grads[i * channels : (i + 1) * channels, :] = (block * grad_scale).astype(jnp.bfloat16)
    share = 4 * channels // frames
    grad_copies = [
        remote(
            grads.at[pl.ds(pl.multiple_of(frame_at[d] * share, share), share)],
            grads_in.at[d],
            grad_sems.at[0, d],
            grad_sems.at[1, d],
            frame_at[d],
            r,
        )
        for d in range(1, frames)
    ]
    for copy in grad_copies:
        copy.start()
    own_total[...] += contract_last(d_query, w_query[...])

    def relay(phase, carry):
        side = jnp.where(phase == 0, 1 - low_half, low_half)
        has_up = jnp.where(side == 0, q > 0, q < pairs - 1)
        count = jnp.where(side == 0, right_count, q)

        def one(i, carry):
            d = jnp.where(side == 0, pairs - 1 - i, i)

            @pl.when(jnp.logical_and(has_up, i < count))
            def _():
                for half in range(2):
                    start, length = halves[half]
                    part = pl.ds(start, length)
                    far(d, side, half).wait_recv()
                    ready[d, part] = (
                        ready[d, part].astype(jnp.float32)
                        + arrive[side, d, part].astype(jnp.float32)
                    ).astype(jnp.bfloat16)
                    far(d, side, half).start()

            return carry

        return lax.fori_loop(0, pairs - 1, one, carry)

    lax.fori_loop(0, 2, relay, 0)

    for copy in grad_copies:
        copy.wait_recv()
    stack = grads[pl.ds(pl.multiple_of(t * share, share), share), :].astype(jnp.float32)
    for d in range(1, frames):
        stack = stack + grads_in[d].astype(jnp.float32)
    stack_out[...] = stack.astype(stack_out.dtype)

    for side in range(2):

        @pl.when(q > 0 if side == 0 else q < pairs - 1)
        def _():
            for half in range(2):
                start, length = halves[half]
                far(q, side, half).wait_recv()
                part = pl.ds(start, length)
                own_total[part, :] += arrive[side, q, part].astype(jnp.float32)

    mixed_f = mixed[...].astype(jnp.float32)
    second_scale = lax.rsqrt(jnp.mean(mixed_f * mixed_f, axis=1, keepdims=True) + epsilon)
    normed_two = mixed_f * second_scale
    scaled_two = gain[...] * own_total[...]
    d_mixed = grad_out[...].astype(jnp.float32) + second_scale * (
        scaled_two - normed_two * jnp.mean(scaled_two * normed_two, axis=1, keepdims=True)
    )
    d_mixed_out[...] = d_mixed
    d_conv_out[...] = d_mixed.astype(jnp.bfloat16).reshape(rows, cols, channels)

    to_sibling.wait_send()
    for side in range(2):
        for step in range(1, pairs):

            @pl.when(onward(step - 1, side))
            def _():
                for half in range(2):
                    hop(step, side, half).wait_send()

            @pl.when(arrives(step, side))
            def _():
                hand(step, side).wait_send()

    for d in range(pairs):
        give(d).wait_send()

        @pl.when(q != d)
        def _():
            for half in range(2):
                far(d, 0, half).wait_send()

    for copy in grad_copies:
        copy.wait_send()


def attend(mixed, cotangent, flag_tile, gain, w_query, w_key, w_value, w_out, scales, collective_id):
    frames, slabs = lax.axis_size("tm"), lax.axis_size("rows")
    pairs = slabs // 2
    rows, cols, channels = cotangent.shape
    size = rows * cols
    bf16, f32 = jnp.bfloat16, jnp.float32
    share = 4 * channels // frames
    dma = pltpu.SemaphoreType.DMA
    return pl.pallas_call(
        functools.partial(attention_kernel, frames, slabs, *scales),
        out_shape=[
            jax.ShapeDtypeStruct((size, channels), f32),
            jax.ShapeDtypeStruct((rows, cols, channels), bf16),
            jax.ShapeDtypeStruct((share, channels), bf16),
        ],
        in_specs=[IN_VMEM] * 8,
        out_specs=[IN_VMEM] * 3,
        scratch_shapes=[
            pltpu.VMEM((slabs, size, channels), bf16),
            pltpu.VMEM((slabs, channels, size), bf16),
            pltpu.VMEM((slabs, size, size), f32),
            pltpu.VMEM((slabs, size, size), f32),
            pltpu.VMEM((slabs, 1, size), f32),
            pltpu.VMEM((slabs, 1, size), f32),
            pltpu.VMEM((slabs, 1, size), f32),
            pltpu.VMEM((slabs,) + flag_tile.shape, bf16),
            pltpu.VMEM((pairs, size, channels), bf16),
            pltpu.VMEM((pairs, size, channels), bf16),
            pltpu.VMEM((pairs, size, channels), bf16),
            pltpu.VMEM((2, pairs, size, channels), bf16),
            pltpu.VMEM((size, channels), f32),
            pltpu.VMEM((channels, size), f32),
            pltpu.VMEM((channels, size), f32),
            pltpu.VMEM((size, channels), bf16),
            pltpu.VMEM((size, channels), bf16),
            pltpu.VMEM((size, channels), bf16),
            pltpu.VMEM((size, channels), bf16),
            pltpu.VMEM((size, channels), bf16),
            pltpu.VMEM((4 * channels, channels), bf16),
            pltpu.VMEM((frames, share, channels), bf16),
            dma((2, slabs)),
            dma((2,)),
            dma((2, 2, pairs + 1, 2)),
            dma((2, 2, pairs)),
            dma((2, pairs)),
            dma((pairs, 2)),
            dma((2, pairs, 2)),
            dma((2, frames)),
        ],
        compiler_params=params(collective_id, 62),
    )(mixed, cotangent, flag_tile, gain, w_query, w_key, w_value, w_out)


def flipped(index, count, d):
    total, bit = index, 1
    while bit < count:
        if d // bit % 2:
            total = total + bit * (1 - 2 * lax.rem(lax.div(index, bit), 2))
        bit *= 2
    return total


def window_rows(count, step):
    return -(-(count + 16 - math.gcd(step, 16)) // 16) * 16


def conv_back_kernel(frames, slabs, own_rows, grad_scale, *refs):
    (d_conv, history_hbm, weight_hbm, d_mixed, latents, flag_tile, gain, stack) = refs[:8]
    (grad_out, conv_out, attn_out) = refs[8:11]
    (spread, shifted, history, history_t, weight, weight_acc) = refs[11:17]
    (normed, first_scale, slope) = refs[17:20]
    (mine, near, ready, arrive, own_total) = refs[20:25]
    (terms, terms_in, own_term, stack_in) = refs[25:29]
    (load_sems, edge_sems, mid_sems, halo_sems, stack_sems) = refs[29:34]
    (near_sems, far_send, far_recv, term_sems) = refs[34:]
    pairs = slabs // 2
    rows, cols, channels = d_conv.shape
    size = rows * cols
    wide = shifted.shape[3]
    narrow = -(-cols // 16) * 16
    tap_count = weight.shape[0] // channels
    tap_total = own_rows * frames // channels
    block_rows = own_rows // slabs
    span = mine.shape[1]
    halves = halves_of(span)
    t, r = lax.axis_index("tm"), lax.axis_index("rows")
    q, c = lax.div(r, 2), lax.rem(r, 2)
    other = 1 - c
    sibling = 2 * q + other
    frame_at = [flipped(t, frames, d) for d in range(frames)]
    slab_at = [lax.rem(r + d, slabs) for d in range(slabs)]
    has_above, has_below = r > 0, r < slabs - 1
    first_tap = lax.div(t * own_rows, channels)
    weight_from = t * own_rows - first_tap * channels
    own_taps = lax.div(weight_from + own_rows + channels - 1, channels)

    def tap_at(j):
        k = jnp.minimum(first_tap + j, tap_total - 1)
        return lax.div(k, 9), lax.rem(lax.div(k, 3), 3), lax.rem(k, 3)

    loads = [
        pltpu.make_async_copy(history_hbm, history, load_sems.at[0]),
        pltpu.make_async_copy(weight_hbm, weight, load_sems.at[1]),
    ]
    for copy in loads:
        copy.start()
    barrier = pltpu.get_barrier_semaphore()
    for d in range(1, slabs):
        signal(barrier, t, slab_at[d])
    for d in range(1, frames):
        signal(barrier, frame_at[d], r)
    for h in range(rows):
        spread[t, h + 1] = d_conv[h]

    @pl.when(r == 0)
    def _():
        for f in range(frames):
            spread[f, 0] = jnp.zeros((cols, channels), spread.dtype)

    @pl.when(r == slabs - 1)
    def _():
        for f in range(frames):
            spread[f, rows + 1] = jnp.zeros((cols, channels), spread.dtype)

    pl.semaphore_wait(barrier, slabs + frames - 2)

    def edge(d, i):
        part = spread.at[t, 1 if i == 0 else rows]
        return remote(
            part, part, edge_sems.at[0, d, i], edge_sems.at[1, d, i], frame_at[d], r
        )

    def middle(d):
        part = spread.at[t, pl.ds(2, rows - 2)]
        return remote(part, part, mid_sems.at[0, d], mid_sems.at[1, d], frame_at[d], r)

    def halo(d, i):
        return remote(
            spread.at[frame_at[d], 1 if i == 0 else rows],
            spread.at[frame_at[d], rows + 1 if i == 0 else 0],
            halo_sems.at[0, d, i],
            halo_sems.at[1, d, i],
            t,
            r - 1 if i == 0 else r + 1,
        )

    def send_halos(d):
        @pl.when(has_above)
        def _():
            halo(d, 0).start()

        @pl.when(has_below)
        def _():
            halo(d, 1).start()

    def pass_edges(d):
        for i in range(2):
            edge(d, i).wait_recv()
        send_halos(d)

    near_frames = [d for d in range(1, frames) if d & (d - 1) == 0]
    late_frames = [d for d in range(1, frames) if d & (d - 1) != 0]
    for d in near_frames:
        edge(d, 0).start()
        edge(d, 1).start()
    send_halos(0)
    for d in near_frames:
        middle(d).start()
    for d in late_frames:
        edge(d, 0).start()
        edge(d, 1).start()
    for d in late_frames:
        middle(d).start()

    share = stack_in.shape[1]
    stack_step = attn_out.shape[0]

    def stack_low(at):
        return pl.multiple_of(lax.div(at * stack_step, 16) * 16, 16)

    stack_copies = [
        remote(
            stack.at[pl.ds(stack_low(slab_at[d]), share)],
            stack_in.at[d],
            stack_sems.at[0, d],
            stack_sems.at[1, d],
            t,
            slab_at[d],
        )
        for d in range(1, slabs)
    ]
    for copy in stack_copies:
        copy.start()

    weight_acc[...] = jnp.zeros_like(weight_acc)
    history_t[0] = jnp.zeros(history_t.shape[1:], history_t.dtype)
    history_t[1] = jnp.zeros(history_t.shape[1:], history_t.dtype)
    for dw in range(3):
        for f in range(2):
            shifted[dw, frames + f] = jnp.zeros(shifted.shape[2:], shifted.dtype)
    for copy in loads:
        copy.wait()
    spare = jnp.zeros((wide - cols, channels), jnp.float32)

    def turn(f, carry):
        for h in range(rows + 2):
            line = jnp.concatenate([history[f, h].astype(jnp.float32), spare], axis=0)
            history_t[f + 2, :, h * wide : (h + 1) * wide] = line.astype(jnp.bfloat16).T
        return carry

    lax.fori_loop(0, frames, turn, 0)
    inputs = latents[...].astype(jnp.float32)
    scale_one = lax.rsqrt(jnp.mean(inputs * inputs, axis=1, keepdims=True) + epsilon)
    normed_one = inputs * scale_one
    first_scale[...] = scale_one
    normed[...] = normed_one
    factor = gain[...] * silu_slope(normed_one * gain[...])
    for h in range(rows):
        flag = flag_tile[h : h + 1, 0:1].astype(jnp.float32)
        part = factor[h * cols : (h + 1) * cols]
        slope[h * cols : (h + 1) * cols, :] = jnp.where(flag > 0, part, 0.0)

    for d in near_frames:
        pass_edges(d)

    def stage(d):
        f = frame_at[d]
        if d > 0:
            middle(d).wait_recv()

        @pl.when(has_below)
        def _():
            halo(d, 0).wait_recv()

        @pl.when(has_above)
        def _():
            halo(d, 1).wait_recv()

        def widen(h, carry):
            line = jnp.concatenate([spread[f, h].astype(jnp.float32), spare], axis=0)
            shifted[0, f, h] = pltpu.roll(line, wide - 1, 0).astype(jnp.bfloat16)
            shifted[1, f, h] = line.astype(jnp.bfloat16)
            shifted[2, f, h] = pltpu.roll(line, 1, 0).astype(jnp.bfloat16)
            return carry

        lax.fori_loop(0, rows + 2, widen, 0)

        def weigh(j, carry):
            dt, dh, dw = tap_at(j)
            lanes = pl.ds(pl.multiple_of(dh * wide, wide), rows * wide)
            ahead = shifted[dw, f, 1 : rows + 1].reshape(rows * wide, channels)
            at = pl.ds(pl.multiple_of(j * channels, channels), channels)
            weight_acc[at, :] += dot(history_t[f + dt, :, lanes], ahead)
            return carry

        lax.fori_loop(0, own_taps, weigh, 0)

    stage(0)
    for i, d in enumerate(near_frames):
        if i == len(near_frames) - 1:
            for e in late_frames:
                pass_edges(e)
        stage(d)
    for d in late_frames:
        stage(d)

    def low_row(block):
        return pl.multiple_of(lax.div(weight_from + block * block_rows, 16) * 16, 16)

    def weight_block(block):
        return weight_acc[pl.ds(low_row(block), span), :] * grad_scale

    def give(d):
        part = mine.at[d]
        return remote(part, near.at[d], near_sems.at[0, d], near_sems.at[1, d], t, sibling)

    def far(d, side, half):
        start, count = halves[half]
        return remote(
            ready.at[d, pl.ds(start, count)],
            arrive.at[side, d, pl.ds(start, count)],
            far_send.at[d, half],
            far_recv.at[side, d, half],
            t,
            r + 2 - 4 * side,
        )

    low_half = (q < (pairs + 1) // 2).astype(jnp.int32)
    right_count = pairs - 1 - q

    def chip_order(i):
        low_order = jnp.where(i < right_count, pairs - 1 - i, i - right_count)
        high_order = jnp.where(i < q, i, pairs - 1 - (i - q))
        order = low_half * low_order + (1 - low_half) * high_order
        return jnp.where(i == pairs - 1, q, order)

    def one_gift(i, carry):
        d = chip_order(i)
        mine[d] = weight_block(2 * d + other).astype(jnp.bfloat16)
        give(d).start()
        return carry

    def one_chip(i, carry):
        d = chip_order(i)
        term = weight_block(2 * d + c)
        give(d).wait_recv()
        term = term + near[d].astype(jnp.float32)

        @pl.when(i == pairs - 1)
        def _():
            own_total[...] = term

        @pl.when(i < pairs - 1)
        def _():
            ready[d] = term.astype(jnp.bfloat16)

        @pl.when(jnp.logical_and(q == 0, d > q))
        def _():
            far(d, 0, 0).start()
            far(d, 0, 1).start()

        @pl.when(jnp.logical_and(q == pairs - 1, d < q))
        def _():
            far(d, 1, 0).start()
            far(d, 1, 1).start()

        return carry

    lax.fori_loop(0, pairs, one_gift, 0)
    lax.fori_loop(0, pairs, one_chip, 0)

    def back(f):
        def one(j, total):
            dt, dh, dw = tap_at(j)
            ahead = shifted[dw, f + 2 - dt, pl.ds(2 - dh, rows), :narrow]
            at = pl.ds(pl.multiple_of(j * channels, channels), channels)
            return total + contract_last(ahead.reshape(rows * narrow, channels), weight[at, :])

        total = lax.fori_loop(
            0, own_taps, one, jnp.zeros((rows * narrow, channels), jnp.float32)
        )
        return total.reshape(rows, narrow, channels)[:, :cols]

    def term_copy(d):
        return remote(
            terms.at[d], terms_in.at[d], term_sems.at[0, d], term_sems.at[1, d], frame_at[d], r
        )

    for d in late_frames + near_frames:
        terms[d] = back(frame_at[d]).astype(jnp.bfloat16)
        term_copy(d).start()

    def relay(phase, carry):
        side = jnp.where(phase == 0, 1 - low_half, low_half)
        has_up = jnp.where(side == 0, q > 0, q < pairs - 1)
        count = jnp.where(side == 0, right_count, q)

        def one(i, carry):
            d = jnp.where(side == 0, pairs - 1 - i, i)

            @pl.when(jnp.logical_and(has_up, i < count))
            def _():
                for half in range(2):
                    start, length = halves[half]
                    part = pl.ds(start, length)
                    far(d, side, half).wait_recv()
                    ready[d, part] = (
                        ready[d, part].astype(jnp.float32)
                        + arrive[side, d, part].astype(jnp.float32)
                    ).astype(jnp.bfloat16)
                    far(d, side, half).start()

            return carry

        return lax.fori_loop(0, pairs - 1, one, carry)

    lax.fori_loop(0, 2, relay, 0)
    own_term[...] = back(t).reshape(size, channels)

    stack_sum = stack[pl.ds(stack_low(r), share), :].astype(jnp.float32)
    for d in range(1, slabs):
        stack_copies[d - 1].wait_recv()
        stack_sum = stack_sum + stack_in[d].astype(jnp.float32)
    if share > stack_step:
        stack_sum = pltpu.roll(stack_sum, share - (r * stack_step - stack_low(r)), 0)
    attn_out[...] = stack_sum[:stack_step]

    for d in near_frames + late_frames:
        term_copy(d).wait_recv()
        own_term[...] += terms_in[d].astype(jnp.float32).reshape(size, channels)
    scaled_one = own_term[...] * slope[...]
    normed_one = normed[...]
    input_grad = d_mixed[...] + first_scale[...] * (
        scaled_one - normed_one * jnp.mean(scaled_one * normed_one, axis=1, keepdims=True)
    )
    grad_out[...] = input_grad.reshape(rows, cols, channels).astype(grad_out.dtype)

    for side in range(2):

        @pl.when(q > 0 if side == 0 else q < pairs - 1)
        def _():
            for half in range(2):
                start, length = halves[half]
                far(q, side, half).wait_recv()
                part = pl.ds(start, length)
                own_total[part, :] += arrive[side, q, part].astype(jnp.float32)

    result = own_total[...]
    if span > block_rows:
        offset = weight_from + r * block_rows - low_row(r)
        result = pltpu.roll(result, span - offset, 0)
    conv_out[...] = result[:block_rows]

    for d in range(frames):
        if d > 0:
            edge(d, 0).wait_send()
            edge(d, 1).wait_send()
            middle(d).wait_send()
            term_copy(d).wait_send()

        @pl.when(has_above)
        def _():
            halo(d, 0).wait_send()

        @pl.when(has_below)
        def _():
            halo(d, 1).wait_send()

    for copy in stack_copies:
        copy.wait_send()
    for d in range(pairs):
        give(d).wait_send()

        @pl.when(q != d)
        def _():
            for half in range(2):
                far(d, 0, half).wait_send()


def conv_back(d_conv, history, weight, own_rows, d_mixed, latents, flag_tile, gain, stack, grad_scale, collective_id):
    frames, slabs = lax.axis_size("tm"), lax.axis_size("rows")
    pairs = slabs // 2
    rows, cols, channels = d_conv.shape
    size = rows * cols
    bf16, f32 = jnp.bfloat16, jnp.float32
    wide = -(-cols // 128) * 128
    block_rows = own_rows // slabs
    span = window_rows(block_rows, math.gcd(own_rows, block_rows))
    stack_rows = stack.shape[0] // slabs
    share = window_rows(stack_rows, stack_rows)
    if share > stack_rows:
        stack = jnp.pad(stack, ((0, 16), (0, 0)))
    dma = pltpu.SemaphoreType.DMA
    return pl.pallas_call(
        functools.partial(conv_back_kernel, frames, slabs, own_rows, grad_scale),
        out_shape=[
            jax.ShapeDtypeStruct((rows, cols, channels), bf16),
            jax.ShapeDtypeStruct((block_rows, channels), f32),
            jax.ShapeDtypeStruct((stack_rows, channels), f32),
        ],
        in_specs=[IN_VMEM, ANY, ANY] + [IN_VMEM] * 5,
        out_specs=[IN_VMEM] * 3,
        scratch_shapes=[
            pltpu.VMEM((frames, rows + 2, cols, channels), bf16),
            pltpu.VMEM((3, frames + 2, rows + 2, wide, channels), bf16),
            pltpu.VMEM((frames, rows + 2, cols, channels), bf16),
            pltpu.VMEM((frames + 2, channels, (rows + 2) * wide), bf16),
            pltpu.VMEM(weight.shape, bf16),
            pltpu.VMEM((weight.shape[0] + 32, channels), f32),
            pltpu.VMEM((size, channels), f32),
            pltpu.VMEM((size, 1), f32),
            pltpu.VMEM((size, channels), f32),
            pltpu.VMEM((pairs, span, channels), bf16),
            pltpu.VMEM((pairs, span, channels), bf16),
            pltpu.VMEM((pairs, span, channels), bf16),
            pltpu.VMEM((2, pairs, span, channels), bf16),
            pltpu.VMEM((span, channels), f32),
            pltpu.VMEM((frames, rows, cols, channels), bf16),
            pltpu.VMEM((frames, rows, cols, channels), bf16),
            pltpu.VMEM((size, channels), f32),
            pltpu.VMEM((slabs, share, channels), bf16),
            dma((2,)),
            dma((2, frames, 2)),
            dma((2, frames)),
            dma((2, frames, 2)),
            dma((2, slabs)),
            dma((2, pairs)),
            dma((pairs, 2)),
            dma((2, pairs, 2)),
            dma((2, frames)),
        ],
        compiler_params=params(collective_id, 62),
    )(d_conv, history, weight, d_mixed, latents, flag_tile, gain, stack)


def finish_kernel(count, *refs):
    sems = refs[2 * count]
    copies = [
        pltpu.make_async_copy(refs[i], refs[count + i], sems.at[i]) for i in range(count)
    ]
    for copy in copies:
        copy.start()
    for copy in copies:
        copy.wait()


def finish(arrays):
    count = len(arrays)
    return pl.pallas_call(
        functools.partial(finish_kernel, count),
        out_shape=[jax.ShapeDtypeStruct(a.shape, a.dtype) for a in arrays],
        in_specs=[ANY] * count,
        out_specs=[ANY] * count,
        scratch_shapes=[pltpu.SemaphoreType.DMA((count,))],
    )(*arrays)


def column_shifts(slabs, before, after):
    cols = slabs.shape[2]
    width = -(-cols // 16) * 16
    spare = width - cols
    edges = ((before, after), (0, 0))
    return jnp.stack(
        [jnp.pad(slabs, edges + ((1, spare - 1), (0, 0)))]
        + [jnp.pad(slabs, edges + ((0, spare), (0, 0)))]
        + [jnp.pad(slabs[:, :, 1:], edges + ((0, spare + 1), (0, 0)))]
    )


def taps_kernel(rows, cols, taps, shifted, weight, out, columns):
    f = pl.program_id(0)
    width, channels = shifted.shape[3:]
    for j in range(taps.shape[0]):
        window = shifted[taps[j, 2], taps[j, 0] + f, pl.ds(taps[j, 1], rows)]
        columns[:, j * channels : (j + 1) * channels] = window.reshape(rows * width, channels)
    total = dot(columns[...], weight[...])
    out[0] = total.astype(out.dtype).reshape(rows, width, channels)[:, :cols]


def sum_taps(shifted, taps, weight, rows, cols):
    frames = shifted.shape[1] - 2
    width, channels = shifted.shape[3:]
    return pl.pallas_call(
        functools.partial(taps_kernel, rows, cols),
        grid=(frames,),
        out_shape=jax.ShapeDtypeStruct((frames, rows, cols, channels), jnp.bfloat16),
        in_specs=[pl.BlockSpec(memory_space=pltpu.SMEM), IN_VMEM, IN_VMEM],
        out_specs=pl.BlockSpec((1, rows, cols, channels), lambda f: (f, 0, 0, 0)),
        scratch_shapes=[pltpu.VMEM((rows * width, weight.shape[0]), jnp.bfloat16)],
        compiler_params=pltpu.CompilerParams(vmem_limit_bytes=48 * 1024 * 1024),
    )(taps, shifted, weight)


def per_device(
    latents, row_valid, norm_gain, conv_weight, attn_gain, w_query, w_key, w_value, w_out, cotangent
):
    bf16 = jnp.bfloat16
    shape_all = latents.shape
    rows_dev, col_count, channels = shape_all[1:]
    slab_size = rows_dev * col_count
    frames, slabs = lax.axis_size("tm"), lax.axis_size("rows")
    t = lax.axis_index("tm")
    grad_scale = 1.0 / math.sqrt(frames * slabs * slab_size)
    inv_root = 1.0 / math.sqrt(channels)

    own_rows = conv_weight.shape[0]
    tap_total = own_rows * frames // channels
    tap_count = max(
        -(-((i * own_rows) % channels + own_rows) // channels) for i in range(frames)
    )
    first_tap = lax.div(t * own_rows, channels)
    weight_from = t * own_rows - first_tap * channels
    own_weight = lax.dynamic_update_slice(
        jnp.zeros((tap_count * channels, channels), bf16), conv_weight, (weight_from, 0)
    )
    k = jnp.minimum(first_tap + jnp.arange(tap_count, dtype=jnp.int32), tap_total - 1)
    taps = jnp.stack([k // 9, k % 9 // 3, k % 3], axis=1)

    cell_factor = jnp.repeat(row_valid.astype(jnp.float32), col_count)[:, None]
    inputs = latents.reshape(slab_size, channels).astype(jnp.float32)
    first_scale = lax.rsqrt(jnp.mean(inputs * inputs, axis=1, keepdims=True) + epsilon)
    normed_one = inputs * first_scale
    gated_in = normed_one * norm_gain
    conv_in = (jax.nn.silu(gated_in) * cell_factor).astype(bf16)

    history = gather_slabs(conv_in.reshape(rows_dev, col_count, channels), 0)
    conv_terms = sum_taps(column_shifts(history, 2, 0), taps, own_weight, rows_dev, col_count)
    conv_terms = conv_terms.reshape(frames, slab_size, channels)
    (conv_terms,) = swap_over_tm([conv_terms], 1)
    conv_out = jnp.sum(conv_terms.astype(jnp.float32), axis=0)

    mixed = (inputs + conv_out).astype(bf16)
    flag_tile = jnp.pad(row_valid.astype(bf16), (0, FLAG_ROWS - rows_dev))
    flag_tile = jnp.broadcast_to(flag_tile[:, None], (FLAG_ROWS, 128))
    d_mixed, d_conv, stack = attend(
        mixed,
        cotangent.reshape(shape_all[1:]),
        flag_tile,
        attn_gain[None],
        w_query,
        w_key,
        w_value,
        w_out,
        (grad_scale, inv_root),
        2,
    )
    results = conv_back(
        d_conv,
        history,
        own_weight,
        own_rows,
        d_mixed,
        latents.reshape(slab_size, channels),
        flag_tile,
        norm_gain[None],
        stack,
        grad_scale,
        3,
    )
    input_grad, conv_weight_grad, attn_weight_grad = finish(results)
    return input_grad.reshape(shape_all), conv_weight_grad, attn_weight_grad


def solution(mesh):
    return jax.shard_map(
        per_device,
        mesh=mesh,
        in_specs=(
            P("tm", "rows", None, None),
            P("rows"),
            P(),
            P("tm", None),
            P(),
            P(),
            P(),
            P(),
            P(),
            P("tm", "rows", None, None),
        ),
        out_specs=(P("tm", "rows", None, None), P(("tm", "rows"), None), P(("tm", "rows"), None)),
        check_vma=False,
    )
```

```python
import functools
import math

import jax
import jax.numpy as jnp
from jax import lax
from jax.experimental import pallas as pl
from jax.experimental.pallas import tpu as pltpu
from jax.sharding import PartitionSpec as P

epsilon = 1e-06
MESH = pl.DeviceIdType.MESH
ANY = pl.BlockSpec(memory_space=pl.ANY)
IN_VMEM = pl.BlockSpec(memory_space=pltpu.VMEM)
FLAG_ROWS = 16


def contract_last(first_op, second_op):
    return lax.dot_general(
        first_op, second_op, (((1,), (1,)), ((), ())), preferred_element_type=jnp.float32
    )


def contract_first(first_op, second_op):
    return lax.dot_general(
        first_op, second_op, (((0,), (0,)), ((), ())), preferred_element_type=jnp.float32
    )


def dot(first_op, second_op):
    return jnp.dot(first_op, second_op, preferred_element_type=jnp.float32)


def silu_slope(inputs):
    logistic = jax.nn.sigmoid(inputs)
    return logistic * (1.0 + inputs * (1.0 - logistic))


def params(collective_id, mebibytes=40):
    return pltpu.CompilerParams(
        collective_id=collective_id,
        has_side_effects=True,
        vmem_limit_bytes=mebibytes * 1024 * 1024,
    )


def signal(barrier, tm_at, row_at):
    pl.semaphore_signal(barrier, inc=1, device_id=(tm_at, row_at), device_id_type=MESH)


def remote(src, dst, send_sem, recv_sem, tm_at, row_at):
    return pltpu.make_async_remote_copy(
        src_ref=src,
        dst_ref=dst,
        send_sem=send_sem,
        recv_sem=recv_sem,
        device_id=(tm_at, row_at),
        device_id_type=MESH,
    )


def flipped(index, count, d):
    total, bit = index, 1
    while bit < count:
        if d // bit % 2:
            total = total + bit * (1 - 2 * lax.rem(lax.div(index, bit), 2))
        bit *= 2
    return total


def padded_taps(own_rows, frames, channels):
    return max(-(-((i * own_rows) % channels + own_rows) // channels) for i in range(frames))


def conv_kernel(frames, slabs, *refs):
    (latents, row_valid, gain, weight_hbm) = refs[:4]
    (history, mixed, flag_tile) = refs[4:7]
    (shifted, weight, terms, terms_in, total) = refs[7:12]
    (load_sem, edge_sems, mid_sems, halo_sems, term_sems) = refs[12:]
    rows, cols, channels = latents.shape
    size = rows * cols
    narrow = shifted.shape[3]
    own_rows = weight_hbm.shape[0]
    tap_total = own_rows * frames // channels
    t, r = lax.axis_index("tm"), lax.axis_index("rows")
    frame_at = [flipped(t, frames, d) for d in range(frames)]
    has_above, has_below = r > 0, r < slabs - 1
    first_tap = lax.div(t * own_rows, channels)
    weight_from = pl.multiple_of(t * own_rows - first_tap * channels, 16)
    own_taps = lax.div(weight_from + own_rows + channels - 1, channels)

    barrier = pltpu.get_barrier_semaphore()
    for d in range(1, frames):
        signal(barrier, frame_at[d], r)

    @pl.when(has_above)
    def _():
        signal(barrier, t, r - 1)

    @pl.when(has_below)
    def _():
        signal(barrier, t, r + 1)

    flag_tile[...] = jnp.zeros_like(flag_tile)
    for h in range(rows):
        flag = row_valid[h].astype(jnp.float32)
        part = latents[h].astype(jnp.float32)
        scale = lax.rsqrt(jnp.mean(part * part, axis=1, keepdims=True) + epsilon)
        part = jax.nn.silu(part * scale * gain[...]) * flag
        history[t, h + 1] = part.astype(jnp.bfloat16)

    @pl.when(r == 0)
    def _():
        for f in range(frames):
            history[f, 0] = jnp.zeros((cols, channels), history.dtype)

    @pl.when(r == slabs - 1)
    def _():
        for f in range(frames):
            history[f, rows + 1] = jnp.zeros((cols, channels), history.dtype)

    sides = has_above.astype(jnp.int32) + has_below.astype(jnp.int32)
    pl.semaphore_wait(barrier, frames - 1 + sides)

    def edge(d, i):
        part = history.at[t, 1 if i == 0 else rows]
        return remote(part, part, edge_sems.at[0, d, i], edge_sems.at[1, d, i], frame_at[d], r)

    def middle(d):
        part = history.at[t, pl.ds(2, rows - 2)]
        return remote(part, part, mid_sems.at[0, d], mid_sems.at[1, d], frame_at[d], r)

    def halo(d, i):
        return remote(
            history.at[frame_at[d], 1 if i == 0 else rows],
            history.at[frame_at[d], rows + 1 if i == 0 else 0],
            halo_sems.at[0, d, i],
            halo_sems.at[1, d, i],
            t,
            r - 1 if i == 0 else r + 1,
        )

    def send_halos(d):
        @pl.when(has_above)
        def _():
            halo(d, 0).start()

        @pl.when(has_below)
        def _():
            halo(d, 1).start()

    def pass_edges(d):
        for i in range(2):
            edge(d, i).wait_recv()
        send_halos(d)

    near_frames = [d for d in range(1, frames) if d & (d - 1) == 0]
    late_frames = [d for d in range(1, frames) if d & (d - 1) != 0]
    for d in near_frames:
        edge(d, 0).start()
        edge(d, 1).start()
    send_halos(0)
    for d in near_frames:
        middle(d).start()
    for d in late_frames:
        edge(d, 0).start()
        edge(d, 1).start()
    for d in late_frames:
        middle(d).start()

    for h in range(rows):
        flag = row_valid[h].astype(jnp.float32)
        flag_tile[h : h + 1, :] = jnp.full((1, flag_tile.shape[1]), flag, flag_tile.dtype)
    weight[...] = jnp.zeros_like(weight)
    load = pltpu.make_async_copy(weight_hbm, weight.at[pl.ds(weight_from, own_rows)], load_sem)
    load.start()
    for dw in range(3):
        for f in range(2):
            shifted[dw, f] = jnp.zeros(shifted.shape[2:], shifted.dtype)
    spare = jnp.zeros((narrow - cols, channels), jnp.float32)

    def stage(d):
        f = frame_at[d]
        if d > 0:
            middle(d).wait_recv()

        @pl.when(has_below)
        def _():
            halo(d, 0).wait_recv()

        @pl.when(has_above)
        def _():
            halo(d, 1).wait_recv()

        def widen(h, carry):
            line = jnp.concatenate([history[f, h].astype(jnp.float32), spare], axis=0)
            shifted[0, f + 2, h] = pltpu.roll(line, 1, 0).astype(jnp.bfloat16)
            shifted[1, f + 2, h] = line.astype(jnp.bfloat16)
            shifted[2, f + 2, h] = pltpu.roll(line, narrow - 1, 0).astype(jnp.bfloat16)
            return carry

        lax.fori_loop(0, rows + 2, widen, 0)

    for d in near_frames:
        pass_edges(d)
    stage(0)
    for i, d in enumerate(near_frames):
        if i == len(near_frames) - 1:
            for e in late_frames:
                pass_edges(e)
        stage(d)
    for d in late_frames:
        stage(d)
    load.wait()

    def convolve(f):
        def one(j, total):
            k = jnp.minimum(first_tap + j, tap_total - 1)
            dt, dh, dw = lax.div(k, 9), lax.rem(lax.div(k, 3), 3), lax.rem(k, 3)
            window = shifted[dw, f + dt, pl.ds(dh, rows)].reshape(rows * narrow, channels)
            at = pl.ds(pl.multiple_of(j * channels, channels), channels)
            return total + dot(window, weight[at, :])

        total = lax.fori_loop(
            0, own_taps, one, jnp.zeros((rows * narrow, channels), jnp.float32)
        )
        return total.reshape(rows, narrow, channels)[:, :cols]

    def term_copy(d):
        return remote(
            terms.at[d], terms_in.at[d], term_sems.at[0, d], term_sems.at[1, d], frame_at[d], r
        )

    for d in late_frames + near_frames:
        terms[d] = convolve(frame_at[d]).astype(jnp.bfloat16)
        term_copy(d).start()
    total[...] = convolve(t) + latents[...].astype(jnp.float32)
    for d in near_frames + late_frames:
        term_copy(d).wait_recv()
        total[...] += terms_in[d].astype(jnp.float32)
    mixed[...] = total[...].reshape(size, channels).astype(mixed.dtype)

    for d in range(frames):
        if d > 0:
            edge(d, 0).wait_send()
            edge(d, 1).wait_send()
            middle(d).wait_send()
            term_copy(d).wait_send()

        @pl.when(has_above)
        def _():
            halo(d, 0).wait_send()

        @pl.when(has_below)
        def _():
            halo(d, 1).wait_send()


def convolve_frames(latents, row_valid, gain, conv_weight, collective_id):
    frames, slabs = lax.axis_size("tm"), lax.axis_size("rows")
    rows, cols, channels = latents.shape
    bf16, f32 = jnp.bfloat16, jnp.float32
    narrow = -(-cols // 16) * 16
    padded = padded_taps(conv_weight.shape[0], frames, channels) * channels
    dma = pltpu.SemaphoreType.DMA
    return pl.pallas_call(
        functools.partial(conv_kernel, frames, slabs),
        out_shape=[
            jax.ShapeDtypeStruct((frames, rows + 2, cols, channels), bf16),
            jax.ShapeDtypeStruct((rows * cols, channels), bf16),
            jax.ShapeDtypeStruct((FLAG_ROWS, 128), bf16),
        ],
        in_specs=[IN_VMEM, pl.BlockSpec(memory_space=pltpu.SMEM), IN_VMEM, ANY],
        out_specs=[IN_VMEM] * 3,
        scratch_shapes=[
            pltpu.VMEM((3, frames + 2, rows + 2, narrow, channels), bf16),
            pltpu.VMEM((padded, channels), bf16),
            pltpu.VMEM((frames, rows, cols, channels), bf16),
            pltpu.VMEM((frames, rows, cols, channels), bf16),
            pltpu.VMEM((rows, cols, channels), f32),
            dma,
            dma((2, frames, 2)),
            dma((2, frames)),
            dma((2, frames, 2)),
            dma((2, frames)),
        ],
        compiler_params=params(collective_id, 62),
    )(latents, row_valid, gain, conv_weight)


def halves_of(size):
    near = size // 2 // 16 * 16
    return ((0, near), (near, size - near))


def attention_kernel(frames, slabs, grad_scale, inv_root, *refs):
    (mixed, cotangent, flag_tile, gain, w_query, w_key, w_value, w_out) = refs[:8]
    (d_mixed_out, d_conv_out, stack_out) = refs[8:11]
    (cells, cells_t, prob, d_weights, tops, sums, dots, flags) = refs[11:19]
    (mine, near, ready, arrive, own_total, weighted_t, d_cells_t) = refs[19:26]
    (queries, key_side, value_side, d_attended, grad_out) = refs[26:31]
    (grads, grads_in) = refs[31:33]
    (flag_sems, sib_sems, hop_sems, hand_sems, near_sems, far_send, far_recv, grad_sems) = refs[33:]
    pairs = slabs // 2
    rows, cols, channels = cotangent.shape
    size = rows * cols
    halves = halves_of(size)
    t, r = lax.axis_index("tm"), lax.axis_index("rows")
    q, c = lax.div(r, 2), lax.rem(r, 2)
    other = 1 - c
    sibling = 2 * q + other
    frame_at = [lax.rem(t + d, frames) for d in range(frames)]
    slab_at = [lax.rem(r + d, slabs) for d in range(slabs)]
    barrier = pltpu.get_barrier_semaphore()
    for d in range(1, slabs):
        signal(barrier, t, slab_at[d])
    for d in range(1, frames):
        signal(barrier, frame_at[d], r)

    mixed_f = mixed[...].astype(jnp.float32)
    second_scale = lax.rsqrt(jnp.mean(mixed_f * mixed_f, axis=1, keepdims=True) + epsilon)
    attn_in = (mixed_f * second_scale * gain[...]).astype(jnp.bfloat16)
    cells[r] = attn_in
    flags[r] = flag_tile[...]
    pl.semaphore_wait(barrier, slabs + frames - 2)

    flag_copies = [
        remote(
            flag_tile, flags.at[r], flag_sems.at[0, d], flag_sems.at[1, d], t, slab_at[d]
        )
        for d in range(1, slabs)
    ]

    def sources(step, side):
        return q - step if side == 0 else q + step

    def arrives(step, side):
        at = sources(step, side)
        return jnp.logical_and(at >= 0, at < pairs)

    def onward(step, side):
        ahead = q < pairs - 1 if side == 0 else q > 0
        return jnp.logical_and(ahead, arrives(step, side))

    def hop(step, side, half):
        start, count = halves[half]
        part = cells.at[2 * sources(step - 1, side) + c, pl.ds(start, count)]
        target = r + 2 if side == 0 else r - 2
        return remote(
            part, part, hop_sems.at[0, side, step, half], hop_sems.at[1, side, step, half], t, target
        )

    def hand(step, side):
        part = cells.at[2 * sources(step, side) + c]
        return remote(
            part, part, hand_sems.at[0, side, step], hand_sems.at[1, side, step], t, sibling
        )

    to_sibling = remote(cells.at[r], cells.at[r], sib_sems.at[0], sib_sems.at[1], t, sibling)
    for half in range(2):
        for side in range(2):

            @pl.when(onward(0, side))
            def _():
                hop(1, side, half).start()

    to_sibling.start()
    for copy in flag_copies:
        copy.start()

    for h in range(rows):
        flag = flag_tile[h : h + 1, 0:1].astype(jnp.float32)
        part = cotangent[h].astype(jnp.float32)
        grad_out[h * cols : (h + 1) * cols, :] = jnp.where(flag > 0, part, 0.0).astype(jnp.bfloat16)
    queries[...] = dot(attn_in, w_query[...]).astype(jnp.bfloat16)
    key_side[...] = contract_last(queries[...], w_key[...]).astype(jnp.bfloat16)
    d_attended[...] = contract_last(grad_out[...], w_out[...]).astype(jnp.bfloat16)
    value_side[...] = contract_last(d_attended[...], w_value[...]).astype(jnp.bfloat16)
    for copy in flag_copies:
        copy.wait()

    lowest = float(jnp.finfo(jnp.float32).min)

    def absorb(j):
        block = cells[j]
        scores = contract_last(block, key_side[...]) * inv_root
        kept = []
        for h in range(rows):
            flag = flags[j, h : h + 1, 0:1].astype(jnp.float32)
            kept.append(jnp.where(flag > 0, scores[h * cols : (h + 1) * cols], lowest))
        scores = jnp.concatenate(kept, axis=0)
        top = jnp.max(scores, axis=0, keepdims=True)
        exponent = jnp.exp(scores - top)
        prob[j] = exponent
        d_weight = contract_last(block, value_side[...])
        d_weights[j] = d_weight
        tops[j] = top
        sums[j] = jnp.sum(exponent, axis=0, keepdims=True)
        dots[j] = jnp.sum(exponent * d_weight, axis=0, keepdims=True)
        cells_t[j] = block.T

    def absorb_pair(step, side):
        @pl.when(arrives(step, side))
        def _():
            base = 2 * sources(step, side)
            absorb(base + c)
            hand(step, side).wait_recv()
            absorb(base + other)

    def pass_on(step, half):
        for side in range(2):

            @pl.when(arrives(step, side))
            def _():
                hop(step, side, half).wait_recv()

            @pl.when(onward(step, side))
            def _():
                hop(step + 1, side, half).start()

            if half == 1:

                @pl.when(arrives(step, side))
                def _():
                    hand(step, side).start()

    def own_pair(i, carry):
        @pl.when(i == 1)
        def _():
            to_sibling.wait_recv()

        absorb(2 * q + c + i * (other - c))
        return carry

    lax.fori_loop(0, 2, own_pair, 0)
    pass_on(1, 0)
    pass_on(1, 1)
    for step in range(1, pairs):
        absorb_pair(step, 0)
        if step < pairs - 1:
            pass_on(step + 1, 0)
        absorb_pair(step, 1)
        if step < pairs - 1:
            pass_on(step + 1, 1)

    top_all = tops[0]
    for j in range(1, slabs):
        top_all = jnp.maximum(top_all, tops[j])
    total_sum = jnp.zeros_like(top_all)
    total_dot = jnp.zeros_like(top_all)
    for j in range(slabs):
        rescale = jnp.exp(tops[j] - top_all)
        total_sum = total_sum + rescale * sums[j]
        total_dot = total_dot + rescale * dots[j]
        tops[j] = rescale
    inverse = 1.0 / total_sum
    row_delta = total_dot * inverse
    weighted_t[...] = jnp.zeros_like(weighted_t)
    d_cells_t[...] = jnp.zeros_like(d_cells_t)

    def emit(j):
        weights = prob[j] * (tops[j] * inverse)
        weights_b = weights.astype(jnp.bfloat16)
        d_scores = (weights * (d_weights[j] - row_delta) * inv_root).astype(jnp.bfloat16)
        block_t = cells_t[j]
        weighted_t[...] += dot(block_t, weights_b)
        d_cells_t[...] += dot(block_t, d_scores)
        return dot(d_scores, key_side[...]) + dot(weights_b, value_side[...])

    def give(d):
        part = mine.at[d]
        return remote(part, near.at[d], near_sems.at[0, d], near_sems.at[1, d], t, sibling)

    def far(d, side, half):
        start, count = halves[half]
        target = r + 2 - 4 * side
        return remote(
            ready.at[d, pl.ds(start, count)],
            arrive.at[side, d, pl.ds(start, count)],
            far_send.at[d, half],
            far_recv.at[side, d, half],
            t,
            target,
        )

    low_half = (q < (pairs + 1) // 2).astype(jnp.int32)
    right_count = pairs - 1 - q

    def chip_order(i):
        from_right = pairs - 1 - i
        low_order = jnp.where(i < right_count, from_right, i - right_count)
        high_order = jnp.where(i < q, i, pairs - 1 - (i - q))
        order = low_half * low_order + (1 - low_half) * high_order
        return jnp.where(i == pairs - 1, q, order)

    def one_chip(i, carry):
        d = chip_order(i)
        mine[d] = emit(2 * d + other).astype(jnp.bfloat16)
        give(d).start()
        term = emit(2 * d + c)
        give(d).wait_recv()
        term = term + near[d].astype(jnp.float32)

        @pl.when(i == pairs - 1)
        def _():
            own_total[...] = term

        @pl.when(i < pairs - 1)
        def _():
            ready[d] = term.astype(jnp.bfloat16)

        @pl.when(jnp.logical_and(q == 0, d > q))
        def _():
            far(d, 0, 0).start()
            far(d, 0, 1).start()

        @pl.when(jnp.logical_and(q == pairs - 1, d < q))
        def _():
            far(d, 1, 0).start()
            far(d, 1, 1).start()

        return carry

    lax.fori_loop(0, pairs, one_chip, 0)

    weighted_b = weighted_t[...].astype(jnp.bfloat16)
    d_cells_b = d_cells_t[...].astype(jnp.bfloat16)
    attended = contract_first(weighted_b, w_value[...]).astype(jnp.bfloat16)
    d_query = contract_first(d_cells_b, w_key[...]).astype(jnp.bfloat16)
    blocks = [
        contract_first(cells[r], d_query),
        dot(d_cells_b, queries[...]),
        dot(weighted_b, d_attended[...]),
        contract_first(attended, grad_out[...]),
    ]
    for i, block in enumerate(blocks):
        grads[i * channels : (i + 1) * channels, :] = (block * grad_scale).astype(jnp.bfloat16)
    share = 4 * channels // frames
    grad_copies = [
        remote(
            grads.at[pl.ds(pl.multiple_of(frame_at[d] * share, share), share)],
            grads_in.at[d],
            grad_sems.at[0, d],
            grad_sems.at[1, d],
            frame_at[d],
            r,
        )
        for d in range(1, frames)
    ]
    for copy in grad_copies:
        copy.start()
    own_total[...] += contract_last(d_query, w_query[...])

    def relay(phase, carry):
        side = jnp.where(phase == 0, 1 - low_half, low_half)
        has_up = jnp.where(side == 0, q > 0, q < pairs - 1)
        count = jnp.where(side == 0, right_count, q)

        def one(i, carry):
            d = jnp.where(side == 0, pairs - 1 - i, i)

            @pl.when(jnp.logical_and(has_up, i < count))
            def _():
                for half in range(2):
                    start, length = halves[half]
                    part = pl.ds(start, length)
                    far(d, side, half).wait_recv()
                    ready[d, part] = (
                        ready[d, part].astype(jnp.float32)
                        + arrive[side, d, part].astype(jnp.float32)
                    ).astype(jnp.bfloat16)
                    far(d, side, half).start()

            return carry

        return lax.fori_loop(0, pairs - 1, one, carry)

    lax.fori_loop(0, 2, relay, 0)

    for copy in grad_copies:
        copy.wait_recv()
    stack = grads[pl.ds(pl.multiple_of(t * share, share), share), :].astype(jnp.float32)
    for d in range(1, frames):
        stack = stack + grads_in[d].astype(jnp.float32)
    stack_out[...] = stack.astype(stack_out.dtype)

    for side in range(2):

        @pl.when(q > 0 if side == 0 else q < pairs - 1)
        def _():
            for half in range(2):
                start, length = halves[half]
                far(q, side, half).wait_recv()
                part = pl.ds(start, length)
                own_total[part, :] += arrive[side, q, part].astype(jnp.float32)

    mixed_f = mixed[...].astype(jnp.float32)
    second_scale = lax.rsqrt(jnp.mean(mixed_f * mixed_f, axis=1, keepdims=True) + epsilon)
    normed_two = mixed_f * second_scale
    scaled_two = gain[...] * own_total[...]
    d_mixed = grad_out[...].astype(jnp.float32) + second_scale * (
        scaled_two - normed_two * jnp.mean(scaled_two * normed_two, axis=1, keepdims=True)
    )
    d_mixed_out[...] = d_mixed
    d_conv_out[...] = d_mixed.astype(jnp.bfloat16).reshape(rows, cols, channels)

    to_sibling.wait_send()
    for side in range(2):
        for step in range(1, pairs):

            @pl.when(onward(step - 1, side))
            def _():
                for half in range(2):
                    hop(step, side, half).wait_send()

            @pl.when(arrives(step, side))
            def _():
                hand(step, side).wait_send()

    for d in range(pairs):
        give(d).wait_send()

        @pl.when(q != d)
        def _():
            for half in range(2):
                far(d, 0, half).wait_send()

    for copy in grad_copies:
        copy.wait_send()


def attend(mixed, cotangent, flag_tile, gain, w_query, w_key, w_value, w_out, scales, collective_id):
    frames, slabs = lax.axis_size("tm"), lax.axis_size("rows")
    pairs = slabs // 2
    rows, cols, channels = cotangent.shape
    size = rows * cols
    bf16, f32 = jnp.bfloat16, jnp.float32
    share = 4 * channels // frames
    dma = pltpu.SemaphoreType.DMA
    return pl.pallas_call(
        functools.partial(attention_kernel, frames, slabs, *scales),
        out_shape=[
            jax.ShapeDtypeStruct((size, channels), f32),
            jax.ShapeDtypeStruct((rows, cols, channels), bf16),
            jax.ShapeDtypeStruct((share, channels), bf16),
        ],
        in_specs=[IN_VMEM] * 8,
        out_specs=[IN_VMEM] * 3,
        scratch_shapes=[
            pltpu.VMEM((slabs, size, channels), bf16),
            pltpu.VMEM((slabs, channels, size), bf16),
            pltpu.VMEM((slabs, size, size), f32),
            pltpu.VMEM((slabs, size, size), f32),
            pltpu.VMEM((slabs, 1, size), f32),
            pltpu.VMEM((slabs, 1, size), f32),
            pltpu.VMEM((slabs, 1, size), f32),
            pltpu.VMEM((slabs,) + flag_tile.shape, bf16),
            pltpu.VMEM((pairs, size, channels), bf16),
            pltpu.VMEM((pairs, size, channels), bf16),
            pltpu.VMEM((pairs, size, channels), bf16),
            pltpu.VMEM((2, pairs, size, channels), bf16),
            pltpu.VMEM((size, channels), f32),
            pltpu.VMEM((channels, size), f32),
            pltpu.VMEM((channels, size), f32),
            pltpu.VMEM((size, channels), bf16),
            pltpu.VMEM((size, channels), bf16),
            pltpu.VMEM((size, channels), bf16),
            pltpu.VMEM((size, channels), bf16),
            pltpu.VMEM((size, channels), bf16),
            pltpu.VMEM((4 * channels, channels), bf16),
            pltpu.VMEM((frames, share, channels), bf16),
            dma((2, slabs)),
            dma((2,)),
            dma((2, 2, pairs + 1, 2)),
            dma((2, 2, pairs)),
            dma((2, pairs)),
            dma((pairs, 2)),
            dma((2, pairs, 2)),
            dma((2, frames)),
        ],
        compiler_params=params(collective_id, 62),
    )(mixed, cotangent, flag_tile, gain, w_query, w_key, w_value, w_out)


def window_rows(count, step):
    return -(-(count + 16 - math.gcd(step, 16)) // 16) * 16


def conv_back_kernel(frames, slabs, grad_scale, *refs):
    (d_conv, history_hbm, weight_hbm, d_mixed, latents, flag_tile, gain, stack) = refs[:8]
    (grad_out, conv_out, attn_out) = refs[8:11]
    (spread, shifted, history, history_t, weight, weight_acc) = refs[11:17]
    (normed, first_scale, slope) = refs[17:20]
    (mine, near, ready, arrive, own_total) = refs[20:25]
    (terms, terms_in, own_term, stack_in) = refs[25:29]
    (load_sems, edge_sems, mid_sems, halo_sems, stack_sems) = refs[29:34]
    (near_sems, far_send, far_recv, term_sems) = refs[34:]
    pairs = slabs // 2
    rows, cols, channels = d_conv.shape
    size = rows * cols
    wide = shifted.shape[3]
    narrow = -(-cols // 16) * 16
    own_rows = weight_hbm.shape[0]
    tap_total = own_rows * frames // channels
    block_rows = own_rows // slabs
    span = mine.shape[1]
    halves = halves_of(span)
    t, r = lax.axis_index("tm"), lax.axis_index("rows")
    q, c = lax.div(r, 2), lax.rem(r, 2)
    other = 1 - c
    sibling = 2 * q + other
    frame_at = [flipped(t, frames, d) for d in range(frames)]
    slab_at = [lax.rem(r + d, slabs) for d in range(slabs)]
    has_above, has_below = r > 0, r < slabs - 1
    first_tap = lax.div(t * own_rows, channels)
    weight_from = pl.multiple_of(t * own_rows - first_tap * channels, 16)
    own_taps = lax.div(weight_from + own_rows + channels - 1, channels)

    def tap_at(j):
        k = jnp.minimum(first_tap + j, tap_total - 1)
        return lax.div(k, 9), lax.rem(lax.div(k, 3), 3), lax.rem(k, 3)

    weight[...] = jnp.zeros_like(weight)
    loads = [
        pltpu.make_async_copy(history_hbm, history, load_sems.at[0]),
        pltpu.make_async_copy(
            weight_hbm, weight.at[pl.ds(weight_from, own_rows)], load_sems.at[1]
        ),
    ]
    for copy in loads:
        copy.start()
    barrier = pltpu.get_barrier_semaphore()
    for d in range(1, slabs):
        signal(barrier, t, slab_at[d])
    for d in range(1, frames):
        signal(barrier, frame_at[d], r)
    for h in range(rows):
        spread[t, h + 1] = d_conv[h]

    @pl.when(r == 0)
    def _():
        for f in range(frames):
            spread[f, 0] = jnp.zeros((cols, channels), spread.dtype)

    @pl.when(r == slabs - 1)
    def _():
        for f in range(frames):
            spread[f, rows + 1] = jnp.zeros((cols, channels), spread.dtype)

    pl.semaphore_wait(barrier, slabs + frames - 2)

    def edge(d, i):
        part = spread.at[t, 1 if i == 0 else rows]
        return remote(
            part, part, edge_sems.at[0, d, i], edge_sems.at[1, d, i], frame_at[d], r
        )

    def middle(d):
        part = spread.at[t, pl.ds(2, rows - 2)]
        return remote(part, part, mid_sems.at[0, d], mid_sems.at[1, d], frame_at[d], r)

    def halo(d, i):
        return remote(
            spread.at[frame_at[d], 1 if i == 0 else rows],
            spread.at[frame_at[d], rows + 1 if i == 0 else 0],
            halo_sems.at[0, d, i],
            halo_sems.at[1, d, i],
            t,
            r - 1 if i == 0 else r + 1,
        )

    def send_halos(d):
        @pl.when(has_above)
        def _():
            halo(d, 0).start()

        @pl.when(has_below)
        def _():
            halo(d, 1).start()

    def pass_edges(d):
        for i in range(2):
            edge(d, i).wait_recv()
        send_halos(d)

    near_frames = [d for d in range(1, frames) if d & (d - 1) == 0]
    late_frames = [d for d in range(1, frames) if d & (d - 1) != 0]
    for d in near_frames:
        edge(d, 0).start()
        edge(d, 1).start()
    send_halos(0)
    for d in near_frames:
        middle(d).start()
    for d in late_frames:
        edge(d, 0).start()
        edge(d, 1).start()
    for d in late_frames:
        middle(d).start()

    share = stack_in.shape[1]
    stack_step = attn_out.shape[0]

    def stack_low(at):
        return pl.multiple_of(lax.div(at * stack_step, 16) * 16, 16)

    stack_copies = [
        remote(
            stack.at[pl.ds(stack_low(slab_at[d]), share)],
            stack_in.at[d],
            stack_sems.at[0, d],
            stack_sems.at[1, d],
            t,
            slab_at[d],
        )
        for d in range(1, slabs)
    ]
    for copy in stack_copies:
        copy.start()

    weight_acc[...] = jnp.zeros_like(weight_acc)
    history_t[0] = jnp.zeros(history_t.shape[1:], history_t.dtype)
    history_t[1] = jnp.zeros(history_t.shape[1:], history_t.dtype)
    for dw in range(3):
        for f in range(2):
            shifted[dw, frames + f] = jnp.zeros(shifted.shape[2:], shifted.dtype)
    for copy in loads:
        copy.wait()
    spare = jnp.zeros((wide - cols, channels), jnp.float32)

    def turn(f, carry):
        for h in range(rows + 2):
            line = jnp.concatenate([history[f, h].astype(jnp.float32), spare], axis=0)
            history_t[f + 2, :, h * wide : (h + 1) * wide] = line.astype(jnp.bfloat16).T
        return carry

    lax.fori_loop(0, frames, turn, 0)
    inputs = latents[...].astype(jnp.float32)
    scale_one = lax.rsqrt(jnp.mean(inputs * inputs, axis=1, keepdims=True) + epsilon)
    normed_one = inputs * scale_one
    first_scale[...] = scale_one
    normed[...] = normed_one
    factor = gain[...] * silu_slope(normed_one * gain[...])
    for h in range(rows):
        flag = flag_tile[h : h + 1, 0:1].astype(jnp.float32)
        part = factor[h * cols : (h + 1) * cols]
        slope[h * cols : (h + 1) * cols, :] = jnp.where(flag > 0, part, 0.0)

    for d in near_frames:
        pass_edges(d)

    def stage(d):
        f = frame_at[d]
        if d > 0:
            middle(d).wait_recv()

        @pl.when(has_below)
        def _():
            halo(d, 0).wait_recv()

        @pl.when(has_above)
        def _():
            halo(d, 1).wait_recv()

        def widen(h, carry):
            line = jnp.concatenate([spread[f, h].astype(jnp.float32), spare], axis=0)
            shifted[0, f, h] = pltpu.roll(line, wide - 1, 0).astype(jnp.bfloat16)
            shifted[1, f, h] = line.astype(jnp.bfloat16)
            shifted[2, f, h] = pltpu.roll(line, 1, 0).astype(jnp.bfloat16)
            return carry

        lax.fori_loop(0, rows + 2, widen, 0)

        def weigh(j, carry):
            dt, dh, dw = tap_at(j)
            lanes = pl.ds(pl.multiple_of(dh * wide, wide), rows * wide)
            ahead = shifted[dw, f, 1 : rows + 1].reshape(rows * wide, channels)
            at = pl.ds(pl.multiple_of(j * channels, channels), channels)
            weight_acc[at, :] += dot(history_t[f + dt, :, lanes], ahead)
            return carry

        lax.fori_loop(0, own_taps, weigh, 0)

    stage(0)
    for i, d in enumerate(near_frames):
        if i == len(near_frames) - 1:
            for e in late_frames:
                pass_edges(e)
        stage(d)
    for d in late_frames:
        stage(d)

    def low_row(block):
        return pl.multiple_of(lax.div(weight_from + block * block_rows, 16) * 16, 16)

    def weight_block(block):
        return weight_acc[pl.ds(low_row(block), span), :] * grad_scale

    def give(d):
        part = mine.at[d]
        return remote(part, near.at[d], near_sems.at[0, d], near_sems.at[1, d], t, sibling)

    def far(d, side, half):
        start, count = halves[half]
        return remote(
            ready.at[d, pl.ds(start, count)],
            arrive.at[side, d, pl.ds(start, count)],
            far_send.at[d, half],
            far_recv.at[side, d, half],
            t,
            r + 2 - 4 * side,
        )

    low_half = (q < (pairs + 1) // 2).astype(jnp.int32)
    right_count = pairs - 1 - q

    def chip_order(i):
        low_order = jnp.where(i < right_count, pairs - 1 - i, i - right_count)
        high_order = jnp.where(i < q, i, pairs - 1 - (i - q))
        order = low_half * low_order + (1 - low_half) * high_order
        return jnp.where(i == pairs - 1, q, order)

    def one_gift(i, carry):
        d = chip_order(i)
        mine[d] = weight_block(2 * d + other).astype(jnp.bfloat16)
        give(d).start()
        return carry

    def one_chip(i, carry):
        d = chip_order(i)
        term = weight_block(2 * d + c)
        give(d).wait_recv()
        term = term + near[d].astype(jnp.float32)

        @pl.when(i == pairs - 1)
        def _():
            own_total[...] = term

        @pl.when(i < pairs - 1)
        def _():
            ready[d] = term.astype(jnp.bfloat16)

        @pl.when(jnp.logical_and(q == 0, d > q))
        def _():
            far(d, 0, 0).start()
            far(d, 0, 1).start()

        @pl.when(jnp.logical_and(q == pairs - 1, d < q))
        def _():
            far(d, 1, 0).start()
            far(d, 1, 1).start()

        return carry

    lax.fori_loop(0, pairs, one_gift, 0)
    lax.fori_loop(0, pairs, one_chip, 0)

    def back(f):
        def one(j, total):
            dt, dh, dw = tap_at(j)
            ahead = shifted[dw, f + 2 - dt, pl.ds(2 - dh, rows), :narrow]
            at = pl.ds(pl.multiple_of(j * channels, channels), channels)
            return total + contract_last(ahead.reshape(rows * narrow, channels), weight[at, :])

        total = lax.fori_loop(
            0, own_taps, one, jnp.zeros((rows * narrow, channels), jnp.float32)
        )
        return total.reshape(rows, narrow, channels)[:, :cols]

    def term_copy(d):
        return remote(
            terms.at[d], terms_in.at[d], term_sems.at[0, d], term_sems.at[1, d], frame_at[d], r
        )

    for d in late_frames + near_frames:
        terms[d] = back(frame_at[d]).astype(jnp.bfloat16)
        term_copy(d).start()

    def relay(phase, carry):
        side = jnp.where(phase == 0, 1 - low_half, low_half)
        has_up = jnp.where(side == 0, q > 0, q < pairs - 1)
        count = jnp.where(side == 0, right_count, q)

        def one(i, carry):
            d = jnp.where(side == 0, pairs - 1 - i, i)

            @pl.when(jnp.logical_and(has_up, i < count))
            def _():
                for half in range(2):
                    start, length = halves[half]
                    part = pl.ds(start, length)
                    far(d, side, half).wait_recv()
                    ready[d, part] = (
                        ready[d, part].astype(jnp.float32)
                        + arrive[side, d, part].astype(jnp.float32)
                    ).astype(jnp.bfloat16)
                    far(d, side, half).start()

            return carry

        return lax.fori_loop(0, pairs - 1, one, carry)

    lax.fori_loop(0, 2, relay, 0)
    own_term[...] = back(t).reshape(size, channels)

    stack_sum = stack[pl.ds(stack_low(r), share), :].astype(jnp.float32)
    for d in range(1, slabs):
        stack_copies[d - 1].wait_recv()
        stack_sum = stack_sum + stack_in[d].astype(jnp.float32)
    if share > stack_step:
        stack_sum = pltpu.roll(stack_sum, share - (r * stack_step - stack_low(r)), 0)
    attn_out[...] = stack_sum[:stack_step]

    for d in near_frames + late_frames:
        term_copy(d).wait_recv()
        own_term[...] += terms_in[d].astype(jnp.float32).reshape(size, channels)
    scaled_one = own_term[...] * slope[...]
    normed_one = normed[...]
    input_grad = d_mixed[...] + first_scale[...] * (
        scaled_one - normed_one * jnp.mean(scaled_one * normed_one, axis=1, keepdims=True)
    )
    grad_out[...] = input_grad.reshape(rows, cols, channels).astype(grad_out.dtype)

    for side in range(2):

        @pl.when(q > 0 if side == 0 else q < pairs - 1)
        def _():
            for half in range(2):
                start, length = halves[half]
                far(q, side, half).wait_recv()
                part = pl.ds(start, length)
                own_total[part, :] += arrive[side, q, part].astype(jnp.float32)

    result = own_total[...]
    if span > block_rows:
        offset = weight_from + r * block_rows - low_row(r)
        result = pltpu.roll(result, span - offset, 0)
    conv_out[...] = result[:block_rows]

    for d in range(frames):
        if d > 0:
            edge(d, 0).wait_send()
            edge(d, 1).wait_send()
            middle(d).wait_send()
            term_copy(d).wait_send()

        @pl.when(has_above)
        def _():
            halo(d, 0).wait_send()

        @pl.when(has_below)
        def _():
            halo(d, 1).wait_send()

    for copy in stack_copies:
        copy.wait_send()
    for d in range(pairs):
        give(d).wait_send()

        @pl.when(q != d)
        def _():
            for half in range(2):
                far(d, 0, half).wait_send()


def conv_back(
    d_conv, history, conv_weight, d_mixed, latents, flag_tile, gain, stack, grad_scale, collective_id
):
    frames, slabs = lax.axis_size("tm"), lax.axis_size("rows")
    pairs = slabs // 2
    rows, cols, channels = d_conv.shape
    size = rows * cols
    bf16, f32 = jnp.bfloat16, jnp.float32
    wide = -(-cols // 128) * 128
    own_rows = conv_weight.shape[0]
    padded = padded_taps(own_rows, frames, channels) * channels
    block_rows = own_rows // slabs
    span = window_rows(block_rows, math.gcd(own_rows, block_rows))
    stack_rows = stack.shape[0] // slabs
    share = window_rows(stack_rows, stack_rows)
    if share > stack_rows:
        stack = jnp.pad(stack, ((0, 16), (0, 0)))
    dma = pltpu.SemaphoreType.DMA
    return pl.pallas_call(
        functools.partial(conv_back_kernel, frames, slabs, grad_scale),
        out_shape=[
            jax.ShapeDtypeStruct((rows, cols, channels), bf16),
            jax.ShapeDtypeStruct((block_rows, channels), f32),
            jax.ShapeDtypeStruct((stack_rows, channels), f32),
        ],
        in_specs=[IN_VMEM, ANY, ANY] + [IN_VMEM] * 5,
        out_specs=[IN_VMEM] * 3,
        scratch_shapes=[
            pltpu.VMEM((frames, rows + 2, cols, channels), bf16),
            pltpu.VMEM((3, frames + 2, rows + 2, wide, channels), bf16),
            pltpu.VMEM((frames, rows + 2, cols, channels), bf16),
            pltpu.VMEM((frames + 2, channels, (rows + 2) * wide), bf16),
            pltpu.VMEM((padded, channels), bf16),
            pltpu.VMEM((padded + 32, channels), f32),
            pltpu.VMEM((size, channels), f32),
            pltpu.VMEM((size, 1), f32),
            pltpu.VMEM((size, channels), f32),
            pltpu.VMEM((pairs, span, channels), bf16),
            pltpu.VMEM((pairs, span, channels), bf16),
            pltpu.VMEM((pairs, span, channels), bf16),
            pltpu.VMEM((2, pairs, span, channels), bf16),
            pltpu.VMEM((span, channels), f32),
            pltpu.VMEM((frames, rows, cols, channels), bf16),
            pltpu.VMEM((frames, rows, cols, channels), bf16),
            pltpu.VMEM((size, channels), f32),
            pltpu.VMEM((slabs, share, channels), bf16),
            dma((2,)),
            dma((2, frames, 2)),
            dma((2, frames)),
            dma((2, frames, 2)),
            dma((2, slabs)),
            dma((2, pairs)),
            dma((pairs, 2)),
            dma((2, pairs, 2)),
            dma((2, frames)),
        ],
        compiler_params=params(collective_id, 62),
    )(d_conv, history, conv_weight, d_mixed, latents, flag_tile, gain, stack)


def finish_kernel(count, *refs):
    for i in range(count):
        refs[count + i][...] = refs[i][...]


def finish(arrays):
    count = len(arrays)
    return pl.pallas_call(
        functools.partial(finish_kernel, count),
        out_shape=[jax.ShapeDtypeStruct(a.shape, a.dtype) for a in arrays],
        in_specs=[IN_VMEM] * count,
        out_specs=[IN_VMEM] * count,
    )(*arrays)


def per_device(
    latents, row_valid, norm_gain, conv_weight, attn_gain, w_query, w_key, w_value, w_out, cotangent
):
    shape_all = latents.shape
    rows, cols, channels = shape_all[1:]
    frames, slabs = lax.axis_size("tm"), lax.axis_size("rows")
    grad_scale = 1.0 / math.sqrt(frames * slabs * rows * cols)
    inv_root = 1.0 / math.sqrt(channels)
    latents = latents.reshape(rows, cols, channels)
    history, mixed, flag_tile = convolve_frames(latents, row_valid, norm_gain, conv_weight, 0)
    d_mixed, d_conv, stack = attend(
        mixed,
        cotangent.reshape(rows, cols, channels),
        flag_tile,
        attn_gain,
        w_query,
        w_key,
        w_value,
        w_out,
        (grad_scale, inv_root),
        1,
    )
    results = conv_back(
        d_conv,
        history,
        conv_weight,
        d_mixed,
        latents.reshape(rows * cols, channels),
        flag_tile,
        norm_gain,
        stack,
        grad_scale,
        2,
    )
    input_grad, conv_weight_grad, attn_weight_grad = finish(results)
    return input_grad.reshape(shape_all), conv_weight_grad, attn_weight_grad


def solution(mesh):
    return jax.shard_map(
        per_device,
        mesh=mesh,
        in_specs=(
            P("tm", "rows", None, None),
            P("rows"),
            P(),
            P("tm", None),
            P(),
            P(),
            P(),
            P(),
            P(),
            P("tm", "rows", None, None),
        ),
        out_specs=(P("tm", "rows", None, None), P(("tm", "rows"), None), P(("tm", "rows"), None)),
        check_vma=False,
    )
```

```python
import functools
import math

import jax
import jax.numpy as jnp
from jax import lax
from jax.experimental import pallas as pl
from jax.experimental.pallas import tpu as pltpu
from jax.sharding import PartitionSpec as P

epsilon = 1e-06
MESH = pl.DeviceIdType.MESH
ANY = pl.BlockSpec(memory_space=pl.ANY)
IN_VMEM = pl.BlockSpec(memory_space=pltpu.VMEM)
FLAG_ROWS = 16


def contract_last(first_op, second_op):
    return lax.dot_general(
        first_op, second_op, (((1,), (1,)), ((), ())), preferred_element_type=jnp.float32
    )


def contract_first(first_op, second_op):
    return lax.dot_general(
        first_op, second_op, (((0,), (0,)), ((), ())), preferred_element_type=jnp.float32
    )


def dot(first_op, second_op):
    return jnp.dot(first_op, second_op, preferred_element_type=jnp.float32)


def silu_slope(inputs):
    logistic = jax.nn.sigmoid(inputs)
    return logistic * (1.0 + inputs * (1.0 - logistic))


def params(collective_id, mebibytes=40):
    return pltpu.CompilerParams(
        collective_id=collective_id,
        has_side_effects=True,
        vmem_limit_bytes=mebibytes * 1024 * 1024,
    )


def signal(barrier, tm_at, row_at):
    pl.semaphore_signal(barrier, inc=1, device_id=(tm_at, row_at), device_id_type=MESH)


def remote(src, dst, send_sem, recv_sem, tm_at, row_at):
    return pltpu.make_async_remote_copy(
        src_ref=src,
        dst_ref=dst,
        send_sem=send_sem,
        recv_sem=recv_sem,
        device_id=(tm_at, row_at),
        device_id_type=MESH,
    )


def flipped(index, count, d):
    total, bit = index, 1
    while bit < count:
        flip = lax.rem(lax.div(jnp.int32(d), bit), 2)
        total = total + flip * bit * (1 - 2 * lax.rem(lax.div(index, bit), 2))
        bit *= 2
    return total


def bits_of(frames):
    return [1 << i for i in range(frames.bit_length() - 1)]


def orders_of(frames):
    bits = bits_of(frames)
    return [bits, bits[::-1]]


def levels_of(frames):
    depth = frames.bit_length() - 1
    return [[m for m in range(frames) if bin(m).count("1") == i] for i in range(depth + 1)]


def greet(barrier, t, r, frames, slabs, frame_at, steps):
    for b in bits_of(frames):
        signal(barrier, frame_at[b], r)
    count = len(bits_of(frames))
    for step in steps:
        ahead, behind = r + step < slabs, r - step >= 0

        @pl.when(ahead)
        def _():
            signal(barrier, t, r + step)

        @pl.when(behind)
        def _():
            signal(barrier, t, r - step)

        count = count + ahead.astype(jnp.int32) + behind.astype(jnp.int32)
    return count


class FrameGather:
    def __init__(self, frames, slabs, slots, sems, halo_sems, rows, t, r, frame_at):
        self.orders, self.slots, self.sems, self.halo_sems = orders_of(frames), slots, sems, halo_sems
        self.frames, self.rows, self.t, self.r, self.frame_at = frames, rows, t, r, frame_at
        self.has_above, self.has_below = r > 0, r < slabs - 1

    def piece(self, part, inner):
        half = self.rows // 2
        if not inner:
            return pl.ds(1 if part == 0 else self.rows, 1)
        return pl.ds(2 if part == 0 else half + 1, half - 1)

    def later(self, part, m):
        order = self.orders[part]
        last = max([i for i, b in enumerate(order) if m & b], default=-1)
        return order[last + 1 :]

    def copy(self, part, inner, m, b):
        rows = self.slots.at[self.frame_at[m], self.piece(part, inner)]
        at = part, inner, m | b
        return remote(
            rows, rows, self.sems.at[(0,) + at], self.sems.at[(1,) + at], self.frame_at[b], self.r
        )

    def arrived(self, part, inner, m):
        b = max(self.orders[part].index(b) for b in self.orders[part] if m & b)
        b = self.orders[part][b]
        return self.copy(part, inner, m - b, b)

    def send(self, part, inner, m):
        for b in self.later(part, m):
            self.copy(part, inner, m, b).start()

    def halo(self, m, i):
        slot = flipped(self.t, self.frames, m)
        return remote(
            self.slots.at[slot, 1 if i == 0 else self.rows],
            self.slots.at[slot, self.rows + 1 if i == 0 else 0],
            self.halo_sems.at[0, m, i],
            self.halo_sems.at[1, m, i],
            self.t,
            self.r - 1 if i == 0 else self.r + 1,
        )

    def send_halo(self, m, i):
        @pl.when(self.has_above if i == 0 else self.has_below)
        def _():
            self.halo(m, i).start()

    def start(self):
        for inner in range(2):
            for i in range(len(self.orders[0])):
                for part in range(2):
                    self.copy(part, inner, 0, self.orders[part][i]).start()
            if inner == 0:
                self.send_halo(0, 0)
                self.send_halo(0, 1)

    def edges(self, frames):
        for m in frames:
            for part in range(2):
                self.arrived(part, 0, m).wait_recv()
                self.send(part, 0, m)
                self.send_halo(m, part)

    def inners(self, frames):
        for m in frames:
            for part in range(2):
                self.arrived(part, 1, m).wait_recv()
                self.send(part, 1, m)

    def wait_halos(self, m):
        @pl.when(self.has_below)
        def _():
            self.halo(m, 0).wait_recv()

        @pl.when(self.has_above)
        def _():
            self.halo(m, 1).wait_recv()

    def run(self, stage):
        levels = levels_of(self.frames)
        before = [[] for _ in range(self.frames)]
        turn = [m for level in levels for m in level]
        before[0].append((self.edges, levels[1]))
        before[1].append((self.inners, levels[1]))
        place = 1
        for i in range(1, len(levels) - 1):
            before[place + 1].append((self.edges, levels[i + 1]))
            place += len(levels[i])
            before[place].append((self.inners, levels[i + 1]))

        def one(k, carry):
            m = 0
            for i in range(self.frames):
                chosen = (k == i).astype(jnp.int32)
                m = m + chosen * turn[i]
                if before[i]:

                    @pl.when(k == i)
                    def _():
                        for action, group in before[i]:
                            action(group)

            stage(m)
            return carry

        lax.fori_loop(0, self.frames, one, 0)

    def close(self):
        for m in range(self.frames):
            for part in range(2):
                for inner in range(2):
                    for b in self.later(part, m):
                        self.copy(part, inner, m, b).wait_send()

            @pl.when(self.has_above)
            def _():
                self.halo(m, 0).wait_send()

            @pl.when(self.has_below)
            def _():
                self.halo(m, 1).wait_send()


class FrameSwap:
    def __init__(self, frames, terms, terms_in, sems, rows, r, frame_at):
        self.orders, self.terms, self.terms_in, self.sems = orders_of(frames), terms, terms_in, sems
        self.frames, self.rows, self.r, self.frame_at = frames, rows, r, frame_at

    def part(self, i):
        half = self.rows // 2
        return pl.ds(i * half, half)

    def first(self, i, d):
        return next((n for n, b in enumerate(self.orders[i]) if d & b), len(self.orders[i]))

    def copy(self, i, d):
        return remote(
            self.terms.at[d, self.part(i)],
            self.terms_in.at[d, self.part(i)],
            self.sems.at[0, i, d],
            self.sems.at[1, i, d],
            self.frame_at[self.orders[i][self.first(i, d)]],
            self.r,
        )

    def computed(self, d):
        for i in range(2):
            if self.first(i, d) == 0:
                self.copy(i, d).start()

    def run(self, term, own):
        turn = [d for level in levels_of(self.frames)[::-1] for d in level]

        def one(k, carry):
            d = 0
            for i in range(self.frames):
                d = d + (k == i).astype(jnp.int32) * turn[i]
            block = term(d)

            @pl.when(k < self.frames - 1)
            def _():
                self.terms[d] = block.astype(self.terms.dtype)

            @pl.when(k == self.frames - 1)
            def _():
                own[...] = block

            for i in range(self.frames - 1):

                @pl.when(k == i)
                def _():
                    self.computed(turn[i])

            return carry

        return lambda start, stop: lax.fori_loop(start, stop, one, 0)

    def received(self, i, d):
        return [d | b for b in self.orders[i][: self.first(i, d)]]

    def pass_on(self):
        for n in range(1, len(self.orders[0])):
            for d in range(self.frames - 1, 0, -1):
                for i in range(2):
                    if self.first(i, d) == n:
                        part = self.part(i)
                        total = self.terms[d, part].astype(jnp.float32)
                        for e in self.received(i, d):
                            self.copy(i, e).wait_recv()
                            total = total + self.terms_in[e, part].astype(jnp.float32)
                        self.terms[d, part] = total.astype(self.terms.dtype)
                        self.copy(i, d).start()

    def add_to(self, total):
        for i in range(2):
            part = self.part(i)
            for e in self.received(i, 0):
                self.copy(i, e).wait_recv()
                total[part] = total[part] + self.terms_in[e, part].astype(jnp.float32)

    def close(self):
        for d in range(1, self.frames):
            for i in range(2):
                self.copy(i, d).wait_send()


def relay_line(pairs, q, far, ready, arrive, halves):
    low = (q < (pairs + 1) // 2).astype(jnp.int32)
    hops = pairs - 1 - 2 * q
    shift = 2 * hops * (2 * low - 1)

    def item(k, side, there):
        i = lax.div(k, 2)
        has_up = jnp.where(side == 0, q > 0, q < pairs - 1)
        count = jnp.where(side == 0, pairs - 1 - q, q)
        d = jnp.where(side == 0, pairs - 1 - i, i)
        for half in range(2):
            start, length = halves[half]
            part = pl.ds(start, length)
            wanted = jnp.logical_and(lax.rem(k, 2) == half, jnp.logical_and(there, i < count))

            @pl.when(jnp.logical_and(has_up, wanted))
            def _():
                far(d, side, half).wait_recv()
                ready[d, part] = (
                    ready[d, part].astype(jnp.float32) + arrive[side, d, part].astype(jnp.float32)
                ).astype(jnp.bfloat16)
                far(d, side, half).start()

    def slot(k, carry):
        item(jnp.maximum(k - shift, 0), low, k >= shift)
        item(k, 1 - low, True)
        return carry

    lax.fori_loop(0, 2 * (pairs - 1), slot, 0)


def padded_taps(own_rows, frames, channels):
    return max(-(-((i * own_rows) % channels + own_rows) // channels) for i in range(frames))


def conv_kernel(frames, slabs, *refs):
    (latents, row_valid, gain, weight_hbm) = refs[:4]
    (history, mixed, flag_tile) = refs[4:7]
    (shifted, weight, terms, terms_in, total) = refs[7:12]
    (load_sem, gather_sems, halo_sems, term_sems) = refs[12:]
    rows, cols, channels = latents.shape
    size = rows * cols
    narrow = shifted.shape[3]
    own_rows = weight_hbm.shape[0]
    tap_total = own_rows * frames // channels
    t, r = lax.axis_index("tm"), lax.axis_index("rows")
    frame_at = [flipped(t, frames, d) for d in range(frames)]
    first_tap = lax.div(t * own_rows, channels)
    weight_from = pl.multiple_of(t * own_rows - first_tap * channels, 16)
    tap_count = weight.shape[0] // channels

    barrier = pltpu.get_barrier_semaphore()
    greeted = greet(barrier, t, r, frames, slabs, frame_at, [1])
    flag_tile[...] = jnp.zeros_like(flag_tile)
    for h in range(rows):
        flag = row_valid[h].astype(jnp.float32)
        part = latents[h].astype(jnp.float32)
        scale = lax.rsqrt(jnp.mean(part * part, axis=1, keepdims=True) + epsilon)
        part = jax.nn.silu(part * scale * gain[...]) * flag
        history[t, h + 1] = part.astype(jnp.bfloat16)

    @pl.when(r == 0)
    def _():
        for f in range(frames):
            history[f, 0] = jnp.zeros((cols, channels), history.dtype)

    @pl.when(r == slabs - 1)
    def _():
        for f in range(frames):
            history[f, rows + 1] = jnp.zeros((cols, channels), history.dtype)

    pl.semaphore_wait(barrier, greeted)
    gather = FrameGather(
        frames, slabs, history, gather_sems, halo_sems, rows, t, r, frame_at
    )
    swap = FrameSwap(frames, terms, terms_in, term_sems, rows, r, frame_at)
    gather.start()
    for h in range(rows):
        flag = row_valid[h].astype(jnp.float32)
        flag_tile[h : h + 1, :] = jnp.full((1, flag_tile.shape[1]), flag, flag_tile.dtype)
    weight[...] = jnp.zeros_like(weight)
    load = pltpu.make_async_copy(weight_hbm, weight.at[pl.ds(weight_from, own_rows)], load_sem)
    load.start()
    for dw in range(3):
        for f in range(2):
            shifted[dw, f] = jnp.zeros(shifted.shape[2:], shifted.dtype)
    spare = jnp.zeros((narrow - cols, channels), jnp.float32)

    def stage(d):
        f = flipped(t, frames, d)
        gather.wait_halos(d)

        def widen(h, carry):
            line = jnp.concatenate([history[f, h].astype(jnp.float32), spare], axis=0)
            shifted[0, f + 2, h] = pltpu.roll(line, 1, 0).astype(jnp.bfloat16)
            shifted[1, f + 2, h] = line.astype(jnp.bfloat16)
            shifted[2, f + 2, h] = pltpu.roll(line, narrow - 1, 0).astype(jnp.bfloat16)
            return carry

        lax.fori_loop(0, rows + 2, widen, 0)

    gather.run(stage)
    load.wait()

    def convolve(f):
        total = None
        for j in range(tap_count):
            k = jnp.minimum(first_tap + j, tap_total - 1)
            dt, dh, dw = lax.div(k, 9), lax.rem(lax.div(k, 3), 3), lax.rem(k, 3)
            window = shifted[dw, f + dt, pl.ds(dh, rows)].reshape(rows * narrow, channels)
            term = dot(window, weight[j * channels : (j + 1) * channels, :])
            total = term if total is None else total + term
        return total.reshape(rows, narrow, channels)[:, :cols]

    swap.run(lambda d: convolve(flipped(t, frames, d)), total)(0, frames)
    total[...] += latents[...].astype(jnp.float32)
    swap.pass_on()
    swap.add_to(total)
    mixed[...] = total[...].reshape(size, channels).astype(mixed.dtype)
    gather.close()
    swap.close()


def convolve_frames(latents, row_valid, gain, conv_weight, collective_id):
    frames, slabs = lax.axis_size("tm"), lax.axis_size("rows")
    rows, cols, channels = latents.shape
    bf16, f32 = jnp.bfloat16, jnp.float32
    narrow = -(-cols // 16) * 16
    padded = padded_taps(conv_weight.shape[0], frames, channels) * channels
    dma = pltpu.SemaphoreType.DMA
    return pl.pallas_call(
        functools.partial(conv_kernel, frames, slabs),
        out_shape=[
            jax.ShapeDtypeStruct((frames, rows + 2, cols, channels), bf16),
            jax.ShapeDtypeStruct((rows * cols, channels), bf16),
            jax.ShapeDtypeStruct((FLAG_ROWS, 128), bf16),
        ],
        in_specs=[IN_VMEM, pl.BlockSpec(memory_space=pltpu.SMEM), IN_VMEM, ANY],
        out_specs=[IN_VMEM] * 3,
        scratch_shapes=[
            pltpu.VMEM((3, frames + 2, rows + 2, narrow, channels), bf16),
            pltpu.VMEM((padded, channels), bf16),
            pltpu.VMEM((frames, rows, cols, channels), bf16),
            pltpu.VMEM((frames, rows, cols, channels), bf16),
            pltpu.VMEM((rows, cols, channels), f32),
            dma,
            dma((2, 2, 2, frames)),
            dma((2, frames, 2)),
            dma((2, 2, frames)),
        ],
        compiler_params=params(collective_id, 62),
    )(latents, row_valid, gain, conv_weight)


def halves_of(size):
    near = size // 2 // 16 * 16
    return ((0, near), (near, size - near))


def attention_kernel(frames, slabs, grad_scale, inv_root, *refs):
    (mixed, cotangent, flag_tile, gain, w_query, w_key, w_value, w_out) = refs[:8]
    (d_mixed_out, d_conv_out, stack_out) = refs[8:11]
    (cells, cells_t, prob, d_weights, tops, sums, dots) = refs[11:18]
    (mine, near, ready, arrive, own_total, weighted_t, d_cells_t) = refs[18:25]
    (queries, key_side, value_side, d_attended, grad_out) = refs[25:30]
    (grads, grads_in) = refs[30:32]
    (sib_sems, hop_sems, hand_sems, near_sems, far_send, far_recv, grad_sems) = refs[32:]
    pairs = slabs // 2
    rows, cols, channels = cotangent.shape
    size = rows * cols
    halves = halves_of(size)
    t, r = lax.axis_index("tm"), lax.axis_index("rows")
    q, c = lax.div(r, 2), lax.rem(r, 2)
    other = 1 - c
    sibling = 2 * q + other
    frame_at = [lax.rem(t + d, frames) for d in range(frames)]
    barrier = pltpu.get_barrier_semaphore()
    for d in range(1, frames):
        signal(barrier, frame_at[d], r)
    has_left, has_right = q > 0, q < pairs - 1
    signal(barrier, t, sibling)

    @pl.when(has_left)
    def _():
        signal(barrier, t, r - 2)

    @pl.when(has_right)
    def _():
        signal(barrier, t, r + 2)

    mixed_f = mixed[...].astype(jnp.float32)
    second_scale = lax.rsqrt(jnp.mean(mixed_f * mixed_f, axis=1, keepdims=True) + epsilon)
    attn_in = (mixed_f * second_scale * gain[...]).astype(jnp.bfloat16)
    cells[r, :size] = attn_in
    for i in range(channels // 128):
        cells[r, size:, i * 128 : (i + 1) * 128] = flag_tile[...]
    sides = has_left.astype(jnp.int32) + has_right.astype(jnp.int32)
    pl.semaphore_wait(barrier, frames + sides)
    cuts = (halves[0], (halves[1][0], halves[1][1] + FLAG_ROWS))

    def sources(step, side):
        return q - step if side == 0 else q + step

    def arrives(step, side):
        at = sources(step, side)
        return jnp.logical_and(step < pairs, jnp.logical_and(at >= 0, at < pairs))

    def onward(step, side):
        ahead = q < pairs - 1 if side == 0 else q > 0
        return jnp.logical_and(ahead, arrives(step, side))

    def hop(step, side, half):
        start, count = cuts[half]
        part = cells.at[2 * sources(step - 1, side) + c, pl.ds(start, count)]
        target = r + 2 if side == 0 else r - 2
        return remote(
            part, part, hop_sems.at[0, side, step, half], hop_sems.at[1, side, step, half], t, target
        )

    def hand(step, side):
        part = cells.at[2 * sources(step, side) + c]
        return remote(
            part, part, hand_sems.at[0, side, step], hand_sems.at[1, side, step], t, sibling
        )

    to_sibling = remote(cells.at[r], cells.at[r], sib_sems.at[0], sib_sems.at[1], t, sibling)
    for half in range(2):
        for side in range(2):

            @pl.when(onward(0, side))
            def _():
                hop(1, side, half).start()

    to_sibling.start()

    for h in range(rows):
        flag = flag_tile[h : h + 1, 0:1].astype(jnp.float32)
        part = cotangent[h].astype(jnp.float32)
        grad_out[h * cols : (h + 1) * cols, :] = jnp.where(flag > 0, part, 0.0).astype(jnp.bfloat16)
    queries[...] = dot(attn_in, w_query[...]).astype(jnp.bfloat16)
    key_side[...] = contract_last(queries[...], w_key[...]).astype(jnp.bfloat16)
    d_attended[...] = contract_last(grad_out[...], w_out[...]).astype(jnp.bfloat16)
    value_side[...] = contract_last(d_attended[...], w_value[...]).astype(jnp.bfloat16)

    lowest = float(jnp.finfo(jnp.float32).min)

    def absorb(j):
        block = cells[j, :size]
        flags = cells[j, size:, :128].astype(jnp.float32)
        scores = contract_last(block, key_side[...]) * inv_root
        kept = []
        for h in range(rows):
            flag = flags[h : h + 1, 0:1]
            kept.append(jnp.where(flag > 0, scores[h * cols : (h + 1) * cols], lowest))
        scores = jnp.concatenate(kept, axis=0)
        top = jnp.max(scores, axis=0, keepdims=True)
        exponent = jnp.exp(scores - top)
        prob[j] = exponent
        d_weight = contract_last(block, value_side[...])
        d_weights[j] = d_weight
        tops[j] = top
        sums[j] = jnp.sum(exponent, axis=0, keepdims=True)
        dots[j] = jnp.sum(exponent * d_weight, axis=0, keepdims=True)
        cells_t[j] = block.T

    def pass_on(step, half):
        for side in range(2):

            @pl.when(arrives(step, side))
            def _():
                hop(step, side, half).wait_recv()

            @pl.when(onward(step, side))
            def _():
                hop(step + 1, side, half).start()

            if half == 1:

                @pl.when(arrives(step, side))
                def _():
                    hand(step, side).start()

    def own_pair(i, carry):
        @pl.when(i == 1)
        def _():
            to_sibling.wait_recv()

        absorb(2 * q + c + i * (other - c))
        return carry

    lax.fori_loop(0, 2, own_pair, 0)
    pass_on(1, 0)
    pass_on(1, 1)

    def two_slabs(k, carry):
        step, side = 1 + lax.div(k, 2), lax.rem(k, 2)
        at = q - step + 2 * step * side
        there = jnp.logical_and(at >= 0, at < pairs)

        def one(i, carry):
            for s in range(2):

                @pl.when(jnp.logical_and(i == 1, side == s))
                def _():
                    hand(step, s).wait_recv()

            absorb(2 * at + c + i * (other - c))
            return carry

        @pl.when(there)
        def _():
            lax.fori_loop(0, 2, one, 0)

        for half in range(2):

            @pl.when(jnp.logical_and(side == half, step < pairs - 1))
            def _():
                pass_on(step + 1, half)

        return carry

    lax.fori_loop(0, 2 * (pairs - 1), two_slabs, 0)

    top_all = tops[0]
    for j in range(1, slabs):
        top_all = jnp.maximum(top_all, tops[j])
    total_sum = jnp.zeros_like(top_all)
    total_dot = jnp.zeros_like(top_all)
    for j in range(slabs):
        rescale = jnp.exp(tops[j] - top_all)
        total_sum = total_sum + rescale * sums[j]
        total_dot = total_dot + rescale * dots[j]
        tops[j] = rescale
    inverse = 1.0 / total_sum
    row_delta = total_dot * inverse
    weighted_t[...] = jnp.zeros_like(weighted_t)
    d_cells_t[...] = jnp.zeros_like(d_cells_t)

    def emit(j):
        weights = prob[j] * (tops[j] * inverse)
        weights_b = weights.astype(jnp.bfloat16)
        d_scores = (weights * (d_weights[j] - row_delta) * inv_root).astype(jnp.bfloat16)
        block_t = cells_t[j]
        weighted_t[...] += dot(block_t, weights_b)
        d_cells_t[...] += dot(block_t, d_scores)
        return dot(d_scores, key_side[...]) + dot(weights_b, value_side[...])

    def give(d):
        part = mine.at[d]
        return remote(part, near.at[d], near_sems.at[0, d], near_sems.at[1, d], t, sibling)

    def far(d, side, half):
        start, count = halves[half]
        target = r + 2 - 4 * side
        return remote(
            ready.at[d, pl.ds(start, count)],
            arrive.at[side, d, pl.ds(start, count)],
            far_send.at[d, half],
            far_recv.at[side, d, half],
            t,
            target,
        )

    low_half = (q < (pairs + 1) // 2).astype(jnp.int32)
    right_count = pairs - 1 - q

    def chip_order(i):
        from_right = pairs - 1 - i
        low_order = jnp.where(i < right_count, from_right, i - right_count)
        high_order = jnp.where(i < q, i, pairs - 1 - (i - q))
        order = low_half * low_order + (1 - low_half) * high_order
        return jnp.where(i == pairs - 1, q, order)

    def one_chip(i, carry):
        d = chip_order(i)
        mine[d] = emit(2 * d + other).astype(jnp.bfloat16)
        give(d).start()
        term = emit(2 * d + c)
        give(d).wait_recv()
        term = term + near[d].astype(jnp.float32)

        @pl.when(i == pairs - 1)
        def _():
            own_total[...] = term

        @pl.when(i < pairs - 1)
        def _():
            ready[d] = term.astype(jnp.bfloat16)

        @pl.when(jnp.logical_and(q == 0, d > q))
        def _():
            far(d, 0, 0).start()
            far(d, 0, 1).start()

        @pl.when(jnp.logical_and(q == pairs - 1, d < q))
        def _():
            far(d, 1, 0).start()
            far(d, 1, 1).start()

        return carry

    lax.fori_loop(0, pairs, one_chip, 0)

    weighted_b = weighted_t[...].astype(jnp.bfloat16)
    d_cells_b = d_cells_t[...].astype(jnp.bfloat16)
    attended = contract_first(weighted_b, w_value[...]).astype(jnp.bfloat16)
    d_query = contract_first(d_cells_b, w_key[...]).astype(jnp.bfloat16)
    blocks = [
        contract_first(cells[r, :size], d_query),
        dot(d_cells_b, queries[...]),
        dot(weighted_b, d_attended[...]),
        contract_first(attended, grad_out[...]),
    ]
    for i, block in enumerate(blocks):
        grads[i * channels : (i + 1) * channels, :] = (block * grad_scale).astype(jnp.bfloat16)
    share = 4 * channels // frames
    grad_copies = [
        remote(
            grads.at[pl.ds(pl.multiple_of(frame_at[d] * share, share), share)],
            grads_in.at[d],
            grad_sems.at[0, d],
            grad_sems.at[1, d],
            frame_at[d],
            r,
        )
        for d in range(1, frames)
    ]
    for copy in grad_copies:
        copy.start()
    own_total[...] += contract_last(d_query, w_query[...])

    relay_line(pairs, q, far, ready, arrive, halves)

    for copy in grad_copies:
        copy.wait_recv()
    stack = grads[pl.ds(pl.multiple_of(t * share, share), share), :].astype(jnp.float32)
    for d in range(1, frames):
        stack = stack + grads_in[d].astype(jnp.float32)
    stack_out[...] = stack.astype(stack_out.dtype)

    for side in range(2):

        @pl.when(q > 0 if side == 0 else q < pairs - 1)
        def _():
            for half in range(2):
                start, length = halves[half]
                far(q, side, half).wait_recv()
                part = pl.ds(start, length)
                own_total[part, :] += arrive[side, q, part].astype(jnp.float32)

    mixed_f = mixed[...].astype(jnp.float32)
    second_scale = lax.rsqrt(jnp.mean(mixed_f * mixed_f, axis=1, keepdims=True) + epsilon)
    normed_two = mixed_f * second_scale
    scaled_two = gain[...] * own_total[...]
    d_mixed = grad_out[...].astype(jnp.float32) + second_scale * (
        scaled_two - normed_two * jnp.mean(scaled_two * normed_two, axis=1, keepdims=True)
    )
    d_mixed_out[...] = d_mixed
    d_conv_out[...] = d_mixed.astype(jnp.bfloat16).reshape(rows, cols, channels)

    to_sibling.wait_send()
    for side in range(2):
        for step in range(1, pairs):

            @pl.when(onward(step - 1, side))
            def _():
                for half in range(2):
                    hop(step, side, half).wait_send()

            @pl.when(arrives(step, side))
            def _():
                hand(step, side).wait_send()

    for d in range(pairs):
        give(d).wait_send()

        @pl.when(q != d)
        def _():
            for half in range(2):
                far(d, 0, half).wait_send()

    for copy in grad_copies:
        copy.wait_send()


def attend(mixed, cotangent, flag_tile, gain, w_query, w_key, w_value, w_out, scales, collective_id):
    frames, slabs = lax.axis_size("tm"), lax.axis_size("rows")
    pairs = slabs // 2
    rows, cols, channels = cotangent.shape
    size = rows * cols
    bf16, f32 = jnp.bfloat16, jnp.float32
    share = 4 * channels // frames
    dma = pltpu.SemaphoreType.DMA
    return pl.pallas_call(
        functools.partial(attention_kernel, frames, slabs, *scales),
        out_shape=[
            jax.ShapeDtypeStruct((size, channels), f32),
            jax.ShapeDtypeStruct((rows, cols, channels), bf16),
            jax.ShapeDtypeStruct((share, channels), bf16),
        ],
        in_specs=[IN_VMEM] * 8,
        out_specs=[IN_VMEM] * 3,
        scratch_shapes=[
            pltpu.VMEM((slabs, size + FLAG_ROWS, channels), bf16),
            pltpu.VMEM((slabs, channels, size), bf16),
            pltpu.VMEM((slabs, size, size), f32),
            pltpu.VMEM((slabs, size, size), f32),
            pltpu.VMEM((slabs, 1, size), f32),
            pltpu.VMEM((slabs, 1, size), f32),
            pltpu.VMEM((slabs, 1, size), f32),
            pltpu.VMEM((pairs, size, channels), bf16),
            pltpu.VMEM((pairs, size, channels), bf16),
            pltpu.VMEM((pairs, size, channels), bf16),
            pltpu.VMEM((2, pairs, size, channels), bf16),
            pltpu.VMEM((size, channels), f32),
            pltpu.VMEM((channels, size), f32),
            pltpu.VMEM((channels, size), f32),
            pltpu.VMEM((size, channels), bf16),
            pltpu.VMEM((size, channels), bf16),
            pltpu.VMEM((size, channels), bf16),
            pltpu.VMEM((size, channels), bf16),
            pltpu.VMEM((size, channels), bf16),
            pltpu.VMEM((4 * channels, channels), bf16),
            pltpu.VMEM((frames, share, channels), bf16),
            dma((2,)),
            dma((2, 2, pairs + 1, 2)),
            dma((2, 2, pairs)),
            dma((2, pairs)),
            dma((pairs, 2)),
            dma((2, pairs, 2)),
            dma((2, frames)),
        ],
        compiler_params=params(collective_id, 62),
    )(mixed, cotangent, flag_tile, gain, w_query, w_key, w_value, w_out)


def window_rows(count, step):
    return -(-(count + 16 - math.gcd(step, 16)) // 16) * 16


def conv_back_kernel(frames, slabs, grad_scale, *refs):
    (d_conv, history_hbm, weight_hbm, d_mixed, latents, flag_tile, gain, stack) = refs[:8]
    (grad_out, conv_out, attn_out) = refs[8:11]
    (spread, shifted, history, history_t, weight, weight_acc) = refs[11:17]
    (normed, first_scale, slope) = refs[17:20]
    (mine, near, ready, arrive, own_total) = refs[20:25]
    (terms, terms_in, own_term, stack_in) = refs[25:29]
    (load_sems, gather_sems, halo_sems, stack_sems) = refs[29:33]
    (near_sems, far_send, far_recv, term_sems) = refs[33:]
    pairs = slabs // 2
    rows, cols, channels = d_conv.shape
    size = rows * cols
    wide = shifted.shape[3]
    narrow = -(-cols // 16) * 16
    own_rows = weight_hbm.shape[0]
    tap_total = own_rows * frames // channels
    block_rows = own_rows // slabs
    span = mine.shape[1]
    halves = halves_of(span)
    t, r = lax.axis_index("tm"), lax.axis_index("rows")
    q, c = lax.div(r, 2), lax.rem(r, 2)
    other = 1 - c
    sibling = 2 * q + other
    frame_at = [flipped(t, frames, d) for d in range(frames)]
    slab_at = [lax.rem(r + d, slabs) for d in range(slabs)]
    first_tap = lax.div(t * own_rows, channels)
    weight_from = pl.multiple_of(t * own_rows - first_tap * channels, 16)
    tap_count = weight.shape[0] // channels

    def tap_at(j):
        k = jnp.minimum(first_tap + j, tap_total - 1)
        return lax.div(k, 9), lax.rem(lax.div(k, 3), 3), lax.rem(k, 3)

    weight[...] = jnp.zeros_like(weight)
    loads = [
        pltpu.make_async_copy(history_hbm, history, load_sems.at[0]),
        pltpu.make_async_copy(
            weight_hbm, weight.at[pl.ds(weight_from, own_rows)], load_sems.at[1]
        ),
    ]
    for copy in loads:
        copy.start()
    barrier = pltpu.get_barrier_semaphore()
    for d in range(1, slabs):
        signal(barrier, t, slab_at[d])
    for b in bits_of(frames):
        signal(barrier, frame_at[b], r)
    for h in range(rows):
        spread[t, h + 1] = d_conv[h]

    @pl.when(r == 0)
    def _():
        for f in range(frames):
            spread[f, 0] = jnp.zeros((cols, channels), spread.dtype)

    @pl.when(r == slabs - 1)
    def _():
        for f in range(frames):
            spread[f, rows + 1] = jnp.zeros((cols, channels), spread.dtype)

    pl.semaphore_wait(barrier, slabs - 1 + len(bits_of(frames)))
    gather = FrameGather(
        frames, slabs, spread, gather_sems, halo_sems, rows, t, r, frame_at
    )
    swap = FrameSwap(frames, terms, terms_in, term_sems, rows, r, frame_at)
    gather.start()
    share = stack_in.shape[1]
    stack_step = attn_out.shape[0]

    def stack_low(at):
        return pl.multiple_of(lax.div(at * stack_step, 16) * 16, 16)

    stack_copies = [
        remote(
            stack.at[pl.ds(stack_low(slab_at[d]), share)],
            stack_in.at[d],
            stack_sems.at[0, d],
            stack_sems.at[1, d],
            t,
            slab_at[d],
        )
        for d in range(1, slabs)
    ]
    for copy in stack_copies:
        copy.start()

    weight_acc[...] = jnp.zeros_like(weight_acc)
    history_t[0] = jnp.zeros(history_t.shape[1:], history_t.dtype)
    history_t[1] = jnp.zeros(history_t.shape[1:], history_t.dtype)
    for dw in range(3):
        for f in range(2):
            shifted[dw, frames + f] = jnp.zeros(shifted.shape[2:], shifted.dtype)
    for copy in loads:
        copy.wait()
    spare = jnp.zeros((wide - cols, channels), jnp.float32)

    def turn(f, carry):
        for h in range(rows + 2):
            line = jnp.concatenate([history[f, h].astype(jnp.float32), spare], axis=0)
            history_t[f + 2, :, h * wide : (h + 1) * wide] = line.astype(jnp.bfloat16).T
        return carry

    lax.fori_loop(0, frames, turn, 0)
    inputs = latents[...].astype(jnp.float32)
    scale_one = lax.rsqrt(jnp.mean(inputs * inputs, axis=1, keepdims=True) + epsilon)
    normed_one = inputs * scale_one
    first_scale[...] = scale_one
    normed[...] = normed_one
    factor = gain[...] * silu_slope(normed_one * gain[...])
    for h in range(rows):
        flag = flag_tile[h : h + 1, 0:1].astype(jnp.float32)
        part = factor[h * cols : (h + 1) * cols]
        slope[h * cols : (h + 1) * cols, :] = jnp.where(flag > 0, part, 0.0)

    def stage(d):
        f = flipped(t, frames, d)
        gather.wait_halos(d)

        def widen(h, carry):
            line = jnp.concatenate([spread[f, h].astype(jnp.float32), spare], axis=0)
            shifted[0, f, h] = pltpu.roll(line, wide - 1, 0).astype(jnp.bfloat16)
            shifted[1, f, h] = line.astype(jnp.bfloat16)
            shifted[2, f, h] = pltpu.roll(line, 1, 0).astype(jnp.bfloat16)
            return carry

        lax.fori_loop(0, rows + 2, widen, 0)

        for j in range(tap_count):
            dt, dh, dw = tap_at(j)
            lanes = pl.ds(pl.multiple_of(dh * wide, wide), rows * wide)
            ahead = shifted[dw, f, 1 : rows + 1].reshape(rows * wide, channels)
            weight_acc[j * channels : (j + 1) * channels, :] += dot(
                history_t[f + dt, :, lanes], ahead
            )

    gather.run(stage)

    def low_row(block):
        return pl.multiple_of(lax.div(weight_from + block * block_rows, 16) * 16, 16)

    def weight_block(block):
        return weight_acc[pl.ds(low_row(block), span), :] * grad_scale

    def give(d):
        part = mine.at[d]
        return remote(part, near.at[d], near_sems.at[0, d], near_sems.at[1, d], t, sibling)

    def far(d, side, half):
        start, count = halves[half]
        return remote(
            ready.at[d, pl.ds(start, count)],
            arrive.at[side, d, pl.ds(start, count)],
            far_send.at[d, half],
            far_recv.at[side, d, half],
            t,
            r + 2 - 4 * side,
        )

    low_half = (q < (pairs + 1) // 2).astype(jnp.int32)
    right_count = pairs - 1 - q

    def chip_order(i):
        low_order = jnp.where(i < right_count, pairs - 1 - i, i - right_count)
        high_order = jnp.where(i < q, i, pairs - 1 - (i - q))
        order = low_half * low_order + (1 - low_half) * high_order
        return jnp.where(i == pairs - 1, q, order)

    def one_gift(i, carry):
        d = chip_order(i)
        mine[d] = weight_block(2 * d + other).astype(jnp.bfloat16)
        give(d).start()
        return carry

    def one_chip(i, carry):
        d = chip_order(i)
        term = weight_block(2 * d + c)
        give(d).wait_recv()
        term = term + near[d].astype(jnp.float32)

        @pl.when(i == pairs - 1)
        def _():
            own_total[...] = term

        @pl.when(i < pairs - 1)
        def _():
            ready[d] = term.astype(jnp.bfloat16)

        @pl.when(jnp.logical_and(q == 0, d > q))
        def _():
            far(d, 0, 0).start()
            far(d, 0, 1).start()

        @pl.when(jnp.logical_and(q == pairs - 1, d < q))
        def _():
            far(d, 1, 0).start()
            far(d, 1, 1).start()

        return carry

    lax.fori_loop(0, pairs, one_gift, 0)
    lax.fori_loop(0, pairs, one_chip, 0)

    def back(f):
        total = None
        for j in range(tap_count):
            dt, dh, dw = tap_at(j)
            ahead = shifted[dw, f + 2 - dt, pl.ds(2 - dh, rows), :narrow]
            term = contract_last(
                ahead.reshape(rows * narrow, channels),
                weight[j * channels : (j + 1) * channels, :],
            )
            total = term if total is None else total + term
        return total.reshape(rows, narrow, channels)[:, :cols]

    swap.run(lambda d: back(flipped(t, frames, d)), own_term)(0, frames)
    swap.pass_on()
    relay_line(pairs, q, far, ready, arrive, halves)

    stack_sum = stack[pl.ds(stack_low(r), share), :].astype(jnp.float32)
    for d in range(1, slabs):
        stack_copies[d - 1].wait_recv()
        stack_sum = stack_sum + stack_in[d].astype(jnp.float32)
    if share > stack_step:
        stack_sum = pltpu.roll(stack_sum, share - (r * stack_step - stack_low(r)), 0)
    attn_out[...] = stack_sum[:stack_step]

    swap.add_to(own_term)
    scaled_one = own_term[...].reshape(size, channels) * slope[...]
    normed_one = normed[...]
    input_grad = d_mixed[...] + first_scale[...] * (
        scaled_one - normed_one * jnp.mean(scaled_one * normed_one, axis=1, keepdims=True)
    )
    grad_out[...] = input_grad.reshape(rows, cols, channels).astype(grad_out.dtype)

    for side in range(2):

        @pl.when(q > 0 if side == 0 else q < pairs - 1)
        def _():
            for half in range(2):
                start, length = halves[half]
                far(q, side, half).wait_recv()
                part = pl.ds(start, length)
                own_total[part, :] += arrive[side, q, part].astype(jnp.float32)

    result = own_total[...]
    if span > block_rows:
        offset = weight_from + r * block_rows - low_row(r)
        result = pltpu.roll(result, span - offset, 0)
    conv_out[...] = result[:block_rows]

    gather.close()
    swap.close()
    for copy in stack_copies:
        copy.wait_send()
    for d in range(pairs):
        give(d).wait_send()

        @pl.when(q != d)
        def _():
            for half in range(2):
                far(d, 0, half).wait_send()


def conv_back(
    d_conv, history, conv_weight, d_mixed, latents, flag_tile, gain, stack, grad_scale, collective_id
):
    frames, slabs = lax.axis_size("tm"), lax.axis_size("rows")
    pairs = slabs // 2
    rows, cols, channels = d_conv.shape
    size = rows * cols
    bf16, f32 = jnp.bfloat16, jnp.float32
    wide = -(-cols // 128) * 128
    own_rows = conv_weight.shape[0]
    padded = padded_taps(own_rows, frames, channels) * channels
    block_rows = own_rows // slabs
    span = window_rows(block_rows, math.gcd(own_rows, block_rows))
    stack_rows = stack.shape[0] // slabs
    share = window_rows(stack_rows, stack_rows)
    if share > stack_rows:
        stack = jnp.pad(stack, ((0, 16), (0, 0)))
    dma = pltpu.SemaphoreType.DMA
    return pl.pallas_call(
        functools.partial(conv_back_kernel, frames, slabs, grad_scale),
        out_shape=[
            jax.ShapeDtypeStruct((rows, cols, channels), bf16),
            jax.ShapeDtypeStruct((block_rows, channels), f32),
            jax.ShapeDtypeStruct((stack_rows, channels), f32),
        ],
        in_specs=[IN_VMEM, ANY, ANY] + [IN_VMEM] * 5,
        out_specs=[IN_VMEM] * 3,
        scratch_shapes=[
            pltpu.VMEM((frames, rows + 2, cols, channels), bf16),
            pltpu.VMEM((3, frames + 2, rows + 2, wide, channels), bf16),
            pltpu.VMEM((frames, rows + 2, cols, channels), bf16),
            pltpu.VMEM((frames + 2, channels, (rows + 2) * wide), bf16),
            pltpu.VMEM((padded, channels), bf16),
            pltpu.VMEM((padded + 32, channels), f32),
            pltpu.VMEM((size, channels), f32),
            pltpu.VMEM((size, 1), f32),
            pltpu.VMEM((size, channels), f32),
            pltpu.VMEM((pairs, span, channels), bf16),
            pltpu.VMEM((pairs, span, channels), bf16),
            pltpu.VMEM((pairs, span, channels), bf16),
            pltpu.VMEM((2, pairs, span, channels), bf16),
            pltpu.VMEM((span, channels), f32),
            pltpu.VMEM((frames, rows, cols, channels), bf16),
            pltpu.VMEM((frames, rows, cols, channels), bf16),
            pltpu.VMEM((rows, cols, channels), f32),
            pltpu.VMEM((slabs, share, channels), bf16),
            dma((2,)),
            dma((2, 2, 2, frames)),
            dma((2, frames, 2)),
            dma((2, slabs)),
            dma((2, pairs)),
            dma((pairs, 2)),
            dma((2, pairs, 2)),
            dma((2, 2, frames)),
        ],
        compiler_params=params(collective_id, 62),
    )(d_conv, history, conv_weight, d_mixed, latents, flag_tile, gain, stack)


def finish_kernel(count, *refs):
    for i in range(count):
        refs[count + i][...] = refs[i][...]


def finish(arrays):
    count = len(arrays)
    return pl.pallas_call(
        functools.partial(finish_kernel, count),
        out_shape=[jax.ShapeDtypeStruct(a.shape, a.dtype) for a in arrays],
        in_specs=[IN_VMEM] * count,
        out_specs=[IN_VMEM] * count,
    )(*arrays)


def per_device(
    latents, row_valid, norm_gain, conv_weight, attn_gain, w_query, w_key, w_value, w_out, cotangent
):
    shape_all = latents.shape
    rows, cols, channels = shape_all[1:]
    frames, slabs = lax.axis_size("tm"), lax.axis_size("rows")
    grad_scale = 1.0 / math.sqrt(frames * slabs * rows * cols)
    inv_root = 1.0 / math.sqrt(channels)
    latents = latents.reshape(rows, cols, channels)
    history, mixed, flag_tile = convolve_frames(latents, row_valid, norm_gain, conv_weight, 0)
    d_mixed, d_conv, stack = attend(
        mixed,
        cotangent.reshape(rows, cols, channels),
        flag_tile,
        attn_gain,
        w_query,
        w_key,
        w_value,
        w_out,
        (grad_scale, inv_root),
        1,
    )
    results = conv_back(
        d_conv,
        history,
        conv_weight,
        d_mixed,
        latents.reshape(rows * cols, channels),
        flag_tile,
        norm_gain,
        stack,
        grad_scale,
        2,
    )
    input_grad, conv_weight_grad, attn_weight_grad = finish(results)
    return input_grad.reshape(shape_all), conv_weight_grad, attn_weight_grad


def solution(mesh):
    return jax.shard_map(
        per_device,
        mesh=mesh,
        in_specs=(
            P("tm", "rows", None, None),
            P("rows"),
            P(),
            P("tm", None),
            P(),
            P(),
            P(),
            P(),
            P(),
            P("tm", "rows", None, None),
        ),
        out_specs=(P("tm", "rows", None, None), P(("tm", "rows"), None), P(("tm", "rows"), None)),
        check_vma=False,
    )
```

```python
import functools
import math

import jax
import jax.numpy as jnp
from jax import lax
from jax.experimental import pallas as pl
from jax.experimental.pallas import tpu as pltpu
from jax.sharding import PartitionSpec as P

epsilon = 1e-06
MESH = pl.DeviceIdType.MESH
ANY = pl.BlockSpec(memory_space=pl.ANY)
IN_VMEM = pl.BlockSpec(memory_space=pltpu.VMEM)
FLAG_ROWS = 16


def contract_last(first_op, second_op):
    return lax.dot_general(
        first_op, second_op, (((1,), (1,)), ((), ())), preferred_element_type=jnp.float32
    )


def contract_first(first_op, second_op):
    return lax.dot_general(
        first_op, second_op, (((0,), (0,)), ((), ())), preferred_element_type=jnp.float32
    )


def dot(first_op, second_op):
    return jnp.dot(first_op, second_op, preferred_element_type=jnp.float32)


def silu_slope(inputs):
    logistic = jax.nn.sigmoid(inputs)
    return logistic * (1.0 + inputs * (1.0 - logistic))


def params(collective_id, mebibytes=40):
    return pltpu.CompilerParams(
        collective_id=collective_id,
        has_side_effects=True,
        vmem_limit_bytes=mebibytes * 1024 * 1024,
    )


def signal(barrier, tm_at, row_at):
    pl.semaphore_signal(barrier, inc=1, device_id=(tm_at, row_at), device_id_type=MESH)


def remote(src, dst, send_sem, recv_sem, tm_at, row_at):
    return pltpu.make_async_remote_copy(
        src_ref=src,
        dst_ref=dst,
        send_sem=send_sem,
        recv_sem=recv_sem,
        device_id=(tm_at, row_at),
        device_id_type=MESH,
    )


def flipped(index, count, d):
    total, bit = index, 1
    while bit < count:
        flip = lax.rem(lax.div(jnp.int32(d), bit), 2)
        total = total + flip * bit * (1 - 2 * lax.rem(lax.div(index, bit), 2))
        bit *= 2
    return total


def bits_of(frames):
    return [1 << i for i in range(frames.bit_length() - 1)]


def orders_of(frames):
    bits = bits_of(frames)
    return [bits, bits[::-1]]


def levels_of(frames):
    depth = frames.bit_length() - 1
    return [[m for m in range(frames) if bin(m).count("1") == i] for i in range(depth + 1)]


def greet(barrier, t, r, frames, slabs, frame_at, steps):
    for b in bits_of(frames):
        signal(barrier, frame_at[b], r)
    count = len(bits_of(frames))
    for step in steps:
        ahead, behind = r + step < slabs, r - step >= 0

        @pl.when(ahead)
        def _():
            signal(barrier, t, r + step)

        @pl.when(behind)
        def _():
            signal(barrier, t, r - step)

        count = count + ahead.astype(jnp.int32) + behind.astype(jnp.int32)
    return count


class FrameGather:
    def __init__(self, frames, slabs, slots, sems, halo_sems, rows, t, r, frame_at):
        self.orders, self.slots, self.sems, self.halo_sems = orders_of(frames), slots, sems, halo_sems
        self.frames, self.rows, self.t, self.r, self.frame_at = frames, rows, t, r, frame_at
        self.has_above, self.has_below = r > 0, r < slabs - 1

    def piece(self, part, inner):
        half = self.rows // 2
        if not inner:
            return pl.ds(1 if part == 0 else self.rows, 1)
        return pl.ds(2 if part == 0 else half + 1, half - 1)

    def later(self, part, m):
        order = self.orders[part]
        last = max([i for i, b in enumerate(order) if m & b], default=-1)
        return order[last + 1 :]

    def copy(self, part, inner, m, b):
        rows = self.slots.at[self.frame_at[m], self.piece(part, inner)]
        at = part, inner, m | b
        return remote(
            rows, rows, self.sems.at[(0,) + at], self.sems.at[(1,) + at], self.frame_at[b], self.r
        )

    def arrived(self, part, inner, m):
        b = max(self.orders[part].index(b) for b in self.orders[part] if m & b)
        b = self.orders[part][b]
        return self.copy(part, inner, m - b, b)

    def send(self, part, inner, m):
        for b in self.later(part, m):
            self.copy(part, inner, m, b).start()

    def halo(self, m, i):
        slot = flipped(self.t, self.frames, m)
        return remote(
            self.slots.at[slot, 1 if i == 0 else self.rows],
            self.slots.at[slot, self.rows + 1 if i == 0 else 0],
            self.halo_sems.at[0, m, i],
            self.halo_sems.at[1, m, i],
            self.t,
            self.r - 1 if i == 0 else self.r + 1,
        )

    def send_halo(self, m, i):
        @pl.when(self.has_above if i == 0 else self.has_below)
        def _():
            self.halo(m, i).start()

    def start(self):
        for inner in range(2):
            for i in range(len(self.orders[0])):
                for part in range(2):
                    self.copy(part, inner, 0, self.orders[part][i]).start()
            if inner == 0:
                self.send_halo(0, 0)
                self.send_halo(0, 1)

    def edges(self, frames):
        for m in frames:
            for part in range(2):
                self.arrived(part, 0, m).wait_recv()
                self.send(part, 0, m)
                self.send_halo(m, part)

    def inners(self, frames):
        for m in frames:
            for part in range(2):
                self.arrived(part, 1, m).wait_recv()
                self.send(part, 1, m)

    def wait_halos(self, m):
        @pl.when(self.has_below)
        def _():
            self.halo(m, 0).wait_recv()

        @pl.when(self.has_above)
        def _():
            self.halo(m, 1).wait_recv()

    def run(self, stage):
        levels = levels_of(self.frames)
        before = [[] for _ in range(self.frames)]
        turn = [m for level in levels for m in level]
        before[0].append((self.edges, levels[1]))
        before[1].append((self.inners, levels[1]))
        place = 1
        for i in range(1, len(levels) - 1):
            before[place + 1].append((self.edges, levels[i + 1]))
            place += len(levels[i])
            before[place].append((self.inners, levels[i + 1]))

        def one(k, carry):
            m = 0
            for i in range(self.frames):
                chosen = (k == i).astype(jnp.int32)
                m = m + chosen * turn[i]
                if before[i]:

                    @pl.when(k == i)
                    def _():
                        for action, group in before[i]:
                            action(group)

            stage(m)
            return carry

        lax.fori_loop(0, self.frames, one, 0)

    def close(self):
        for m in range(self.frames):
            for part in range(2):
                for inner in range(2):
                    for b in self.later(part, m):
                        self.copy(part, inner, m, b).wait_send()

            @pl.when(self.has_above)
            def _():
                self.halo(m, 0).wait_send()

            @pl.when(self.has_below)
            def _():
                self.halo(m, 1).wait_send()


class FrameSwap:
    def __init__(self, frames, terms, terms_in, sems, rows, r, frame_at):
        self.orders, self.terms, self.terms_in, self.sems = orders_of(frames), terms, terms_in, sems
        self.frames, self.rows, self.r, self.frame_at = frames, rows, r, frame_at

    def part(self, i):
        half = self.rows // 2
        return pl.ds(i * half, half)

    def first(self, i, d):
        return next((n for n, b in enumerate(self.orders[i]) if d & b), len(self.orders[i]))

    def copy(self, i, d):
        return remote(
            self.terms.at[d, self.part(i)],
            self.terms_in.at[d, self.part(i)],
            self.sems.at[0, i, d],
            self.sems.at[1, i, d],
            self.frame_at[self.orders[i][self.first(i, d)]],
            self.r,
        )

    def computed(self, d):
        for i in range(2):
            if self.first(i, d) == 0:
                self.copy(i, d).start()

    def run(self, term, own):
        turn = [d for level in levels_of(self.frames)[::-1] for d in level]

        def one(k, carry):
            d = 0
            for i in range(self.frames):
                d = d + (k == i).astype(jnp.int32) * turn[i]
            block = term(d)

            @pl.when(k < self.frames - 1)
            def _():
                self.terms[d] = block.astype(self.terms.dtype)

            @pl.when(k == self.frames - 1)
            def _():
                own[...] = block

            for i in range(self.frames - 1):

                @pl.when(k == i)
                def _():
                    self.computed(turn[i])

            return carry

        return lambda start, stop: lax.fori_loop(start, stop, one, 0)

    def received(self, i, d):
        return [d | b for b in self.orders[i][: self.first(i, d)]]

    def pass_on(self):
        for n in range(1, len(self.orders[0])):
            for d in range(self.frames - 1, 0, -1):
                for i in range(2):
                    if self.first(i, d) == n:
                        part = self.part(i)
                        total = self.terms[d, part].astype(jnp.float32)
                        for e in self.received(i, d):
                            self.copy(i, e).wait_recv()
                            total = total + self.terms_in[e, part].astype(jnp.float32)
                        self.terms[d, part] = total.astype(self.terms.dtype)
                        self.copy(i, d).start()

    def add_to(self, total):
        for i in range(2):
            part = self.part(i)
            for e in self.received(i, 0):
                self.copy(i, e).wait_recv()
                total[part] = total[part] + self.terms_in[e, part].astype(jnp.float32)

    def close(self):
        for d in range(1, self.frames):
            for i in range(2):
                self.copy(i, d).wait_send()


def relay_line(pairs, q, far, ready, arrive, halves):
    low = (q < (pairs + 1) // 2).astype(jnp.int32)
    hops = pairs - 1 - 2 * q
    shift = 2 * hops * (2 * low - 1)

    def item(k, side, there):
        i = lax.div(k, 2)
        has_up = jnp.where(side == 0, q > 0, q < pairs - 1)
        count = jnp.where(side == 0, pairs - 1 - q, q)
        d = jnp.where(side == 0, pairs - 1 - i, i)
        for half in range(2):
            start, length = halves[half]
            part = pl.ds(start, length)
            wanted = jnp.logical_and(lax.rem(k, 2) == half, jnp.logical_and(there, i < count))

            @pl.when(jnp.logical_and(has_up, wanted))
            def _():
                far(d, side, half).wait_recv()
                ready[d, part] = (
                    ready[d, part].astype(jnp.float32) + arrive[side, d, part].astype(jnp.float32)
                ).astype(jnp.bfloat16)
                far(d, side, half).start()

    def slot(k, carry):
        item(jnp.maximum(k - shift, 0), low, k >= shift)
        item(k, 1 - low, True)
        return carry

    lax.fori_loop(0, 2 * (pairs - 1), slot, 0)


def padded_taps(own_rows, frames, channels):
    return max(-(-((i * own_rows) % channels + own_rows) // channels) for i in range(frames))


def conv_kernel(frames, slabs, *refs):
    (latents, row_valid, gain, weight_hbm) = refs[:4]
    (history, mixed, flag_tile) = refs[4:7]
    (shifted, weight, terms, terms_in, total) = refs[7:12]
    (load_sem, gather_sems, halo_sems, term_sems) = refs[12:]
    rows, cols, channels = latents.shape
    size = rows * cols
    narrow = shifted.shape[3]
    own_rows = weight_hbm.shape[0]
    tap_total = own_rows * frames // channels
    t, r = lax.axis_index("tm"), lax.axis_index("rows")
    frame_at = [flipped(t, frames, d) for d in range(frames)]
    first_tap = lax.div(t * own_rows, channels)
    weight_from = pl.multiple_of(t * own_rows - first_tap * channels, 16)
    tap_count = weight.shape[0] // channels

    barrier = pltpu.get_barrier_semaphore()
    greeted = greet(barrier, t, r, frames, slabs, frame_at, [1])
    flag_tile[...] = jnp.zeros_like(flag_tile)
    for h in range(rows):
        flag = row_valid[h].astype(jnp.float32)
        part = latents[h].astype(jnp.float32)
        scale = lax.rsqrt(jnp.mean(part * part, axis=1, keepdims=True) + epsilon)
        part = jax.nn.silu(part * scale * gain[...]) * flag
        history[t, h + 1] = part.astype(jnp.bfloat16)

    @pl.when(r == 0)
    def _():
        for f in range(frames):
            history[f, 0] = jnp.zeros((cols, channels), history.dtype)

    @pl.when(r == slabs - 1)
    def _():
        for f in range(frames):
            history[f, rows + 1] = jnp.zeros((cols, channels), history.dtype)

    pl.semaphore_wait(barrier, greeted)
    gather = FrameGather(
        frames, slabs, history, gather_sems, halo_sems, rows, t, r, frame_at
    )
    swap = FrameSwap(frames, terms, terms_in, term_sems, rows, r, frame_at)
    gather.start()
    for h in range(rows):
        flag = row_valid[h].astype(jnp.float32)
        flag_tile[h : h + 1, :] = jnp.full((1, flag_tile.shape[1]), flag, flag_tile.dtype)
    weight[...] = jnp.zeros_like(weight)
    load = pltpu.make_async_copy(weight_hbm, weight.at[pl.ds(weight_from, own_rows)], load_sem)
    load.start()
    for dw in range(3):
        for f in range(2):
            shifted[dw, f] = jnp.zeros(shifted.shape[2:], shifted.dtype)
    spare = jnp.zeros((narrow - cols, channels), jnp.float32)

    def stage(d):
        f = flipped(t, frames, d)
        gather.wait_halos(d)

        def widen(h, carry):
            line = jnp.concatenate([history[f, h].astype(jnp.float32), spare], axis=0)
            shifted[0, f + 2, h] = pltpu.roll(line, 1, 0).astype(jnp.bfloat16)
            shifted[1, f + 2, h] = line.astype(jnp.bfloat16)
            shifted[2, f + 2, h] = pltpu.roll(line, narrow - 1, 0).astype(jnp.bfloat16)
            return carry

        lax.fori_loop(0, rows + 2, widen, 0)

    gather.run(stage)
    load.wait()

    def convolve(f):
        total = None
        for j in range(tap_count):
            k = jnp.minimum(first_tap + j, tap_total - 1)
            dt, dh, dw = lax.div(k, 9), lax.rem(lax.div(k, 3), 3), lax.rem(k, 3)
            window = shifted[dw, f + dt, pl.ds(dh, rows)].reshape(rows * narrow, channels)
            term = dot(window, weight[j * channels : (j + 1) * channels, :])
            total = term if total is None else total + term
        return total.reshape(rows, narrow, channels)[:, :cols]

    swap.run(lambda d: convolve(flipped(t, frames, d)), total)(0, frames)
    total[...] += latents[...].astype(jnp.float32)
    swap.pass_on()
    swap.add_to(total)
    mixed[...] = total[...].reshape(size, channels).astype(mixed.dtype)
    gather.close()
    swap.close()


def convolve_frames(latents, row_valid, gain, conv_weight, collective_id):
    frames, slabs = lax.axis_size("tm"), lax.axis_size("rows")
    rows, cols, channels = latents.shape
    bf16, f32 = jnp.bfloat16, jnp.float32
    narrow = -(-cols // 16) * 16
    padded = padded_taps(conv_weight.shape[0], frames, channels) * channels
    dma = pltpu.SemaphoreType.DMA
    return pl.pallas_call(
        functools.partial(conv_kernel, frames, slabs),
        out_shape=[
            jax.ShapeDtypeStruct((frames, rows + 2, cols, channels), bf16),
            jax.ShapeDtypeStruct((rows * cols, channels), bf16),
            jax.ShapeDtypeStruct((FLAG_ROWS, 128), bf16),
        ],
        in_specs=[IN_VMEM, pl.BlockSpec(memory_space=pltpu.SMEM), IN_VMEM, ANY],
        out_specs=[IN_VMEM] * 3,
        scratch_shapes=[
            pltpu.VMEM((3, frames + 2, rows + 2, narrow, channels), bf16),
            pltpu.VMEM((padded, channels), bf16),
            pltpu.VMEM((frames, rows, cols, channels), bf16),
            pltpu.VMEM((frames, rows, cols, channels), bf16),
            pltpu.VMEM((rows, cols, channels), f32),
            dma,
            dma((2, 2, 2, frames)),
            dma((2, frames, 2)),
            dma((2, 2, frames)),
        ],
        compiler_params=params(collective_id, 62),
    )(latents, row_valid, gain, conv_weight)


def halves_of(size):
    near = size // 2 // 16 * 16
    return ((0, near), (near, size - near))


def attention_kernel(frames, slabs, grad_scale, inv_root, *refs):
    (mixed, cotangent, flag_tile, gain) = refs[:4]
    projections = refs[4:8]
    (d_mixed_out, d_conv_out, stack_out) = refs[8:11]
    (cells, cells_t, prob, d_weights, tops, sums, dots) = refs[11:18]
    (mine, near, ready, arrive, own_total, weighted_t, d_cells_t) = refs[18:25]
    (queries, key_side, value_side, d_attended, grad_out) = refs[25:30]
    (grads, grads_in, stack) = refs[30:33]
    (w_query, w_key, w_value, w_out) = refs[33:37]
    (load_sems, sib_sems, hop_sems, hand_sems, near_sems, far_send, far_recv, grad_sems) = refs[37:]
    pairs = slabs // 2
    rows, cols, channels = cotangent.shape
    size = rows * cols
    halves = halves_of(size)
    t, r = lax.axis_index("tm"), lax.axis_index("rows")
    q, c = lax.div(r, 2), lax.rem(r, 2)
    other = 1 - c
    sibling = 2 * q + other
    frame_at = [flipped(t, frames, d) for d in range(frames)]
    loads = [
        pltpu.make_async_copy(source, target, load_sems.at[i])
        for i, (source, target) in enumerate(
            zip(projections, (w_query, w_key, w_value, w_out))
        )
    ]
    for copy in loads:
        copy.start()
    barrier = pltpu.get_barrier_semaphore()
    for b in bits_of(frames):
        signal(barrier, frame_at[b], r)
    has_left, has_right = q > 0, q < pairs - 1
    signal(barrier, t, sibling)

    @pl.when(has_left)
    def _():
        signal(barrier, t, r - 2)

    @pl.when(has_right)
    def _():
        signal(barrier, t, r + 2)

    mixed_f = mixed[...].astype(jnp.float32)
    second_scale = lax.rsqrt(jnp.mean(mixed_f * mixed_f, axis=1, keepdims=True) + epsilon)
    attn_in = (mixed_f * second_scale * gain[...]).astype(jnp.bfloat16)
    cells[r, :size] = attn_in
    for i in range(channels // 128):
        cells[r, size:, i * 128 : (i + 1) * 128] = flag_tile[...]
    sides = has_left.astype(jnp.int32) + has_right.astype(jnp.int32)
    pl.semaphore_wait(barrier, 1 + len(bits_of(frames)) + sides)
    cuts = (halves[0], (halves[1][0], halves[1][1] + FLAG_ROWS))

    def sources(step, side):
        return q - step if side == 0 else q + step

    def arrives(step, side):
        at = sources(step, side)
        return jnp.logical_and(step < pairs, jnp.logical_and(at >= 0, at < pairs))

    def onward(step, side):
        ahead = q < pairs - 1 if side == 0 else q > 0
        return jnp.logical_and(ahead, arrives(step, side))

    def hop(step, side, half):
        start, count = cuts[half]
        part = cells.at[2 * sources(step - 1, side) + c, pl.ds(start, count)]
        target = r + 2 if side == 0 else r - 2
        return remote(
            part, part, hop_sems.at[0, side, step, half], hop_sems.at[1, side, step, half], t, target
        )

    def hand(step, side):
        part = cells.at[2 * sources(step, side) + c]
        return remote(
            part, part, hand_sems.at[0, side, step], hand_sems.at[1, side, step], t, sibling
        )

    to_sibling = remote(cells.at[r], cells.at[r], sib_sems.at[0], sib_sems.at[1], t, sibling)
    for half in range(2):
        for side in range(2):

            @pl.when(onward(0, side))
            def _():
                hop(1, side, half).start()

    to_sibling.start()

    for h in range(rows):
        flag = flag_tile[h : h + 1, 0:1].astype(jnp.float32)
        part = cotangent[h].astype(jnp.float32)
        grad_out[h * cols : (h + 1) * cols, :] = jnp.where(flag > 0, part, 0.0).astype(jnp.bfloat16)
    for copy in loads:
        copy.wait()
    queries[...] = dot(attn_in, w_query[...]).astype(jnp.bfloat16)
    key_side[...] = contract_last(queries[...], w_key[...]).astype(jnp.bfloat16)
    d_attended[...] = contract_last(grad_out[...], w_out[...]).astype(jnp.bfloat16)
    value_side[...] = contract_last(d_attended[...], w_value[...]).astype(jnp.bfloat16)

    lowest = float(jnp.finfo(jnp.float32).min)

    def absorb(j):
        block = cells[j, :size]
        flags = cells[j, size:, :128].astype(jnp.float32)
        scores = contract_last(block, key_side[...]) * inv_root
        kept = []
        for h in range(rows):
            flag = flags[h : h + 1, 0:1]
            kept.append(jnp.where(flag > 0, scores[h * cols : (h + 1) * cols], lowest))
        scores = jnp.concatenate(kept, axis=0)
        top = jnp.max(scores, axis=0, keepdims=True)
        exponent = jnp.exp(scores - top)
        prob[j] = exponent
        d_weight = contract_last(block, value_side[...])
        d_weights[j] = d_weight
        tops[j] = top
        sums[j] = jnp.sum(exponent, axis=0, keepdims=True)
        dots[j] = jnp.sum(exponent * d_weight, axis=0, keepdims=True)
        cells_t[j] = block.T

    def pass_on(step, half):
        for side in range(2):

            @pl.when(arrives(step, side))
            def _():
                hop(step, side, half).wait_recv()

            @pl.when(onward(step, side))
            def _():
                hop(step + 1, side, half).start()

            if half == 1:

                @pl.when(arrives(step, side))
                def _():
                    hand(step, side).start()

    def own_pair(i, carry):
        @pl.when(i == 1)
        def _():
            to_sibling.wait_recv()

        absorb(2 * q + c + i * (other - c))
        return carry

    lax.fori_loop(0, 2, own_pair, 0)
    pass_on(1, 0)
    pass_on(1, 1)

    def two_slabs(k, carry):
        step, side = 1 + lax.div(k, 2), lax.rem(k, 2)
        at = q - step + 2 * step * side
        there = jnp.logical_and(at >= 0, at < pairs)

        def one(i, carry):
            for s in range(2):

                @pl.when(jnp.logical_and(i == 1, side == s))
                def _():
                    hand(step, s).wait_recv()

            absorb(2 * at + c + i * (other - c))
            return carry

        @pl.when(there)
        def _():
            lax.fori_loop(0, 2, one, 0)

        for half in range(2):

            @pl.when(jnp.logical_and(side == half, step < pairs - 1))
            def _():
                pass_on(step + 1, half)

        return carry

    lax.fori_loop(0, 2 * (pairs - 1), two_slabs, 0)

    top_all = tops[0]
    for j in range(1, slabs):
        top_all = jnp.maximum(top_all, tops[j])
    total_sum = jnp.zeros_like(top_all)
    total_dot = jnp.zeros_like(top_all)
    for j in range(slabs):
        rescale = jnp.exp(tops[j] - top_all)
        total_sum = total_sum + rescale * sums[j]
        total_dot = total_dot + rescale * dots[j]
        tops[j] = rescale
    inverse = 1.0 / total_sum
    row_delta = total_dot * inverse
    weighted_t[...] = jnp.zeros_like(weighted_t)
    d_cells_t[...] = jnp.zeros_like(d_cells_t)

    def emit(j):
        weights = prob[j] * (tops[j] * inverse)
        weights_b = weights.astype(jnp.bfloat16)
        d_scores = (weights * (d_weights[j] - row_delta) * inv_root).astype(jnp.bfloat16)
        block_t = cells_t[j]
        weighted_t[...] += dot(block_t, weights_b)
        d_cells_t[...] += dot(block_t, d_scores)
        return dot(d_scores, key_side[...]) + dot(weights_b, value_side[...])

    def give(d):
        part = mine.at[d]
        return remote(part, near.at[d], near_sems.at[0, d], near_sems.at[1, d], t, sibling)

    def far(d, side, half):
        start, count = halves[half]
        target = r + 2 - 4 * side
        return remote(
            ready.at[d, pl.ds(start, count)],
            arrive.at[side, d, pl.ds(start, count)],
            far_send.at[d, half],
            far_recv.at[side, d, half],
            t,
            target,
        )

    low_half = (q < (pairs + 1) // 2).astype(jnp.int32)
    right_count = pairs - 1 - q

    def chip_order(i):
        from_right = pairs - 1 - i
        low_order = jnp.where(i < right_count, from_right, i - right_count)
        high_order = jnp.where(i < q, i, pairs - 1 - (i - q))
        order = low_half * low_order + (1 - low_half) * high_order
        return jnp.where(i == pairs - 1, q, order)

    def one_chip(i, carry):
        d = chip_order(i)
        mine[d] = emit(2 * d + other).astype(jnp.bfloat16)
        give(d).start()
        term = emit(2 * d + c)
        give(d).wait_recv()
        term = term + near[d].astype(jnp.float32)

        @pl.when(i == pairs - 1)
        def _():
            own_total[...] = term

        @pl.when(i < pairs - 1)
        def _():
            ready[d] = term.astype(jnp.bfloat16)

        @pl.when(jnp.logical_and(q == 0, d > q))
        def _():
            far(d, 0, 0).start()
            far(d, 0, 1).start()

        @pl.when(jnp.logical_and(q == pairs - 1, d < q))
        def _():
            far(d, 1, 0).start()
            far(d, 1, 1).start()

        return carry

    lax.fori_loop(0, pairs, one_chip, 0)

    weighted_b = weighted_t[...].astype(jnp.bfloat16)
    d_cells_b = d_cells_t[...].astype(jnp.bfloat16)
    attended = contract_first(weighted_b, w_value[...]).astype(jnp.bfloat16)
    d_query = contract_first(d_cells_b, w_key[...]).astype(jnp.bfloat16)
    blocks = [
        contract_first(cells[r, :size], d_query),
        dot(d_cells_b, queries[...]),
        dot(weighted_b, d_attended[...]),
        contract_first(attended, grad_out[...]),
    ]
    share = 4 * channels // frames
    swap = FrameSwap(frames, grads, grads_in, grad_sems, share, r, frame_at)
    for g in range(frames):
        i, start = divmod(g * share, channels)
        part = blocks[i][start : start + share] * grad_scale
        grads[flipped(t, frames, g)] = part.astype(jnp.bfloat16)
    for d in range(frames - 1, 0, -1):
        swap.computed(d)
    own_total[...] += contract_last(d_query, w_query[...])

    relay_line(pairs, q, far, ready, arrive, halves)

    swap.pass_on()
    for side in range(2):

        @pl.when(q > 0 if side == 0 else q < pairs - 1)
        def _():
            for half in range(2):
                start, length = halves[half]
                far(q, side, half).wait_recv()
                part = pl.ds(start, length)
                own_total[part, :] += arrive[side, q, part].astype(jnp.float32)

    mixed_f = mixed[...].astype(jnp.float32)
    second_scale = lax.rsqrt(jnp.mean(mixed_f * mixed_f, axis=1, keepdims=True) + epsilon)
    normed_two = mixed_f * second_scale
    scaled_two = gain[...] * own_total[...]
    d_mixed = grad_out[...].astype(jnp.float32) + second_scale * (
        scaled_two - normed_two * jnp.mean(scaled_two * normed_two, axis=1, keepdims=True)
    )
    d_mixed_out[...] = d_mixed
    d_conv_out[...] = d_mixed.astype(jnp.bfloat16).reshape(rows, cols, channels)
    stack[...] = grads[0].astype(jnp.float32)
    swap.add_to(stack)
    stack_out[...] = stack[...].astype(stack_out.dtype)

    to_sibling.wait_send()
    for side in range(2):
        for step in range(1, pairs):

            @pl.when(onward(step - 1, side))
            def _():
                for half in range(2):
                    hop(step, side, half).wait_send()

            @pl.when(arrives(step, side))
            def _():
                hand(step, side).wait_send()

    for d in range(pairs):
        give(d).wait_send()

        @pl.when(q != d)
        def _():
            for half in range(2):
                far(d, 0, half).wait_send()

    swap.close()


def attend(mixed, cotangent, flag_tile, gain, w_query, w_key, w_value, w_out, scales, collective_id):
    frames, slabs = lax.axis_size("tm"), lax.axis_size("rows")
    pairs = slabs // 2
    rows, cols, channels = cotangent.shape
    size = rows * cols
    bf16, f32 = jnp.bfloat16, jnp.float32
    share = 4 * channels // frames
    dma = pltpu.SemaphoreType.DMA
    return pl.pallas_call(
        functools.partial(attention_kernel, frames, slabs, *scales),
        out_shape=[
            jax.ShapeDtypeStruct((size, channels), f32),
            jax.ShapeDtypeStruct((rows, cols, channels), bf16),
            jax.ShapeDtypeStruct((share, channels), bf16),
        ],
        in_specs=[IN_VMEM] * 4 + [ANY] * 4,
        out_specs=[IN_VMEM] * 3,
        scratch_shapes=[
            pltpu.VMEM((slabs, size + FLAG_ROWS, channels), bf16),
            pltpu.VMEM((slabs, channels, size), bf16),
            pltpu.VMEM((slabs, size, size), f32),
            pltpu.VMEM((slabs, size, size), f32),
            pltpu.VMEM((slabs, 1, size), f32),
            pltpu.VMEM((slabs, 1, size), f32),
            pltpu.VMEM((slabs, 1, size), f32),
            pltpu.VMEM((pairs, size, channels), bf16),
            pltpu.VMEM((pairs, size, channels), bf16),
            pltpu.VMEM((pairs, size, channels), bf16),
            pltpu.VMEM((2, pairs, size, channels), bf16),
            pltpu.VMEM((size, channels), f32),
            pltpu.VMEM((channels, size), f32),
            pltpu.VMEM((channels, size), f32),
            pltpu.VMEM((size, channels), bf16),
            pltpu.VMEM((size, channels), bf16),
            pltpu.VMEM((size, channels), bf16),
            pltpu.VMEM((size, channels), bf16),
            pltpu.VMEM((size, channels), bf16),
            pltpu.VMEM((frames, share, channels), bf16),
            pltpu.VMEM((frames, share, channels), bf16),
            pltpu.VMEM((share, channels), f32),
            pltpu.VMEM((channels, channels), bf16),
            pltpu.VMEM((channels, channels), bf16),
            pltpu.VMEM((channels, channels), bf16),
            pltpu.VMEM((channels, channels), bf16),
            dma((4,)),
            dma((2,)),
            dma((2, 2, pairs + 1, 2)),
            dma((2, 2, pairs)),
            dma((2, pairs)),
            dma((pairs, 2)),
            dma((2, pairs, 2)),
            dma((2, 2, frames)),
        ],
        compiler_params=params(collective_id, 62),
    )(mixed, cotangent, flag_tile, gain, w_query, w_key, w_value, w_out)


def window_rows(count, step):
    return -(-(count + 16 - math.gcd(step, 16)) // 16) * 16


def conv_back_kernel(frames, slabs, grad_scale, *refs):
    (d_conv, history_hbm, weight_hbm, d_mixed_hbm, latents_hbm, flag_tile, gain, stack) = refs[:8]
    (grad_out, conv_out, attn_out) = refs[8:11]
    (spread, shifted, history, history_t, weight, weight_acc) = refs[11:17]
    (normed, first_scale, slope) = refs[17:20]
    (mine, near, ready, arrive, own_total) = refs[20:25]
    (terms, terms_in, own_term, stack_in, d_mixed, latents) = refs[25:31]
    (load_sems, gather_sems, halo_sems, stack_sems) = refs[31:35]
    (near_sems, far_send, far_recv, term_sems) = refs[35:]
    pairs = slabs // 2
    rows, cols, channels = d_conv.shape
    size = rows * cols
    wide = shifted.shape[3]
    narrow = -(-cols // 16) * 16
    own_rows = weight_hbm.shape[0]
    tap_total = own_rows * frames // channels
    block_rows = own_rows // slabs
    span = mine.shape[1]
    halves = halves_of(span)
    t, r = lax.axis_index("tm"), lax.axis_index("rows")
    q, c = lax.div(r, 2), lax.rem(r, 2)
    other = 1 - c
    sibling = 2 * q + other
    frame_at = [flipped(t, frames, d) for d in range(frames)]
    slab_at = [lax.rem(r + d, slabs) for d in range(slabs)]
    first_tap = lax.div(t * own_rows, channels)
    weight_from = pl.multiple_of(t * own_rows - first_tap * channels, 16)
    tap_count = weight.shape[0] // channels

    def tap_at(j):
        k = jnp.minimum(first_tap + j, tap_total - 1)
        return lax.div(k, 9), lax.rem(lax.div(k, 3), 3), lax.rem(k, 3)

    weight[...] = jnp.zeros_like(weight)
    loads = [
        pltpu.make_async_copy(history_hbm, history, load_sems.at[0]),
        pltpu.make_async_copy(d_mixed_hbm, d_mixed, load_sems.at[2]),
        pltpu.make_async_copy(latents_hbm, latents, load_sems.at[3]),
        pltpu.make_async_copy(
            weight_hbm, weight.at[pl.ds(weight_from, own_rows)], load_sems.at[1]
        ),
    ]
    for copy in loads:
        copy.start()
    barrier = pltpu.get_barrier_semaphore()
    for d in range(1, slabs):
        signal(barrier, t, slab_at[d])
    for b in bits_of(frames):
        signal(barrier, frame_at[b], r)
    for h in range(rows):
        spread[t, h + 1] = d_conv[h]

    @pl.when(r == 0)
    def _():
        for f in range(frames):
            spread[f, 0] = jnp.zeros((cols, channels), spread.dtype)

    @pl.when(r == slabs - 1)
    def _():
        for f in range(frames):
            spread[f, rows + 1] = jnp.zeros((cols, channels), spread.dtype)

    pl.semaphore_wait(barrier, slabs - 1 + len(bits_of(frames)))
    gather = FrameGather(
        frames, slabs, spread, gather_sems, halo_sems, rows, t, r, frame_at
    )
    swap = FrameSwap(frames, terms, terms_in, term_sems, rows, r, frame_at)
    gather.start()
    share = stack_in.shape[1]
    stack_step = attn_out.shape[0]

    def stack_low(at):
        return pl.multiple_of(lax.div(at * stack_step, 16) * 16, 16)

    stack_copies = [
        remote(
            stack.at[pl.ds(stack_low(slab_at[d]), share)],
            stack_in.at[d],
            stack_sems.at[0, d],
            stack_sems.at[1, d],
            t,
            slab_at[d],
        )
        for d in range(1, slabs)
    ]
    for copy in stack_copies:
        copy.start()

    weight_acc[...] = jnp.zeros_like(weight_acc)
    history_t[0] = jnp.zeros(history_t.shape[1:], history_t.dtype)
    history_t[1] = jnp.zeros(history_t.shape[1:], history_t.dtype)
    for dw in range(3):
        for f in range(2):
            shifted[dw, frames + f] = jnp.zeros(shifted.shape[2:], shifted.dtype)
    for copy in loads:
        copy.wait()
    spare = jnp.zeros((wide - cols, channels), jnp.float32)

    def turn(f, carry):
        for h in range(rows + 2):
            line = jnp.concatenate([history[f, h].astype(jnp.float32), spare], axis=0)
            history_t[f + 2, :, h * wide : (h + 1) * wide] = line.astype(jnp.bfloat16).T
        return carry

    lax.fori_loop(0, frames, turn, 0)
    inputs = latents[...].astype(jnp.float32)
    scale_one = lax.rsqrt(jnp.mean(inputs * inputs, axis=1, keepdims=True) + epsilon)
    normed_one = inputs * scale_one
    first_scale[...] = scale_one
    normed[...] = normed_one
    factor = gain[...] * silu_slope(normed_one * gain[...])
    for h in range(rows):
        flag = flag_tile[h : h + 1, 0:1].astype(jnp.float32)
        part = factor[h * cols : (h + 1) * cols]
        slope[h * cols : (h + 1) * cols, :] = jnp.where(flag > 0, part, 0.0)

    def stage(d):
        f = flipped(t, frames, d)
        gather.wait_halos(d)

        def widen(h, carry):
            line = jnp.concatenate([spread[f, h].astype(jnp.float32), spare], axis=0)
            shifted[0, f, h] = pltpu.roll(line, wide - 1, 0).astype(jnp.bfloat16)
            shifted[1, f, h] = line.astype(jnp.bfloat16)
            shifted[2, f, h] = pltpu.roll(line, 1, 0).astype(jnp.bfloat16)
            return carry

        lax.fori_loop(0, rows + 2, widen, 0)

        for j in range(tap_count):
            dt, dh, dw = tap_at(j)
            lanes = pl.ds(pl.multiple_of(dh * wide, wide), rows * wide)
            ahead = shifted[dw, f, 1 : rows + 1].reshape(rows * wide, channels)
            weight_acc[j * channels : (j + 1) * channels, :] += dot(
                history_t[f + dt, :, lanes], ahead
            )

    gather.run(stage)

    def low_row(block):
        return pl.multiple_of(lax.div(weight_from + block * block_rows, 16) * 16, 16)

    def weight_block(block):
        return weight_acc[pl.ds(low_row(block), span), :] * grad_scale

    def give(d):
        part = mine.at[d]
        return remote(part, near.at[d], near_sems.at[0, d], near_sems.at[1, d], t, sibling)

    def far(d, side, half):
        start, count = halves[half]
        return remote(
            ready.at[d, pl.ds(start, count)],
            arrive.at[side, d, pl.ds(start, count)],
            far_send.at[d, half],
            far_recv.at[side, d, half],
            t,
            r + 2 - 4 * side,
        )

    low_half = (q < (pairs + 1) // 2).astype(jnp.int32)
    right_count = pairs - 1 - q

    def chip_order(i):
        low_order = jnp.where(i < right_count, pairs - 1 - i, i - right_count)
        high_order = jnp.where(i < q, i, pairs - 1 - (i - q))
        order = low_half * low_order + (1 - low_half) * high_order
        return jnp.where(i == pairs - 1, q, order)

    def one_gift(i, carry):
        d = chip_order(i)
        mine[d] = weight_block(2 * d + other).astype(jnp.bfloat16)
        give(d).start()
        return carry

    def one_chip(i, carry):
        d = chip_order(i)
        term = weight_block(2 * d + c)
        give(d).wait_recv()
        term = term + near[d].astype(jnp.float32)

        @pl.when(i == pairs - 1)
        def _():
            own_total[...] = term

        @pl.when(i < pairs - 1)
        def _():
            ready[d] = term.astype(jnp.bfloat16)

        @pl.when(jnp.logical_and(q == 0, d > q))
        def _():
            far(d, 0, 0).start()
            far(d, 0, 1).start()

        @pl.when(jnp.logical_and(q == pairs - 1, d < q))
        def _():
            far(d, 1, 0).start()
            far(d, 1, 1).start()

        return carry

    lax.fori_loop(0, pairs, one_gift, 0)
    lax.fori_loop(0, pairs, one_chip, 0)

    def back(f):
        total = None
        for j in range(tap_count):
            dt, dh, dw = tap_at(j)
            ahead = shifted[dw, f + 2 - dt, pl.ds(2 - dh, rows), :narrow]
            term = contract_last(
                ahead.reshape(rows * narrow, channels),
                weight[j * channels : (j + 1) * channels, :],
            )
            total = term if total is None else total + term
        return total.reshape(rows, narrow, channels)[:, :cols]

    swap.run(lambda d: back(flipped(t, frames, d)), own_term)(0, frames)
    swap.pass_on()
    relay_line(pairs, q, far, ready, arrive, halves)

    stack_sum = stack[pl.ds(stack_low(r), share), :].astype(jnp.float32)
    for d in range(1, slabs):
        stack_copies[d - 1].wait_recv()
        stack_sum = stack_sum + stack_in[d].astype(jnp.float32)
    if share > stack_step:
        stack_sum = pltpu.roll(stack_sum, share - (r * stack_step - stack_low(r)), 0)
    attn_out[...] = stack_sum[:stack_step]

    swap.add_to(own_term)
    scaled_one = own_term[...].reshape(size, channels) * slope[...]
    normed_one = normed[...]
    input_grad = d_mixed[...] + first_scale[...] * (
        scaled_one - normed_one * jnp.mean(scaled_one * normed_one, axis=1, keepdims=True)
    )
    grad_out[...] = input_grad.reshape(rows, cols, channels).astype(grad_out.dtype)

    for side in range(2):

        @pl.when(q > 0 if side == 0 else q < pairs - 1)
        def _():
            for half in range(2):
                start, length = halves[half]
                far(q, side, half).wait_recv()
                part = pl.ds(start, length)
                own_total[part, :] += arrive[side, q, part].astype(jnp.float32)

    result = own_total[...]
    if span > block_rows:
        offset = weight_from + r * block_rows - low_row(r)
        result = pltpu.roll(result, span - offset, 0)
    conv_out[...] = result[:block_rows]

    gather.close()
    swap.close()
    for copy in stack_copies:
        copy.wait_send()
    for d in range(pairs):
        give(d).wait_send()

        @pl.when(q != d)
        def _():
            for half in range(2):
                far(d, 0, half).wait_send()


def conv_back(
    d_conv, history, conv_weight, d_mixed, latents, flag_tile, gain, stack, grad_scale, collective_id
):
    frames, slabs = lax.axis_size("tm"), lax.axis_size("rows")
    pairs = slabs // 2
    rows, cols, channels = d_conv.shape
    size = rows * cols
    bf16, f32 = jnp.bfloat16, jnp.float32
    wide = -(-cols // 128) * 128
    own_rows = conv_weight.shape[0]
    padded = padded_taps(own_rows, frames, channels) * channels
    block_rows = own_rows // slabs
    span = window_rows(block_rows, math.gcd(own_rows, block_rows))
    stack_rows = stack.shape[0] // slabs
    share = window_rows(stack_rows, stack_rows)
    if share > stack_rows:
        stack = jnp.pad(stack, ((0, 16), (0, 0)))
    dma = pltpu.SemaphoreType.DMA
    return pl.pallas_call(
        functools.partial(conv_back_kernel, frames, slabs, grad_scale),
        out_shape=[
            jax.ShapeDtypeStruct((rows, cols, channels), bf16),
            jax.ShapeDtypeStruct((block_rows, channels), f32),
            jax.ShapeDtypeStruct((stack_rows, channels), f32),
        ],
        in_specs=[IN_VMEM] + [ANY] * 4 + [IN_VMEM] * 3,
        out_specs=[IN_VMEM] * 3,
        scratch_shapes=[
            pltpu.VMEM((frames, rows + 2, cols, channels), bf16),
            pltpu.VMEM((3, frames + 2, rows + 2, wide, channels), bf16),
            pltpu.VMEM((frames, rows + 2, cols, channels), bf16),
            pltpu.VMEM((frames + 2, channels, (rows + 2) * wide), bf16),
            pltpu.VMEM((padded, channels), bf16),
            pltpu.VMEM((padded + 32, channels), f32),
            pltpu.VMEM((size, channels), f32),
            pltpu.VMEM((size, 1), f32),
            pltpu.VMEM((size, channels), f32),
            pltpu.VMEM((pairs, span, channels), bf16),
            pltpu.VMEM((pairs, span, channels), bf16),
            pltpu.VMEM((pairs, span, channels), bf16),
            pltpu.VMEM((2, pairs, span, channels), bf16),
            pltpu.VMEM((span, channels), f32),
            pltpu.VMEM((frames, rows, cols, channels), bf16),
            pltpu.VMEM((frames, rows, cols, channels), bf16),
            pltpu.VMEM((rows, cols, channels), f32),
            pltpu.VMEM((slabs, share, channels), bf16),
            pltpu.VMEM((size, channels), f32),
            pltpu.VMEM((size, channels), bf16),
            dma((4,)),
            dma((2, 2, 2, frames)),
            dma((2, frames, 2)),
            dma((2, slabs)),
            dma((2, pairs)),
            dma((pairs, 2)),
            dma((2, pairs, 2)),
            dma((2, 2, frames)),
        ],
        compiler_params=params(collective_id, 62),
    )(d_conv, history, conv_weight, d_mixed, latents, flag_tile, gain, stack)


def finish_kernel(count, *refs):
    for i in range(count):
        refs[count + i][...] = refs[i][...]


def finish(arrays):
    count = len(arrays)
    return pl.pallas_call(
        functools.partial(finish_kernel, count),
        out_shape=[jax.ShapeDtypeStruct(a.shape, a.dtype) for a in arrays],
        in_specs=[IN_VMEM] * count,
        out_specs=[IN_VMEM] * count,
    )(*arrays)


def per_device(
    latents, row_valid, norm_gain, conv_weight, attn_gain, w_query, w_key, w_value, w_out, cotangent
):
    shape_all = latents.shape
    rows, cols, channels = shape_all[1:]
    frames, slabs = lax.axis_size("tm"), lax.axis_size("rows")
    grad_scale = 1.0 / math.sqrt(frames * slabs * rows * cols)
    inv_root = 1.0 / math.sqrt(channels)
    latents = latents.reshape(rows, cols, channels)
    history, mixed, flag_tile = convolve_frames(latents, row_valid, norm_gain, conv_weight, 0)
    d_mixed, d_conv, stack = attend(
        mixed,
        cotangent.reshape(rows, cols, channels),
        flag_tile,
        attn_gain,
        w_query,
        w_key,
        w_value,
        w_out,
        (grad_scale, inv_root),
        1,
    )
    results = conv_back(
        d_conv,
        history,
        conv_weight,
        d_mixed,
        latents.reshape(rows * cols, channels),
        flag_tile,
        norm_gain,
        stack,
        grad_scale,
        2,
    )
    input_grad, conv_weight_grad, attn_weight_grad = finish(results)
    return input_grad.reshape(shape_all), conv_weight_grad, attn_weight_grad


def solution(mesh):
    return jax.shard_map(
        per_device,
        mesh=mesh,
        in_specs=(
            P("tm", "rows", None, None),
            P("rows"),
            P(),
            P("tm", None),
            P(),
            P(),
            P(),
            P(),
            P(),
            P("tm", "rows", None, None),
        ),
        out_specs=(P("tm", "rows", None, None), P(("tm", "rows"), None), P(("tm", "rows"), None)),
        check_vma=False,
    )
```

```python
import functools
import math

import jax
import jax.numpy as jnp
from jax import lax
from jax.experimental import pallas as pl
from jax.experimental.pallas import tpu as pltpu
from jax.sharding import PartitionSpec as P

epsilon = 1e-06
MESH = pl.DeviceIdType.MESH
ANY = pl.BlockSpec(memory_space=pl.ANY)
IN_VMEM = pl.BlockSpec(memory_space=pltpu.VMEM)
FLAG_ROWS = 16


def contract_last(first_op, second_op):
    return lax.dot_general(
        first_op, second_op, (((1,), (1,)), ((), ())), preferred_element_type=jnp.float32
    )


def contract_first(first_op, second_op):
    return lax.dot_general(
        first_op, second_op, (((0,), (0,)), ((), ())), preferred_element_type=jnp.float32
    )


def dot(first_op, second_op):
    return jnp.dot(first_op, second_op, preferred_element_type=jnp.float32)


def silu_slope(inputs):
    logistic = jax.nn.sigmoid(inputs)
    return logistic * (1.0 + inputs * (1.0 - logistic))


def params(collective_id, mebibytes=40):
    return pltpu.CompilerParams(
        collective_id=collective_id,
        has_side_effects=True,
        vmem_limit_bytes=mebibytes * 1024 * 1024,
    )


def signal(barrier, tm_at, row_at):
    pl.semaphore_signal(barrier, inc=1, device_id=(tm_at, row_at), device_id_type=MESH)


def remote(src, dst, send_sem, recv_sem, tm_at, row_at):
    return pltpu.make_async_remote_copy(
        src_ref=src,
        dst_ref=dst,
        send_sem=send_sem,
        recv_sem=recv_sem,
        device_id=(tm_at, row_at),
        device_id_type=MESH,
    )


def flipped(index, count, d):
    total, bit = index, 1
    while bit < count:
        flip = lax.rem(lax.div(jnp.int32(d), bit), 2)
        total = total + flip * bit * (1 - 2 * lax.rem(lax.div(index, bit), 2))
        bit *= 2
    return total


def bits_of(frames):
    return [1 << i for i in range(frames.bit_length() - 1)]


def orders_of(frames):
    bits = bits_of(frames)
    return [bits, bits[::-1]]


def levels_of(frames):
    depth = frames.bit_length() - 1
    return [[m for m in range(frames) if bin(m).count("1") == i] for i in range(depth + 1)]


def greet(barrier, t, r, frames, slabs, frame_at, steps):
    for b in bits_of(frames):
        signal(barrier, frame_at[b], r)
    count = len(bits_of(frames))
    for step in steps:
        ahead, behind = r + step < slabs, r - step >= 0

        @pl.when(ahead)
        def _():
            signal(barrier, t, r + step)

        @pl.when(behind)
        def _():
            signal(barrier, t, r - step)

        count = count + ahead.astype(jnp.int32) + behind.astype(jnp.int32)
    return count


class FrameGather:
    def __init__(self, frames, slabs, slots, sems, halo_sems, rows, t, r, frame_at):
        self.orders, self.slots, self.sems, self.halo_sems = orders_of(frames), slots, sems, halo_sems
        self.frames, self.rows, self.t, self.r, self.frame_at = frames, rows, t, r, frame_at
        self.has_above, self.has_below = r > 0, r < slabs - 1

    def piece(self, part, inner):
        half = self.rows // 2
        if not inner:
            return pl.ds(1 if part == 0 else self.rows, 1)
        return pl.ds(2 if part == 0 else half + 1, half - 1)

    def later(self, part, m):
        order = self.orders[part]
        last = max([i for i, b in enumerate(order) if m & b], default=-1)
        return order[last + 1 :]

    def copy(self, part, inner, m, b):
        rows = self.slots.at[self.frame_at[m], self.piece(part, inner)]
        at = part, inner, m | b
        return remote(
            rows, rows, self.sems.at[(0,) + at], self.sems.at[(1,) + at], self.frame_at[b], self.r
        )

    def arrived(self, part, inner, m):
        b = max(self.orders[part].index(b) for b in self.orders[part] if m & b)
        b = self.orders[part][b]
        return self.copy(part, inner, m - b, b)

    def send(self, part, inner, m):
        for b in self.later(part, m):
            self.copy(part, inner, m, b).start()

    def halo(self, m, i):
        slot = flipped(self.t, self.frames, m)
        return remote(
            self.slots.at[slot, 1 if i == 0 else self.rows],
            self.slots.at[slot, self.rows + 1 if i == 0 else 0],
            self.halo_sems.at[0, m, i],
            self.halo_sems.at[1, m, i],
            self.t,
            self.r - 1 if i == 0 else self.r + 1,
        )

    def send_halo(self, m, i):
        @pl.when(self.has_above if i == 0 else self.has_below)
        def _():
            self.halo(m, i).start()

    def start(self):
        for inner in range(2):
            for i in range(len(self.orders[0])):
                for part in range(2):
                    self.copy(part, inner, 0, self.orders[part][i]).start()
            if inner == 0:
                self.send_halo(0, 0)
                self.send_halo(0, 1)

    def edges(self, frames):
        for m in frames:
            for part in range(2):
                self.arrived(part, 0, m).wait_recv()
                self.send(part, 0, m)
                self.send_halo(m, part)

    def inners(self, frames):
        for m in frames:
            for part in range(2):
                self.arrived(part, 1, m).wait_recv()
                self.send(part, 1, m)

    def wait_halos(self, m):
        @pl.when(self.has_below)
        def _():
            self.halo(m, 0).wait_recv()

        @pl.when(self.has_above)
        def _():
            self.halo(m, 1).wait_recv()

    def run(self, stage):
        levels = levels_of(self.frames)
        before = [[] for _ in range(self.frames)]
        turn = [m for level in levels for m in level]
        before[0].append((self.edges, levels[1]))
        before[1].append((self.inners, levels[1]))
        place = 1
        for i in range(1, len(levels) - 1):
            before[place + 1].append((self.edges, levels[i + 1]))
            place += len(levels[i])
            before[place].append((self.inners, levels[i + 1]))

        def one(k, carry):
            m = 0
            for i in range(self.frames):
                chosen = (k == i).astype(jnp.int32)
                m = m + chosen * turn[i]
                if before[i]:

                    @pl.when(k == i)
                    def _():
                        for action, group in before[i]:
                            action(group)

            stage(m)
            return carry

        lax.fori_loop(0, self.frames, one, 0)

    def close(self):
        for m in range(self.frames):
            for part in range(2):
                for inner in range(2):
                    for b in self.later(part, m):
                        self.copy(part, inner, m, b).wait_send()

            @pl.when(self.has_above)
            def _():
                self.halo(m, 0).wait_send()

            @pl.when(self.has_below)
            def _():
                self.halo(m, 1).wait_send()


class FrameSwap:
    def __init__(self, frames, terms, terms_in, sems, rows, r, frame_at):
        self.orders, self.terms, self.terms_in, self.sems = orders_of(frames), terms, terms_in, sems
        self.frames, self.rows, self.r, self.frame_at = frames, rows, r, frame_at

    def part(self, i):
        half = self.rows // 2
        return pl.ds(i * half, half)

    def first(self, i, d):
        return next((n for n, b in enumerate(self.orders[i]) if d & b), len(self.orders[i]))

    def copy(self, i, d):
        return remote(
            self.terms.at[d, self.part(i)],
            self.terms_in.at[d, self.part(i)],
            self.sems.at[0, i, d],
            self.sems.at[1, i, d],
            self.frame_at[self.orders[i][self.first(i, d)]],
            self.r,
        )

    def computed(self, d):
        for i in range(2):
            if self.first(i, d) == 0:
                self.copy(i, d).start()

    def run(self, term, own):
        turn = [d for level in levels_of(self.frames)[::-1] for d in level]

        def one(k, carry):
            d = 0
            for i in range(self.frames):
                d = d + (k == i).astype(jnp.int32) * turn[i]
            block = term(d)

            @pl.when(k < self.frames - 1)
            def _():
                self.terms[d] = block.astype(self.terms.dtype)

            @pl.when(k == self.frames - 1)
            def _():
                own[...] = block

            for i in range(self.frames - 1):

                @pl.when(k == i)
                def _():
                    self.computed(turn[i])

            return carry

        return lambda start, stop: lax.fori_loop(start, stop, one, 0)

    def received(self, i, d):
        return [d | b for b in self.orders[i][: self.first(i, d)]]

    def pass_on(self):
        for n in range(1, len(self.orders[0])):
            for d in range(self.frames - 1, 0, -1):
                for i in range(2):
                    if self.first(i, d) == n:
                        part = self.part(i)
                        total = self.terms[d, part].astype(jnp.float32)
                        for e in self.received(i, d):
                            self.copy(i, e).wait_recv()
                            total = total + self.terms_in[e, part].astype(jnp.float32)
                        self.terms[d, part] = total.astype(self.terms.dtype)
                        self.copy(i, d).start()

    def add_to(self, total):
        for i in range(2):
            part = self.part(i)
            for e in self.received(i, 0):
                self.copy(i, e).wait_recv()
                total[part] = total[part] + self.terms_in[e, part].astype(jnp.float32)

    def close(self):
        for d in range(1, self.frames):
            for i in range(2):
                self.copy(i, d).wait_send()


def relay_line(pairs, q, far, ready, arrive, halves):
    low = (q < (pairs + 1) // 2).astype(jnp.int32)
    hops = pairs - 1 - 2 * q
    shift = 2 * hops * (2 * low - 1)

    def item(k, side, there):
        i = lax.div(k, 2)
        has_up = jnp.where(side == 0, q > 0, q < pairs - 1)
        count = jnp.where(side == 0, pairs - 1 - q, q)
        d = jnp.where(side == 0, pairs - 1 - i, i)
        for half in range(2):
            start, length = halves[half]
            part = pl.ds(start, length)
            wanted = jnp.logical_and(lax.rem(k, 2) == half, jnp.logical_and(there, i < count))

            @pl.when(jnp.logical_and(has_up, wanted))
            def _():
                far(d, side, half).wait_recv()
                ready[d, part] = (
                    ready[d, part].astype(jnp.float32) + arrive[side, d, part].astype(jnp.float32)
                ).astype(jnp.bfloat16)
                far(d, side, half).start()

    def slot(k, carry):
        item(jnp.maximum(k - shift, 0), low, k >= shift)
        item(k, 1 - low, True)
        return carry

    lax.fori_loop(0, 2 * (pairs - 1), slot, 0)


def padded_taps(own_rows, frames, channels):
    return max(-(-((i * own_rows) % channels + own_rows) // channels) for i in range(frames))


def conv_kernel(frames, slabs, *refs):
    (latents, row_valid, gain, weight_hbm) = refs[:4]
    (history, mixed, flag_tile) = refs[4:7]
    (shifted, weight, terms, terms_in, total) = refs[7:12]
    (load_sem, gather_sems, halo_sems, term_sems) = refs[12:]
    rows, cols, channels = latents.shape
    size = rows * cols
    narrow = shifted.shape[3]
    own_rows = weight_hbm.shape[0]
    tap_total = own_rows * frames // channels
    t, r = lax.axis_index("tm"), lax.axis_index("rows")
    frame_at = [flipped(t, frames, d) for d in range(frames)]
    first_tap = lax.div(t * own_rows, channels)
    weight_from = pl.multiple_of(t * own_rows - first_tap * channels, 16)
    tap_count = weight.shape[0] // channels

    barrier = pltpu.get_barrier_semaphore()
    greeted = greet(barrier, t, r, frames, slabs, frame_at, [1])
    flag_tile[...] = jnp.zeros_like(flag_tile)
    for h in range(rows):
        flag = row_valid[h].astype(jnp.float32)
        part = latents[h].astype(jnp.float32)
        scale = lax.rsqrt(jnp.mean(part * part, axis=1, keepdims=True) + epsilon)
        part = jax.nn.silu(part * scale * gain[...]) * flag
        history[t, h + 1] = part.astype(jnp.bfloat16)

    @pl.when(r == 0)
    def _():
        for f in range(frames):
            history[f, 0] = jnp.zeros((cols, channels), history.dtype)

    @pl.when(r == slabs - 1)
    def _():
        for f in range(frames):
            history[f, rows + 1] = jnp.zeros((cols, channels), history.dtype)

    pl.semaphore_wait(barrier, greeted)
    gather = FrameGather(
        frames, slabs, history, gather_sems, halo_sems, rows, t, r, frame_at
    )
    swap = FrameSwap(frames, terms, terms_in, term_sems, rows, r, frame_at)
    gather.start()
    for h in range(rows):
        flag = row_valid[h].astype(jnp.float32)
        flag_tile[h : h + 1, :] = jnp.full((1, flag_tile.shape[1]), flag, flag_tile.dtype)
    weight[...] = jnp.zeros_like(weight)
    load = pltpu.make_async_copy(weight_hbm, weight.at[pl.ds(weight_from, own_rows)], load_sem)
    load.start()
    for dw in range(3):
        for f in range(2):
            shifted[dw, f] = jnp.zeros(shifted.shape[2:], shifted.dtype)
    spare = jnp.zeros((narrow - cols, channels), jnp.float32)

    def stage(d):
        f = flipped(t, frames, d)
        gather.wait_halos(d)

        def widen(h, carry):
            line = jnp.concatenate([history[f, h].astype(jnp.float32), spare], axis=0)
            shifted[0, f + 2, h] = pltpu.roll(line, 1, 0).astype(jnp.bfloat16)
            shifted[1, f + 2, h] = line.astype(jnp.bfloat16)
            shifted[2, f + 2, h] = pltpu.roll(line, narrow - 1, 0).astype(jnp.bfloat16)
            return carry

        lax.fori_loop(0, rows + 2, widen, 0)

    gather.run(stage)
    load.wait()

    def convolve(f):
        total = None
        for j in range(tap_count):
            k = jnp.minimum(first_tap + j, tap_total - 1)
            dt, dh, dw = lax.div(k, 9), lax.rem(lax.div(k, 3), 3), lax.rem(k, 3)
            window = shifted[dw, f + dt, pl.ds(dh, rows)].reshape(rows * narrow, channels)
            term = dot(window, weight[j * channels : (j + 1) * channels, :])
            total = term if total is None else total + term
        return total.reshape(rows, narrow, channels)[:, :cols]

    swap.run(lambda d: convolve(flipped(t, frames, d)), total)(0, frames)
    total[...] += latents[...].astype(jnp.float32)
    swap.pass_on()
    swap.add_to(total)
    mixed[...] = total[...].reshape(size, channels).astype(mixed.dtype)
    gather.close()
    swap.close()


def convolve_frames(latents, row_valid, gain, conv_weight, collective_id):
    frames, slabs = lax.axis_size("tm"), lax.axis_size("rows")
    rows, cols, channels = latents.shape
    bf16, f32 = jnp.bfloat16, jnp.float32
    narrow = -(-cols // 16) * 16
    padded = padded_taps(conv_weight.shape[0], frames, channels) * channels
    dma = pltpu.SemaphoreType.DMA
    return pl.pallas_call(
        functools.partial(conv_kernel, frames, slabs),
        out_shape=[
            jax.ShapeDtypeStruct((frames, rows + 2, cols, channels), bf16),
            jax.ShapeDtypeStruct((rows * cols, channels), bf16),
            jax.ShapeDtypeStruct((FLAG_ROWS, 128), bf16),
        ],
        in_specs=[IN_VMEM, pl.BlockSpec(memory_space=pltpu.SMEM), IN_VMEM, ANY],
        out_specs=[IN_VMEM] * 3,
        scratch_shapes=[
            pltpu.VMEM((3, frames + 2, rows + 2, narrow, channels), bf16),
            pltpu.VMEM((padded, channels), bf16),
            pltpu.VMEM((frames, rows, cols, channels), bf16),
            pltpu.VMEM((frames, rows, cols, channels), bf16),
            pltpu.VMEM((rows, cols, channels), f32),
            dma,
            dma((2, 2, 2, frames)),
            dma((2, frames, 2)),
            dma((2, 2, frames)),
        ],
        compiler_params=params(collective_id, 62),
    )(latents, row_valid, gain, conv_weight)


def halves_of(size):
    near = size // 2 // 16 * 16
    return ((0, near), (near, size - near))


def attention_kernel(frames, slabs, grad_scale, inv_root, *refs):
    (mixed, cotangent, flag_tile, gain) = refs[:4]
    projections = refs[4:8]
    (d_mixed_out, d_conv_out, stack_out) = refs[8:11]
    (cells, cells_t, prob, d_weights, tops, sums, dots) = refs[11:18]
    (mine, near, ready, arrive, own_total, weighted_t, d_cells_t) = refs[18:25]
    (queries, key_side, value_side, d_attended, grad_out) = refs[25:30]
    (grads, grads_in, stack) = refs[30:33]
    (w_query, w_key, w_value, w_out) = refs[33:37]
    (load_sems, sib_sems, hop_sems, hand_sems, near_sems, far_send, far_recv, grad_sems) = refs[37:]
    pairs = slabs // 2
    rows, cols, channels = cotangent.shape
    size = rows * cols
    halves = halves_of(size)
    t, r = lax.axis_index("tm"), lax.axis_index("rows")
    q, c = lax.div(r, 2), lax.rem(r, 2)
    other = 1 - c
    sibling = 2 * q + other
    frame_at = [flipped(t, frames, d) for d in range(frames)]
    loads = [
        pltpu.make_async_copy(source, target, load_sems.at[i])
        for i, (source, target) in enumerate(
            zip(projections, (w_query, w_key, w_value, w_out))
        )
    ]
    for copy in loads:
        copy.start()
    barrier = pltpu.get_barrier_semaphore()
    for b in bits_of(frames):
        signal(barrier, frame_at[b], r)
    has_left, has_right = q > 0, q < pairs - 1
    signal(barrier, t, sibling)

    @pl.when(has_left)
    def _():
        signal(barrier, t, r - 2)

    @pl.when(has_right)
    def _():
        signal(barrier, t, r + 2)

    mixed_f = mixed[...].astype(jnp.float32)
    second_scale = lax.rsqrt(jnp.mean(mixed_f * mixed_f, axis=1, keepdims=True) + epsilon)
    attn_in = (mixed_f * second_scale * gain[...]).astype(jnp.bfloat16)
    cells[r, :size] = attn_in
    for i in range(channels // 128):
        cells[r, size:, i * 128 : (i + 1) * 128] = flag_tile[...]
    sides = has_left.astype(jnp.int32) + has_right.astype(jnp.int32)
    pl.semaphore_wait(barrier, 1 + len(bits_of(frames)) + sides)
    cuts = (halves[0], (halves[1][0], halves[1][1] + FLAG_ROWS))

    def sources(step, side):
        return q - step if side == 0 else q + step

    def arrives(step, side):
        at = sources(step, side)
        return jnp.logical_and(step < pairs, jnp.logical_and(at >= 0, at < pairs))

    def onward(step, side):
        ahead = q < pairs - 1 if side == 0 else q > 0
        return jnp.logical_and(ahead, arrives(step, side))

    def hop(step, side, half):
        start, count = cuts[half]
        part = cells.at[2 * sources(step - 1, side) + c, pl.ds(start, count)]
        target = r + 2 if side == 0 else r - 2
        return remote(
            part, part, hop_sems.at[0, side, step, half], hop_sems.at[1, side, step, half], t, target
        )

    def hand(step, side):
        part = cells.at[2 * sources(step, side) + c]
        return remote(
            part, part, hand_sems.at[0, side, step], hand_sems.at[1, side, step], t, sibling
        )

    to_sibling = remote(cells.at[r], cells.at[r], sib_sems.at[0], sib_sems.at[1], t, sibling)
    for half in range(2):
        for side in range(2):

            @pl.when(onward(0, side))
            def _():
                hop(1, side, half).start()

    to_sibling.start()

    for h in range(rows):
        flag = flag_tile[h : h + 1, 0:1].astype(jnp.float32)
        part = cotangent[h].astype(jnp.float32)
        grad_out[h * cols : (h + 1) * cols, :] = jnp.where(flag > 0, part, 0.0).astype(jnp.bfloat16)
    for copy in loads:
        copy.wait()
    queries[...] = dot(attn_in, w_query[...]).astype(jnp.bfloat16)
    key_side[...] = contract_last(queries[...], w_key[...]).astype(jnp.bfloat16)
    d_attended[...] = contract_last(grad_out[...], w_out[...]).astype(jnp.bfloat16)
    value_side[...] = contract_last(d_attended[...], w_value[...]).astype(jnp.bfloat16)

    lowest = float(jnp.finfo(jnp.float32).min)

    def absorb(j):
        block = cells[j, :size]
        flags = cells[j, size:, :128].astype(jnp.float32)
        scores = contract_last(block, key_side[...]) * inv_root
        kept = []
        for h in range(rows):
            flag = flags[h : h + 1, 0:1]
            kept.append(jnp.where(flag > 0, scores[h * cols : (h + 1) * cols], lowest))
        scores = jnp.concatenate(kept, axis=0)
        top = jnp.max(scores, axis=0, keepdims=True)
        exponent = jnp.exp(scores - top)
        prob[j] = exponent
        d_weight = contract_last(block, value_side[...])
        d_weights[j] = d_weight
        tops[j] = top
        sums[j] = jnp.sum(exponent, axis=0, keepdims=True)
        dots[j] = jnp.sum(exponent * d_weight, axis=0, keepdims=True)
        cells_t[j] = block.T

    def pass_on(step, half):
        for side in range(2):

            @pl.when(arrives(step, side))
            def _():
                hop(step, side, half).wait_recv()

            @pl.when(onward(step, side))
            def _():
                hop(step + 1, side, half).start()

            if half == 1:

                @pl.when(arrives(step, side))
                def _():
                    hand(step, side).start()

    def own_pair(i, carry):
        @pl.when(i == 1)
        def _():
            to_sibling.wait_recv()

        absorb(2 * q + c + i * (other - c))
        return carry

    lax.fori_loop(0, 2, own_pair, 0)
    pass_on(1, 0)
    pass_on(1, 1)

    def two_slabs(k, carry):
        step, side = 1 + lax.div(k, 2), lax.rem(k, 2)
        at = q - step + 2 * step * side
        there = jnp.logical_and(at >= 0, at < pairs)

        def one(i, carry):
            for s in range(2):

                @pl.when(jnp.logical_and(i == 1, side == s))
                def _():
                    hand(step, s).wait_recv()

            absorb(2 * at + c + i * (other - c))
            return carry

        @pl.when(there)
        def _():
            lax.fori_loop(0, 2, one, 0)

        for half in range(2):

            @pl.when(jnp.logical_and(side == half, step < pairs - 1))
            def _():
                pass_on(step + 1, half)

        return carry

    lax.fori_loop(0, 2 * (pairs - 1), two_slabs, 0)

    top_all = tops[0]
    for j in range(1, slabs):
        top_all = jnp.maximum(top_all, tops[j])
    total_sum = jnp.zeros_like(top_all)
    total_dot = jnp.zeros_like(top_all)
    for j in range(slabs):
        rescale = jnp.exp(tops[j] - top_all)
        total_sum = total_sum + rescale * sums[j]
        total_dot = total_dot + rescale * dots[j]
        tops[j] = rescale
    inverse = 1.0 / total_sum
    row_delta = total_dot * inverse
    weighted_t[...] = jnp.zeros_like(weighted_t)
    d_cells_t[...] = jnp.zeros_like(d_cells_t)

    def emit(j):
        weights = prob[j] * (tops[j] * inverse)
        weights_b = weights.astype(jnp.bfloat16)
        d_scores = (weights * (d_weights[j] - row_delta) * inv_root).astype(jnp.bfloat16)
        block_t = cells_t[j]
        weighted_t[...] += dot(block_t, weights_b)
        d_cells_t[...] += dot(block_t, d_scores)
        return dot(d_scores, key_side[...]) + dot(weights_b, value_side[...])

    def give(d):
        part = mine.at[d]
        return remote(part, near.at[d], near_sems.at[0, d], near_sems.at[1, d], t, sibling)

    def far(d, side, half):
        start, count = halves[half]
        target = r + 2 - 4 * side
        return remote(
            ready.at[d, pl.ds(start, count)],
            arrive.at[side, d, pl.ds(start, count)],
            far_send.at[d, half],
            far_recv.at[side, d, half],
            t,
            target,
        )

    low_half = (q < (pairs + 1) // 2).astype(jnp.int32)
    right_count = pairs - 1 - q

    def chip_order(i):
        from_right = pairs - 1 - i
        low_order = jnp.where(i < right_count, from_right, i - right_count)
        high_order = jnp.where(i < q, i, pairs - 1 - (i - q))
        order = low_half * low_order + (1 - low_half) * high_order
        return jnp.where(i == pairs - 1, q, order)

    def one_chip(i, carry):
        d = chip_order(i)
        mine[d] = emit(2 * d + other).astype(jnp.bfloat16)
        give(d).start()
        term = emit(2 * d + c)
        give(d).wait_recv()
        term = term + near[d].astype(jnp.float32)

        @pl.when(i == pairs - 1)
        def _():
            own_total[...] = term

        @pl.when(i < pairs - 1)
        def _():
            ready[d] = term.astype(jnp.bfloat16)

        @pl.when(jnp.logical_and(q == 0, d > q))
        def _():
            far(d, 0, 0).start()
            far(d, 0, 1).start()

        @pl.when(jnp.logical_and(q == pairs - 1, d < q))
        def _():
            far(d, 1, 0).start()
            far(d, 1, 1).start()

        return carry

    lax.fori_loop(0, pairs, one_chip, 0)

    weighted_b = weighted_t[...].astype(jnp.bfloat16)
    d_cells_b = d_cells_t[...].astype(jnp.bfloat16)
    attended = contract_first(weighted_b, w_value[...]).astype(jnp.bfloat16)
    d_query = contract_first(d_cells_b, w_key[...]).astype(jnp.bfloat16)
    blocks = [
        contract_first(cells[r, :size], d_query),
        dot(d_cells_b, queries[...]),
        dot(weighted_b, d_attended[...]),
        contract_first(attended, grad_out[...]),
    ]
    share = 4 * channels // frames
    swap = FrameSwap(frames, grads, grads_in, grad_sems, share, r, frame_at)
    for g in range(frames):
        i, start = divmod(g * share, channels)
        part = blocks[i][start : start + share] * grad_scale
        grads[flipped(t, frames, g)] = part.astype(jnp.bfloat16)
    for d in range(frames - 1, 0, -1):
        swap.computed(d)
    own_total[...] += contract_last(d_query, w_query[...])

    relay_line(pairs, q, far, ready, arrive, halves)

    swap.pass_on()
    for half in range(2):
        start, length = halves[half]
        part = pl.ds(start, length)
        for side in range(2):

            @pl.when(q > 0 if side == 0 else q < pairs - 1)
            def _():
                far(q, side, half).wait_recv()
                own_total[part, :] += arrive[side, q, part].astype(jnp.float32)

        mixed_f = mixed[part, :].astype(jnp.float32)
        second_scale = lax.rsqrt(jnp.mean(mixed_f * mixed_f, axis=1, keepdims=True) + epsilon)
        normed_two = mixed_f * second_scale
        scaled_two = gain[...] * own_total[part, :]
        d_mixed = grad_out[part, :].astype(jnp.float32) + second_scale * (
            scaled_two - normed_two * jnp.mean(scaled_two * normed_two, axis=1, keepdims=True)
        )
        d_mixed_out[part, :] = d_mixed
        d_conv_out[pl.ds(start // cols, length // cols)] = d_mixed.astype(jnp.bfloat16).reshape(
            length // cols, cols, channels
        )
    stack[...] = grads[0].astype(jnp.float32)
    swap.add_to(stack)
    stack_out[...] = stack[...].astype(stack_out.dtype)

    to_sibling.wait_send()
    for side in range(2):
        for step in range(1, pairs):

            @pl.when(onward(step - 1, side))
            def _():
                for half in range(2):
                    hop(step, side, half).wait_send()

            @pl.when(arrives(step, side))
            def _():
                hand(step, side).wait_send()

    for d in range(pairs):
        give(d).wait_send()

        @pl.when(q != d)
        def _():
            for half in range(2):
                far(d, 0, half).wait_send()

    swap.close()


def attend(mixed, cotangent, flag_tile, gain, w_query, w_key, w_value, w_out, scales, collective_id):
    frames, slabs = lax.axis_size("tm"), lax.axis_size("rows")
    pairs = slabs // 2
    rows, cols, channels = cotangent.shape
    size = rows * cols
    bf16, f32 = jnp.bfloat16, jnp.float32
    share = 4 * channels // frames
    dma = pltpu.SemaphoreType.DMA
    return pl.pallas_call(
        functools.partial(attention_kernel, frames, slabs, *scales),
        out_shape=[
            jax.ShapeDtypeStruct((size, channels), f32),
            jax.ShapeDtypeStruct((rows, cols, channels), bf16),
            jax.ShapeDtypeStruct((share, channels), bf16),
        ],
        in_specs=[IN_VMEM] * 4 + [ANY] * 4,
        out_specs=[IN_VMEM] * 3,
        scratch_shapes=[
            pltpu.VMEM((slabs, size + FLAG_ROWS, channels), bf16),
            pltpu.VMEM((slabs, channels, size), bf16),
            pltpu.VMEM((slabs, size, size), f32),
            pltpu.VMEM((slabs, size, size), f32),
            pltpu.VMEM((slabs, 1, size), f32),
            pltpu.VMEM((slabs, 1, size), f32),
            pltpu.VMEM((slabs, 1, size), f32),
            pltpu.VMEM((pairs, size, channels), bf16),
            pltpu.VMEM((pairs, size, channels), bf16),
            pltpu.VMEM((pairs, size, channels), bf16),
            pltpu.VMEM((2, pairs, size, channels), bf16),
            pltpu.VMEM((size, channels), f32),
            pltpu.VMEM((channels, size), f32),
            pltpu.VMEM((channels, size), f32),
            pltpu.VMEM((size, channels), bf16),
            pltpu.VMEM((size, channels), bf16),
            pltpu.VMEM((size, channels), bf16),
            pltpu.VMEM((size, channels), bf16),
            pltpu.VMEM((size, channels), bf16),
            pltpu.VMEM((frames, share, channels), bf16),
            pltpu.VMEM((frames, share, channels), bf16),
            pltpu.VMEM((share, channels), f32),
            pltpu.VMEM((channels, channels), bf16),
            pltpu.VMEM((channels, channels), bf16),
            pltpu.VMEM((channels, channels), bf16),
            pltpu.VMEM((channels, channels), bf16),
            dma((4,)),
            dma((2,)),
            dma((2, 2, pairs + 1, 2)),
            dma((2, 2, pairs)),
            dma((2, pairs)),
            dma((pairs, 2)),
            dma((2, pairs, 2)),
            dma((2, 2, frames)),
        ],
        compiler_params=params(collective_id, 62),
    )(mixed, cotangent, flag_tile, gain, w_query, w_key, w_value, w_out)


def window_rows(count, step):
    return -(-(count + 16 - math.gcd(step, 16)) // 16) * 16


def conv_back_kernel(frames, slabs, grad_scale, *refs):
    (d_conv, history_hbm, weight_hbm, d_mixed_hbm, latents_hbm, flag_tile, gain, stack) = refs[:8]
    (grad_out, conv_out, attn_out) = refs[8:11]
    (spread, shifted, history, history_t, weight, weight_acc) = refs[11:17]
    (normed, first_scale, slope) = refs[17:20]
    (mine, near, ready, arrive, own_total) = refs[20:25]
    (terms, terms_in, own_term, stack_in, d_mixed, latents) = refs[25:31]
    (load_sems, gather_sems, halo_sems, stack_sems) = refs[31:35]
    (near_sems, far_send, far_recv, term_sems) = refs[35:]
    pairs = slabs // 2
    rows, cols, channels = d_conv.shape
    size = rows * cols
    wide = shifted.shape[3]
    narrow = -(-cols // 16) * 16
    own_rows = weight_hbm.shape[0]
    tap_total = own_rows * frames // channels
    block_rows = own_rows // slabs
    span = mine.shape[1]
    halves = halves_of(span)
    t, r = lax.axis_index("tm"), lax.axis_index("rows")
    q, c = lax.div(r, 2), lax.rem(r, 2)
    other = 1 - c
    sibling = 2 * q + other
    frame_at = [flipped(t, frames, d) for d in range(frames)]
    slab_at = [lax.rem(r + d, slabs) for d in range(slabs)]
    first_tap = lax.div(t * own_rows, channels)
    weight_from = pl.multiple_of(t * own_rows - first_tap * channels, 16)
    tap_count = weight.shape[0] // channels

    def tap_at(j):
        k = jnp.minimum(first_tap + j, tap_total - 1)
        return lax.div(k, 9), lax.rem(lax.div(k, 3), 3), lax.rem(k, 3)

    weight[:channels, :] = jnp.zeros((channels, channels), weight.dtype)
    tail = own_rows // 16 * 16
    weight[tail:, :] = jnp.zeros((weight.shape[0] - tail, channels), weight.dtype)
    loads = [
        pltpu.make_async_copy(history_hbm, history, load_sems.at[0]),
        pltpu.make_async_copy(d_mixed_hbm, d_mixed, load_sems.at[2]),
        pltpu.make_async_copy(latents_hbm, latents, load_sems.at[3]),
        pltpu.make_async_copy(
            weight_hbm, weight.at[pl.ds(weight_from, own_rows)], load_sems.at[1]
        ),
    ]
    for copy in loads:
        copy.start()
    barrier = pltpu.get_barrier_semaphore()
    for d in range(1, slabs):
        signal(barrier, t, slab_at[d])
    for b in bits_of(frames):
        signal(barrier, frame_at[b], r)
    for h in range(rows):
        spread[t, h + 1] = d_conv[h]

    @pl.when(r == 0)
    def _():
        for f in range(frames):
            spread[f, 0] = jnp.zeros((cols, channels), spread.dtype)

    @pl.when(r == slabs - 1)
    def _():
        for f in range(frames):
            spread[f, rows + 1] = jnp.zeros((cols, channels), spread.dtype)

    pl.semaphore_wait(barrier, slabs - 1 + len(bits_of(frames)))
    gather = FrameGather(
        frames, slabs, spread, gather_sems, halo_sems, rows, t, r, frame_at
    )
    swap = FrameSwap(frames, terms, terms_in, term_sems, rows, r, frame_at)
    gather.start()
    share = stack_in.shape[1]
    stack_step = attn_out.shape[0]

    def stack_low(at):
        return pl.multiple_of(lax.div(at * stack_step, 16) * 16, 16)

    stack_copies = [
        remote(
            stack.at[pl.ds(stack_low(slab_at[d]), share)],
            stack_in.at[d],
            stack_sems.at[0, d],
            stack_sems.at[1, d],
            t,
            slab_at[d],
        )
        for d in range(1, slabs)
    ]
    for copy in stack_copies:
        copy.start()

    weight_acc[...] = jnp.zeros_like(weight_acc)
    history_t[0] = jnp.zeros(history_t.shape[1:], history_t.dtype)
    history_t[1] = jnp.zeros(history_t.shape[1:], history_t.dtype)
    for copy in loads:
        copy.wait()
    spare = jnp.zeros((wide - cols, channels), jnp.float32)

    def turn(f, carry):
        for h in range(rows + 2):
            line = jnp.concatenate([history[f, h].astype(jnp.float32), spare], axis=0)
            history_t[f + 2, :, h * wide : (h + 1) * wide] = line.astype(jnp.bfloat16).T
        return carry

    lax.fori_loop(0, frames, turn, 0)
    def stage(d):
        f = flipped(t, frames, d)
        gather.wait_halos(d)

        def widen(h, carry):
            line = jnp.concatenate([spread[f, h].astype(jnp.float32), spare], axis=0)
            shifted[0, f, h] = pltpu.roll(line, wide - 1, 0).astype(jnp.bfloat16)
            shifted[1, f, h] = line.astype(jnp.bfloat16)
            shifted[2, f, h] = pltpu.roll(line, 1, 0).astype(jnp.bfloat16)
            return carry

        lax.fori_loop(0, rows + 2, widen, 0)

        for j in range(tap_count):
            dt, dh, dw = tap_at(j)
            lanes = pl.ds(pl.multiple_of(dh * wide, wide), rows * wide)
            ahead = shifted[dw, f, 1 : rows + 1].reshape(rows * wide, channels)
            weight_acc[j * channels : (j + 1) * channels, :] += dot(
                history_t[f + dt, :, lanes], ahead
            )

    gather.run(stage)

    def low_row(block):
        return pl.multiple_of(lax.div(weight_from + block * block_rows, 16) * 16, 16)

    def weight_block(block):
        return weight_acc[pl.ds(low_row(block), span), :] * grad_scale

    def give(d):
        part = mine.at[d]
        return remote(part, near.at[d], near_sems.at[0, d], near_sems.at[1, d], t, sibling)

    def far(d, side, half):
        start, count = halves[half]
        return remote(
            ready.at[d, pl.ds(start, count)],
            arrive.at[side, d, pl.ds(start, count)],
            far_send.at[d, half],
            far_recv.at[side, d, half],
            t,
            r + 2 - 4 * side,
        )

    low_half = (q < (pairs + 1) // 2).astype(jnp.int32)
    right_count = pairs - 1 - q

    def chip_order(i):
        low_order = jnp.where(i < right_count, pairs - 1 - i, i - right_count)
        high_order = jnp.where(i < q, i, pairs - 1 - (i - q))
        order = low_half * low_order + (1 - low_half) * high_order
        return jnp.where(i == pairs - 1, q, order)

    def one_gift(i, carry):
        d = chip_order(i)
        mine[d] = weight_block(2 * d + other).astype(jnp.bfloat16)
        give(d).start()
        return carry

    def one_chip(i, carry):
        @pl.when(i < pairs - 1)
        def _():
            one_gift(i + 1, 0)

        d = chip_order(i)
        term = weight_block(2 * d + c)
        give(d).wait_recv()
        term = term + near[d].astype(jnp.float32)

        @pl.when(i == pairs - 1)
        def _():
            own_total[...] = term

        @pl.when(i < pairs - 1)
        def _():
            ready[d] = term.astype(jnp.bfloat16)

        @pl.when(jnp.logical_and(q == 0, d > q))
        def _():
            far(d, 0, 0).start()
            far(d, 0, 1).start()

        @pl.when(jnp.logical_and(q == pairs - 1, d < q))
        def _():
            far(d, 1, 0).start()
            far(d, 1, 1).start()

        return carry

    one_gift(0, 0)
    lax.fori_loop(0, pairs, one_chip, 0)
    for dw in range(3):
        for f in range(2):
            shifted[dw, frames + f] = jnp.zeros(shifted.shape[2:], shifted.dtype)

    def back(f):
        total = None
        for j in range(tap_count):
            dt, dh, dw = tap_at(j)
            ahead = shifted[dw, f + 2 - dt, pl.ds(2 - dh, rows), :narrow]
            term = contract_last(
                ahead.reshape(rows * narrow, channels),
                weight[j * channels : (j + 1) * channels, :],
            )
            total = term if total is None else total + term
        return total.reshape(rows, narrow, channels)[:, :cols]

    swap.run(lambda d: back(flipped(t, frames, d)), own_term)(0, frames)
    swap.pass_on()
    relay_line(pairs, q, far, ready, arrive, halves)
    inputs = latents[...].astype(jnp.float32)
    scale_one = lax.rsqrt(jnp.mean(inputs * inputs, axis=1, keepdims=True) + epsilon)
    normed_one = inputs * scale_one
    first_scale[...] = scale_one
    normed[...] = normed_one
    factor = gain[...] * silu_slope(normed_one * gain[...])
    for h in range(rows):
        flag = flag_tile[h : h + 1, 0:1].astype(jnp.float32)
        part = factor[h * cols : (h + 1) * cols]
        slope[h * cols : (h + 1) * cols, :] = jnp.where(flag > 0, part, 0.0)

    stack_sum = stack[pl.ds(stack_low(r), share), :].astype(jnp.float32)
    for d in range(1, slabs):
        stack_copies[d - 1].wait_recv()
        stack_sum = stack_sum + stack_in[d].astype(jnp.float32)
    if share > stack_step:
        stack_sum = pltpu.roll(stack_sum, share - (r * stack_step - stack_low(r)), 0)
    attn_out[...] = stack_sum[:stack_step]

    swap.add_to(own_term)
    scaled_one = own_term[...].reshape(size, channels) * slope[...]
    normed_one = normed[...]
    input_grad = d_mixed[...] + first_scale[...] * (
        scaled_one - normed_one * jnp.mean(scaled_one * normed_one, axis=1, keepdims=True)
    )
    grad_out[...] = input_grad.reshape(rows, cols, channels).astype(grad_out.dtype)

    for side in range(2):

        @pl.when(q > 0 if side == 0 else q < pairs - 1)
        def _():
            for half in range(2):
                start, length = halves[half]
                far(q, side, half).wait_recv()
                part = pl.ds(start, length)
                own_total[part, :] += arrive[side, q, part].astype(jnp.float32)

    result = own_total[...]
    if span > block_rows:
        offset = weight_from + r * block_rows - low_row(r)
        result = pltpu.roll(result, span - offset, 0)
    conv_out[...] = result[:block_rows]

    gather.close()
    swap.close()
    for copy in stack_copies:
        copy.wait_send()
    for d in range(pairs):
        give(d).wait_send()

        @pl.when(q != d)
        def _():
            for half in range(2):
                far(d, 0, half).wait_send()


def conv_back(
    d_conv, history, conv_weight, d_mixed, latents, flag_tile, gain, stack, grad_scale, collective_id
):
    frames, slabs = lax.axis_size("tm"), lax.axis_size("rows")
    pairs = slabs // 2
    rows, cols, channels = d_conv.shape
    size = rows * cols
    bf16, f32 = jnp.bfloat16, jnp.float32
    wide = -(-cols // 128) * 128
    own_rows = conv_weight.shape[0]
    padded = padded_taps(own_rows, frames, channels) * channels
    block_rows = own_rows // slabs
    span = window_rows(block_rows, math.gcd(own_rows, block_rows))
    stack_rows = stack.shape[0] // slabs
    share = window_rows(stack_rows, stack_rows)
    if share > stack_rows:
        stack = jnp.pad(stack, ((0, 16), (0, 0)))
    dma = pltpu.SemaphoreType.DMA
    return pl.pallas_call(
        functools.partial(conv_back_kernel, frames, slabs, grad_scale),
        out_shape=[
            jax.ShapeDtypeStruct((rows, cols, channels), bf16),
            jax.ShapeDtypeStruct((block_rows, channels), f32),
            jax.ShapeDtypeStruct((stack_rows, channels), f32),
        ],
        in_specs=[IN_VMEM] + [ANY] * 4 + [IN_VMEM] * 3,
        out_specs=[IN_VMEM] * 3,
        scratch_shapes=[
            pltpu.VMEM((frames, rows + 2, cols, channels), bf16),
            pltpu.VMEM((3, frames + 2, rows + 2, wide, channels), bf16),
            pltpu.VMEM((frames, rows + 2, cols, channels), bf16),
            pltpu.VMEM((frames + 2, channels, (rows + 2) * wide), bf16),
            pltpu.VMEM((padded, channels), bf16),
            pltpu.VMEM((padded + 32, channels), f32),
            pltpu.VMEM((size, channels), f32),
            pltpu.VMEM((size, 1), f32),
            pltpu.VMEM((size, channels), f32),
            pltpu.VMEM((pairs, span, channels), bf16),
            pltpu.VMEM((pairs, span, channels), bf16),
            pltpu.VMEM((pairs, span, channels), bf16),
            pltpu.VMEM((2, pairs, span, channels), bf16),
            pltpu.VMEM((span, channels), f32),
            pltpu.VMEM((frames, rows, cols, channels), bf16),
            pltpu.VMEM((frames, rows, cols, channels), bf16),
            pltpu.VMEM((rows, cols, channels), f32),
            pltpu.VMEM((slabs, share, channels), bf16),
            pltpu.VMEM((size, channels), f32),
            pltpu.VMEM((size, channels), bf16),
            dma((4,)),
            dma((2, 2, 2, frames)),
            dma((2, frames, 2)),
            dma((2, slabs)),
            dma((2, pairs)),
            dma((pairs, 2)),
            dma((2, pairs, 2)),
            dma((2, 2, frames)),
        ],
        compiler_params=params(collective_id, 62),
    )(d_conv, history, conv_weight, d_mixed, latents, flag_tile, gain, stack)


def finish_kernel(count, *refs):
    for i in range(count):
        refs[count + i][...] = refs[i][...]


def finish(arrays):
    count = len(arrays)
    return pl.pallas_call(
        functools.partial(finish_kernel, count),
        out_shape=[jax.ShapeDtypeStruct(a.shape, a.dtype) for a in arrays],
        in_specs=[IN_VMEM] * count,
        out_specs=[IN_VMEM] * count,
    )(*arrays)


def per_device(
    latents, row_valid, norm_gain, conv_weight, attn_gain, w_query, w_key, w_value, w_out, cotangent
):
    shape_all = latents.shape
    rows, cols, channels = shape_all[1:]
    frames, slabs = lax.axis_size("tm"), lax.axis_size("rows")
    grad_scale = 1.0 / math.sqrt(frames * slabs * rows * cols)
    inv_root = 1.0 / math.sqrt(channels)
    latents = latents.reshape(rows, cols, channels)
    history, mixed, flag_tile = convolve_frames(latents, row_valid, norm_gain, conv_weight, 0)
    d_mixed, d_conv, stack = attend(
        mixed,
        cotangent.reshape(rows, cols, channels),
        flag_tile,
        attn_gain,
        w_query,
        w_key,
        w_value,
        w_out,
        (grad_scale, inv_root),
        1,
    )
    results = conv_back(
        d_conv,
        history,
        conv_weight,
        d_mixed,
        latents.reshape(rows * cols, channels),
        flag_tile,
        norm_gain,
        stack,
        grad_scale,
        2,
    )
    input_grad, conv_weight_grad, attn_weight_grad = finish(results)
    return input_grad.reshape(shape_all), conv_weight_grad, attn_weight_grad


def solution(mesh):
    return jax.shard_map(
        per_device,
        mesh=mesh,
        in_specs=(
            P("tm", "rows", None, None),
            P("rows"),
            P(),
            P("tm", None),
            P(),
            P(),
            P(),
            P(),
            P(),
            P("tm", "rows", None, None),
        ),
        out_specs=(P("tm", "rows", None, None), P(("tm", "rows"), None), P(("tm", "rows"), None)),
        check_vma=False,
    )
```
